32 devices in a mesh: groups: 2 (over y), seq: 4 (over x, core), head: 4 (over z).
Axes of the slice: x: 2, y: 2, z: 4, core: 2. Of those that a mesh axis runs over, the one named last changes fastest.
Arguments:
- lin_qkv: bfloat16 [8192, 3, 2048], P(('groups', 'seq'), None, 'head'), parts along dimension 0, may hold values from -6 to 6
- level_weights: float32 [16, 16], P(None, 'head'), may hold values from 0.3 to 1.7
- soft_q: bfloat16 [8192, 2048], P(('groups', 'seq'), 'head'), parts along dimension 0, may hold values from -6 to 6
- soft_kv: bfloat16 [8192, 2, 256], P(('groups', 'seq')), parts along dimension 0, may hold values from -6 to 6
Outputs:
- mixed: bfloat16 [8192, 2, 2048], P(('groups', 'seq'), None, 'head'), parts along dimension 0
The draws below stay inside these ranges and needn't reach their ends.
There are 2 independent parts, one for each index of `groups`. The reference program is written for one: setup_inputs(seed, part) draws one part's arguments, and reference() takes and returns one part's arrays. A program takes and returns all parts, laid end to end along the dimension named above; an argument that names none is the same for every part. Nothing has to cross between parts.
All inputs are finite; a program needn't handle non-finite values.
Results may differ from the reference program's by a relative error of at most 0.0049.
Values may be sent and summed in bfloat16 or wider, within the bound.
No kernel may reach another device: no remote copies, remote signals or barrier semaphores. Data moves between devices by JAX's collectives and lax.ppermute only.
A program may use at most 128 MiB of HBM per device.

```python
import jax
import jax.numpy as jnp
from jax import lax

HD = 128
HEADS_LIN = 16
HEADS_SM = 16
KV_HEADS = 2
WINDOW = 1024
LEVELS = 16
TOK_DEV = 1024
TOKENS = 4096
N_SEQ = 4


def soft_inputs(key):
    query_key = jax.random.fold_in(key, 7001)
    pair_key = jax.random.fold_in(key, 7002)
    query_rows = jnp.clip(jax.random.normal(query_key, (TOKENS, HEADS_SM * HD), jnp.float32), -6.0, 6.0)
    pair_rows = jnp.clip(jax.random.normal(pair_key, (TOKENS, 2, KV_HEADS * HD), jnp.float32), -6.0, 6.0)
    return (query_rows, pair_rows)


def draw_soft_q(key, part):
    return soft_inputs(key)[0].astype(jnp.bfloat16)


def draw_soft_kv(key, part):
    return soft_inputs(key)[1].astype(jnp.bfloat16)


def shard_levels(rng, extent, cuts, low, top_value):
    loudness, own = 1.0, jax.random.fold_in(rng, 6)
    for axis_at, shards_of in cuts:
        heights = jnp.exp(jax.random.uniform(jax.random.fold_in(own, axis_at), (shards_of,), jnp.float32, low / len(cuts), top_value / len(cuts)))
        loudness = loudness * jnp.repeat(heights, extent[axis_at] // shards_of).reshape([-1 if axis == axis_at else 1 for axis in range(len(extent))])
    return loudness


def noise(own_key, extent, deviation, reach, cuts=(), held_as=jnp.bfloat16):
    gain = shard_levels(own_key, extent, cuts, -0.22, 0.18) if cuts else 1.0
    drawn = jax.random.normal(own_key, extent, jnp.float32) * deviation * gain
    return jnp.minimum(jnp.maximum(drawn, -reach), reach).astype(held_as)


def setup_inputs(seed: int = 0, part: int = 0) -> dict:
    key_of = jax.random.split(jax.random.key(seed), 5)
    part_keys = jax.random.split(jax.random.fold_in(key_of[4], part), 5)
    return {
        "lin_qkv": noise(part_keys[0], (TOKENS, 3, HEADS_LIN * HD), 1.0, 6.0, ((0, 4), (2, 4))),
        "level_weights": jnp.clip(0.3 + 1.40000004 * jax.random.uniform(key_of[1], (LEVELS, HEADS_LIN), jnp.float32) ** shard_levels(key_of[1], (LEVELS, HEADS_LIN), ((1, 4),), -0.2, 0.2), 0.3, 1.7),
        "soft_q": draw_soft_q(jax.random.fold_in(jax.random.fold_in(key_of[4], part), 71), part),
        "soft_kv": draw_soft_kv(jax.random.fold_in(jax.random.fold_in(key_of[4], part), 71), part),
    }


def bit_count(values):
    total = jnp.zeros_like(values)
    for power in range(LEVELS):
        total = total + (values >= 2 ** power).astype(jnp.int32)
    return total

def level_table(levels, table, first, count):
    result = jnp.zeros(levels.shape + (table.shape[1],), jnp.float32)
    for lev in range(first, first + count):
        result = result + (levels == lev).astype(jnp.float32)[..., None] * table[lev]
    return result

def reference(lin_qkv, level_weights, soft_q, soft_kv):
    heads = HEADS_LIN
    tok = TOK_DEV
    local_bits = tok.bit_length() - 1
    blocks_qkv = lin_qkv.reshape(N_SEQ, tok, 3, heads, HD)

    def local_part(block_qkv):
        query = block_qkv[:, 0].astype(jnp.float32)
        keys = block_qkv[:, 1].astype(jnp.float32)
        values = block_qkv[:, 2].astype(jnp.float32)
        pos = jnp.arange(tok, dtype=jnp.int32)
        levels = bit_count(jnp.bitwise_xor(pos[:, None], pos[None, :]))
        causal = pos[None, :] <= pos[:, None]
        weight = level_table(levels, level_weights, 0, local_bits + 1)
        weight = jnp.where(causal[:, :, None], weight, 0.0)
        scores = jnp.einsum('thd,shd->tsh', query, keys)
        weighted = (scores * weight).astype(jnp.bfloat16)
        intra = jnp.einsum('tsh,shd->thd', weighted.astype(jnp.float32), values)
        state = jnp.einsum('thd,the->hde', keys, values)
        return (intra, state)
    intra, states = lax.map(local_part, blocks_qkv)
    spans = jnp.arange(N_SEQ, dtype=jnp.int32)
    span_levels = local_bits + bit_count(jnp.bitwise_xor(spans[:, None], spans[None, :]))
    span_levels = jnp.where(spans[None, :] < spans[:, None], span_levels, 0)
    span_weight = level_table(span_levels, level_weights, 1, LEVELS - 1)
    span_weight = jnp.where((spans[None, :] < spans[:, None])[:, :, None], span_weight, 0.0)
    cross_state = jnp.einsum('cqh,qhde->chde', span_weight, states, precision=lax.Precision.HIGHEST).astype(jnp.bfloat16)
    query_all = blocks_qkv[:, :, 0].astype(jnp.float32)
    cross = jnp.einsum('cthd,chde->cthe', query_all, cross_state.astype(jnp.float32))
    lin_sum = intra + cross
    normed = lin_sum * lax.rsqrt(lax.optimization_barrier(jnp.mean(lin_sum * lin_sum, axis=-1, keepdims=True)) + 1e-06)
    lin_out = normed.astype(jnp.bfloat16).reshape(TOKENS, heads * HD)
    group = HEADS_SM // KV_HEADS
    block = min(512, TOK_DEV)
    queries = soft_q.reshape(TOKENS, HEADS_SM, HD)
    kv_all = soft_kv.reshape(TOKENS, 2, KV_HEADS, HD)
    padded = jnp.concatenate([jnp.zeros((WINDOW, 2, KV_HEADS, HD), jnp.bfloat16), kv_all], axis=0)
    scale = 1.0 / HD ** 0.5

    def one_block(index):
        start = (index * block).astype(jnp.int32)
        q_block = lax.dynamic_slice_in_dim(queries, start, block, 0).astype(jnp.float32)
        kv_block = lax.dynamic_slice_in_dim(padded, start, WINDOW + block, 0)
        keys = jnp.repeat(kv_block[:, 0], group, axis=1).astype(jnp.float32)
        values = jnp.repeat(kv_block[:, 1], group, axis=1).astype(jnp.float32)
        scores = jnp.einsum('ahd,jhd->haj', q_block, keys) * scale
        rows = jnp.arange(block, dtype=jnp.int32)[:, None]
        cols = jnp.arange(WINDOW + block, dtype=jnp.int32)[None, :]
        valid = (cols >= rows) & (cols <= rows + WINDOW) & (start + cols - WINDOW >= 0)
        scores = jnp.where(valid[None], scores, -1e+30)
        probs = jax.nn.softmax(scores, axis=-1).astype(jnp.bfloat16)
        out = jnp.einsum('haj,jhd->ahd', probs.astype(jnp.float32), values)
        return out.astype(jnp.bfloat16)
    soft_out = lax.map(one_block, jnp.arange(TOKENS // block, dtype=jnp.int32))
    soft_out = soft_out.reshape(TOKENS, HEADS_SM * HD)
    return jnp.stack([lin_out, soft_out], axis=1)
```

```python
import functools

import jax
import jax.numpy as jnp
import numpy as np
from jax import lax
from jax.experimental import pallas as pl
from jax.experimental.pallas import tpu as pltpu
from jax.sharding import PartitionSpec as P

HD = 128
HEADS_SM = 16
KV_HEADS = 2
WINDOW = 1024
CHUNK = 128
NEG = -1e30
F32 = jnp.float32
BF16 = jnp.bfloat16


def partner_2(value, axis, distance):
    mask = 2**distance
    pairs = [(source, source ^ mask) for source in range(lax.axis_size(axis))]
    return lax.ppermute(value, axis, pairs)


def passed_along(x, axis, by):
    size = lax.axis_size(axis)
    pairs = [(i, i + by) for i in range(size) if 0 <= i + by < size]
    return lax.ppermute(x, axis, pairs)


def nt_dot(a, b):
    return lax.dot_general(a, b, (((1,), (1,)), ((), ())), preferred_element_type=F32)


def tn_dot(a, b):
    return lax.dot_general(a, b, (((0,), (0,)), ((), ())), preferred_element_type=F32)


def states_kernel(heads, x_ref, state_ref):
    step = pl.program_id(0)
    for h in range(heads):
        lanes = slice(h * HD, (h + 1) * HD)
        part = tn_dot(x_ref[1, :, lanes], x_ref[2, :, lanes])

        @pl.when(step == 0)
        def _():
            state_ref[h] = part

        @pl.when(step > 0)
        def _():
            state_ref[h] += part


def states_call(planes):
    _, tok, width = planes.shape
    heads = width // HD
    rows = min(256, tok)
    return pl.pallas_call(
        functools.partial(states_kernel, heads),
        grid=(tok // rows,),
        in_specs=[pl.BlockSpec((3, rows, width), lambda i: (0, i, 0))],
        out_specs=pl.BlockSpec((heads, HD, HD), lambda i: (0, 0, 0)),
        out_shape=jax.ShapeDtypeStruct((heads, HD, HD), F32),
    )(planes)


def layer_kernel(
    heads, q_heads, block, first_ref, table_ref, x_ref, cross_ref, sq_ref, kb_ref, ko_ref, out_ref,
    stage, k_all, v_all, states, rows_out,
):
    tok = x_ref.shape[1]
    first = first_ref[0] > 0
    scale = float(np.log2(np.e) / np.sqrt(HD))
    for part, ref in enumerate((kb_ref, ko_ref)):
        here = pl.ds(part * tok, tok)
        stage[...] = ref[...].astype(F32)
        keys = stage[pl.ds(0, tok, stride=2), :] * scale
        high = keys.astype(BF16)
        k_all[here, 0:HD] = high
        k_all[here, HD : 2 * HD] = (keys - high.astype(F32)).astype(BF16)
        v_all[here, 0:HD] = stage[pl.ds(1, tok, stride=2), :].astype(BF16)
    v_all[:, HD : 2 * HD] = jnp.ones((2 * tok, HD), BF16)

    chunks = tok // CHUNK
    chunk_bits = CHUNK.bit_length() - 1
    row = lax.broadcasted_iota(jnp.int32, (CHUNK, CHUNK), 0)
    col = lax.broadcasted_iota(jnp.int32, (CHUNK, CHUNK), 1)
    differ = jnp.bitwise_xor(row, col)
    causal = col <= row
    stride = 2 * q_heads
    for h in range(heads):
        lanes = slice(h * HD, (h + 1) * HD)
        weight = jnp.full((CHUNK, CHUNK), table_ref[h, 0], F32)
        for level in range(1, chunk_bits + 1):
            weight = jnp.where(differ >= 2 ** (level - 1), table_ref[h, level], weight)
        weight = jnp.where(causal, weight, 0.0)
        groups = {}
        for c in range(chunks):
            here = slice(c * CHUNK, (c + 1) * CHUNK)
            q = x_ref[0, here, lanes]
            k = x_ref[1, here, lanes]
            v = x_ref[2, here, lanes]
            prefix = cross_ref[h]
            bit = 0
            while (1 << bit) <= c:
                if (c >> bit) & 1:
                    prefix = prefix + table_ref[h, chunk_bits + bit + 1] * states[groups[bit, (c >> bit) - 1]]
                bit += 1
            tile = (nt_dot(q, k) * weight).astype(BF16)
            total = jnp.dot(
                jnp.concatenate([tile, q], axis=1),
                jnp.concatenate([v, prefix.astype(BF16)], axis=0),
                preferred_element_type=F32,
            )
            norm = total * lax.rsqrt(jnp.mean(total * total, axis=1, keepdims=True) + 1e-06)
            rows_out[pl.ds(c * CHUNK * stride + 2 * h, CHUNK, stride=stride), :] = norm
            if c < chunks - 1:
                state = tn_dot(k, v)
                bit, index = 0, c
                slot = len(groups)
                groups[0, c] = slot
                states[slot] = state
                while index & 1:
                    state = states[groups[bit, index - 1]] + state
                    bit, index = bit + 1, index >> 1
                    slot = len(groups)
                    groups[bit, index] = slot
                    states[slot] = state

    row = lax.broadcasted_iota(jnp.int32, (block, block), 0)
    col = lax.broadcasted_iota(jnp.int32, (block, block), 1)
    low = jnp.where(col >= row, 0.0, NEG).astype(F32)
    high = jnp.where(col <= row, 0.0, NEG).astype(F32)
    for index in range(tok // block):
        start = index * block
        before = tok - start
        for h in range(q_heads):
            q = sq_ref[start : start + block, h * HD : (h + 1) * HD]
            scores = nt_dot(jnp.concatenate([q, q], axis=1), k_all[start : start + tok + block, :])
            left = scores[:, :block] + low
            if before > block:
                left = jnp.concatenate([left, scores[:, block:before]], axis=1)
            right = scores[:, tok:] + high
            if before < tok:
                right = jnp.concatenate([scores[:, before:tok], right], axis=1)
            m_left = jnp.max(left, axis=1, keepdims=True)
            m_right = jnp.max(right, axis=1, keepdims=True)
            m = jnp.where(first, m_right, jnp.maximum(m_left, m_right))
            m_left = jnp.where(first, 1e30, m)
            probs = jnp.concatenate(
                [jnp.exp2(left - m_left).astype(BF16), jnp.exp2(right - m).astype(BF16)], axis=1
            )
            out = jnp.dot(probs, v_all[start : start + tok + block, :], preferred_element_type=F32)
            rows_out[pl.ds(start * stride + 2 * h + 1, block, stride=stride), :] = out[:, :HD] / out[:, HD:]
    out_ref[...] = rows_out[...].astype(BF16)


def layer_call(first, table, planes, cross, soft_q, kb, ko):
    _, tok, width = planes.shape
    heads = width // HD
    q_heads = soft_q.shape[1] // HD
    block = min(256, tok)
    smem = pl.BlockSpec(memory_space=pltpu.SMEM)
    vmem = pl.BlockSpec(memory_space=pltpu.VMEM)
    return pl.pallas_call(
        functools.partial(layer_kernel, heads, q_heads, block),
        in_specs=[smem, smem, vmem, vmem, vmem, vmem, vmem],
        out_specs=vmem,
        out_shape=jax.ShapeDtypeStruct((tok * 2 * q_heads, HD), BF16),
        scratch_shapes=[
            pltpu.VMEM((2 * tok, HD), F32),
            pltpu.VMEM((2 * tok, 2 * HD), BF16),
            pltpu.VMEM((2 * tok, 2 * HD), BF16),
            pltpu.VMEM((2 * (tok // CHUNK), HD, HD), F32),
            pltpu.VMEM((tok * 2 * q_heads, HD), F32),
        ],
    )(first, table, planes, cross, soft_q, kb, ko)


def local(lin_qkv, level_weights, soft_q, soft_kv):
    tok = lin_qkv.shape[0]
    heads = lin_qkv.shape[2] // HD
    q_heads = soft_q.shape[1] // HD
    group = HEADS_SM // KV_HEADS
    local_bits = tok.bit_length() - 1
    my_seq = lax.axis_index("seq")

    kv_index = lax.axis_index("head") * q_heads // group
    own_kv = lax.dynamic_slice_in_dim(soft_kv, kv_index * HD, HD, 2).reshape(2 * tok, HD)
    before = passed_along(own_kv, "seq", 1)

    planes = jnp.transpose(lin_qkv, (1, 0, 2))
    state = states_call(planes)
    group_sum = state
    cross_state = jnp.zeros((heads, HD, HD), F32)
    for bit_pos in range(lax.axis_size("seq").bit_length() - 1):
        partner = partner_2(group_sum, "seq", bit_pos)
        upper = jnp.right_shift(my_seq, bit_pos) % 2 == 1
        factor = jnp.where(upper, level_weights[local_bits + bit_pos + 1], 0.0)
        cross_state = cross_state + factor[:, None, None] * partner
        group_sum = group_sum + partner

    first = (my_seq == 0).astype(jnp.int32).reshape(1)
    table = jnp.transpose(level_weights)
    out = layer_call(first, table, planes, cross_state, soft_q, before, own_kv)
    out = out.reshape(tok, q_heads, 2, HD).transpose(0, 2, 1, 3)
    return out.reshape(tok, 2, q_heads * HD)


def solution(mesh):
    in_specs = (
        P(("groups", "seq"), None, "head"),
        P(None, "head"),
        P(("groups", "seq"), "head"),
        P(("groups", "seq"), None, None),
    )
    out_specs = P(("groups", "seq"), None, "head")
    return jax.shard_map(local, mesh=mesh, in_specs=in_specs, out_specs=out_specs, check_vma=False)
```

```python
import functools

import jax
import jax.numpy as jnp
import numpy as np
from jax import lax
from jax.experimental import pallas as pl
from jax.experimental.pallas import tpu as pltpu
from jax.sharding import PartitionSpec as P


HD = 128
HEADS_SM = 16
KV_HEADS = 2
CHUNK = 256
NEG = -1e30
FAR = 1e30
F32 = jnp.float32
BF16 = jnp.bfloat16
SCALE = float(np.log2(np.e) / np.sqrt(HD))
ANY = pl.BlockSpec(memory_space=pl.ANY)
SMEM = pl.BlockSpec(memory_space=pltpu.SMEM)
PARAMS = pltpu.CompilerParams(vmem_limit_bytes=32 * 2**20)


def partner_2(value, axis, distance):
    mask = 2**distance
    pairs = [(source, source ^ mask) for source in range(lax.axis_size(axis))]
    return lax.ppermute(value, axis, pairs)


def passed_along(x, axis, by):
    size = lax.axis_size(axis)
    pairs = [(i, i + by) for i in range(size) if 0 <= i + by < size]
    return lax.ppermute(x, axis, pairs)


def nt_dot(a, b):
    return lax.dot_general(a, b, (((1,), (1,)), ((), ())), preferred_element_type=F32)


def tn_dot(a, b):
    return lax.dot_general(a, b, (((0,), (0,)), ((), ())), preferred_element_type=F32)


def lanes(h):
    return slice(h * HD, (h + 1) * HD)


def states_kernel(heads, k_ref, v_ref, state_ref):
    @pl.when(pl.program_id(0) == 0)
    def _():
        state_ref[...] = jnp.zeros_like(state_ref)

    for h in range(heads):
        state_ref[h] += tn_dot(k_ref[0, :, lanes(h)], v_ref[0, :, lanes(h)])


def states_call(planes):
    _, tok, width = planes.shape
    heads = width // HD
    rows = tok // 2
    return pl.pallas_call(
        functools.partial(states_kernel, heads),
        grid=(tok // rows,),
        in_specs=[
            pl.BlockSpec((1, rows, width), lambda i: (1, i, 0)),
            pl.BlockSpec((1, rows, width), lambda i: (2, i, 0)),
        ],
        out_specs=pl.BlockSpec((heads, HD, HD), lambda i: (0, 0, 0)),
        out_shape=jax.ShapeDtypeStruct((heads, HD, HD), F32),
        compiler_params=PARAMS,
        cost_estimate=pl.CostEstimate(
            flops=2 * tok * width * HD, bytes_accessed=4 * tok * width, transcendentals=0
        ),
    )(planes, planes)


def linear_kernel(heads, table_ref, x_hbm, out_hbm, x_ref, out_ref, states, in_sems, out_sems):
    tok = x_ref.shape[1]
    chunks = tok // CHUNK
    bits = CHUNK.bit_length() - 1
    rows = [pl.ds(c * CHUNK, CHUNK) for c in range(chunks)]
    loads = [
        pltpu.make_async_copy(x_hbm.at[:, rows[c], :], x_ref.at[:, rows[c], :], in_sems.at[c])
        for c in range(chunks)
    ]
    for load in loads:
        load.start()
    row = lax.broadcasted_iota(jnp.int32, (CHUNK, CHUNK), 0)
    col = lax.broadcasted_iota(jnp.int32, (CHUNK, CHUNK), 1)
    differ = jnp.bitwise_xor(row, col)
    weights = []
    for h in range(heads):
        weight = jnp.full((CHUNK, CHUNK), table_ref[h, 0], F32)
        for level in range(1, bits + 1):
            weight = jnp.where(differ >= 2 ** (level - 1), table_ref[h, level], weight)
        weights.append(jnp.where(col <= row, weight, 0.0))
    groups = [{} for _ in range(heads)]
    stores = []
    for c in range(chunks):
        loads[c].wait()
        for h in range(heads):
            base = h * 2 * chunks
            q, k, v = (x_ref[part, rows[c], lanes(h)] for part in range(3))
            tile = (nt_dot(q, k) * weights[h]).astype(BF16)
            prefix, bit = None, 0
            while (1 << bit) <= c:
                if (c >> bit) & 1:
                    term = table_ref[h, bits + bit + 1] * states[base + groups[h][bit, (c >> bit) - 1]]
                    prefix = term if prefix is None else prefix + term
                bit += 1
            if prefix is None:
                total = jnp.dot(tile, v, preferred_element_type=F32)
            else:
                total = jnp.dot(
                    jnp.concatenate([tile, q], axis=1),
                    jnp.concatenate([v, prefix.astype(BF16)], axis=0),
                    preferred_element_type=F32,
                )
            out_ref[rows[c], lanes(h)] = total
            if c < chunks - 1:
                state, bit, index = tn_dot(k, v), 0, c
                slot = len(groups[h])
                groups[h][0, c] = slot
                states[base + slot] = state
                while index & 1:
                    state = states[base + groups[h][bit, index - 1]] + state
                    bit, index = bit + 1, index >> 1
                    slot = len(groups[h])
                    groups[h][bit, index] = slot
                    states[base + slot] = state
        store = pltpu.make_async_copy(out_ref.at[rows[c], :], out_hbm.at[rows[c], :], out_sems.at[c])
        store.start()
        stores.append(store)
    for store in stores:
        store.wait()


def linear_call(table, planes):
    _, tok, width = planes.shape
    heads = width // HD
    chunks = tok // CHUNK
    return pl.pallas_call(
        functools.partial(linear_kernel, heads),
        in_specs=[SMEM, ANY],
        out_specs=ANY,
        out_shape=jax.ShapeDtypeStruct((tok, width), F32),
        scratch_shapes=[
            pltpu.VMEM((3, tok, width), BF16),
            pltpu.VMEM((tok, width), F32),
            pltpu.VMEM((heads * 2 * chunks, HD, HD), F32),
            pltpu.SemaphoreType.DMA((chunks,)),
            pltpu.SemaphoreType.DMA((chunks,)),
        ],
        compiler_params=PARAMS,
        cost_estimate=pl.CostEstimate(
            flops=8 * tok * width * CHUNK, bytes_accessed=10 * tok * width, transcendentals=0
        ),
    )(table, planes)


def take_apart(pairs, stage, k_all, v_all, at, count):
    here = pl.ds(at, count)
    rows = pl.ds(2 * at, 2 * count)
    stage[rows, :] = pairs.astype(F32)
    keys = stage[pl.ds(2 * at, count, stride=2), :] * SCALE
    high = keys.astype(BF16)
    k_all[here, 0:HD] = high
    k_all[here, HD : 2 * HD] = (keys - high.astype(F32)).astype(BF16)
    v_all[here, 0:HD] = stage[pl.ds(2 * at + 1, count, stride=2), :].astype(BF16)
    v_all[here, HD : 2 * HD] = jnp.ones((count, HD), BF16)


def edge_masks(block):
    row = lax.broadcasted_iota(jnp.int32, (block, block), 0)
    col = lax.broadcasted_iota(jnp.int32, (block, block), 1)
    low = jnp.where(col >= row, 0.0, NEG).astype(F32)
    high = jnp.where(col <= row, 0.0, NEG).astype(F32)
    return low, high


def softmax_block(q, keys, values, before, masks, first):
    low, high = masks
    block, width = q.shape[0], keys.shape[0]
    scores = nt_dot(jnp.concatenate([q, q], axis=1), keys)
    left = scores[:, :block] + low
    if before > block:
        left = jnp.concatenate([left, scores[:, block:before]], axis=1)
    right = scores[:, width - block :] + high
    if before < width - block:
        right = jnp.concatenate([scores[:, before : width - block], right], axis=1)
    m_left = jnp.max(left, axis=1, keepdims=True)
    m_right = jnp.max(right, axis=1, keepdims=True)
    m = jnp.where(first, m_right, jnp.maximum(m_left, m_right))
    m_left = jnp.where(first, FAR, m)
    probs = jnp.concatenate([jnp.exp2(left - m_left).astype(BF16), jnp.exp2(right - m).astype(BF16)], axis=1)
    out = jnp.dot(probs, values, preferred_element_type=F32)
    return out[:, :HD] / out[:, HD:]


def late_kernel(q_heads, block, first_ref, q_ref, before_ref, own_ref, out_ref, stage, k_all, v_all):
    half = q_ref.shape[0]
    tok = 2 * half
    first = first_ref[0] > 0
    take_apart(before_ref[...], stage, k_all, v_all, 0, half)
    take_apart(own_ref[...], stage, k_all, v_all, half, tok)
    masks = edge_masks(block)
    for start in range(0, half, block):
        keys = k_all[start : start + tok + block, :]
        values = v_all[start : start + tok + block, :]
        for h in range(q_heads):
            q = q_ref[start : start + block, lanes(h)]
            out = softmax_block(q, keys, values, half - start, masks, first)
            out_ref[start : start + block, lanes(h)] = out.astype(BF16)


def late_call(first, soft_q, before_late, own_kv, block):
    tok, width = soft_q.shape
    half = tok // 2
    q_heads = width // HD
    whole = lambda i: (0, 0)
    return pl.pallas_call(
        functools.partial(late_kernel, q_heads, block),
        grid=(1,),
        in_specs=[
            SMEM,
            pl.BlockSpec((half, width), lambda i: (1, 0)),
            pl.BlockSpec(before_late.shape, whole),
            pl.BlockSpec(own_kv.shape, whole),
        ],
        out_specs=pl.BlockSpec((half, width), whole),
        out_shape=jax.ShapeDtypeStruct((half, width), BF16),
        scratch_shapes=[
            pltpu.VMEM((3 * tok, HD), F32),
            pltpu.VMEM((tok + half, 2 * HD), BF16),
            pltpu.VMEM((tok + half, 2 * HD), BF16),
        ],
        compiler_params=PARAMS,
        cost_estimate=pl.CostEstimate(
            flops=6 * half * tok * width, bytes_accessed=6 * tok * width, transcendentals=half * tok * q_heads
        ),
    )(first, soft_q, before_late, own_kv)


def last_kernel(
    heads, block, first_ref, q_hbm, lin_hbm, x_hbm, cross_hbm, early_hbm, late_hbm, own_hbm, soft_hbm, out_hbm,
    q_ref, lin_ref, x_ref, cross_ref, early_ref, late_ref, own_ref, soft_ref, mixed, packed,
    stage, k_all, v_all, in_sems, out_sems,
):
    half = q_ref.shape[0]
    tok = 2 * half
    first = first_ref[0] > 0
    stride = 2 * heads
    copies = [
        (late_hbm, late_ref),
        (early_hbm, early_ref),
        (own_hbm.at[pl.ds(0, tok), :], own_ref),
        (q_hbm.at[pl.ds(0, half), :], q_ref),
        (cross_hbm, cross_ref),
        (x_hbm.at[0], x_ref),
        (lin_hbm, lin_ref),
        (soft_hbm, soft_ref),
    ]
    loads = [pltpu.make_async_copy(src, dst, in_sems.at[i]) for i, (src, dst) in enumerate(copies)]
    for load in loads:
        load.start()
    masks = edge_masks(block)
    stores = []

    def linear_rows(start):
        rows = slice(start, start + block)
        for h in range(heads):
            total = lin_ref[rows, lanes(h)] + jnp.dot(
                x_ref[rows, lanes(h)], cross_ref[h].astype(BF16), preferred_element_type=F32
            )
            norm = total * lax.rsqrt(jnp.mean(total * total, axis=1, keepdims=True) + 1e-06)
            mixed[pl.ds(start * stride + 2 * h, block, stride=stride), :] = norm

    def send(start):
        rows = pl.ds(start * stride, block * stride)
        packed[rows, :] = mixed[rows, :].astype(BF16)
        store = pltpu.make_async_copy(packed.at[rows, :], out_hbm.at[rows, :], out_sems.at[start // block])
        store.start()
        stores.append(store)

    loads[0].wait()
    loads[1].wait()
    take_apart(early_ref[...], stage, k_all, v_all, 0, half)
    take_apart(late_ref[...], stage, k_all, v_all, half, half)
    loads[2].wait()
    take_apart(own_ref[...], stage, k_all, v_all, tok, half)
    loads[3].wait()
    for start in range(0, half, block):
        keys = k_all[start : start + tok + block, :]
        values = v_all[start : start + tok + block, :]
        for h in range(heads):
            out = softmax_block(q_ref[start : start + block, lanes(h)], keys, values, tok - start, masks, first)
            mixed[pl.ds(start * stride + 2 * h + 1, block, stride=stride), :] = out
        if start == 0:
            for load in loads[4:]:
                load.wait()
        linear_rows(start)
        send(start)
    for start in range(half, tok, block):
        for h in range(heads):
            mixed[pl.ds(start * stride + 2 * h + 1, block, stride=stride), :] = soft_ref[
                start - half : start - half + block, lanes(h)
            ].astype(F32)
        linear_rows(start)
        send(start)
    for store in stores:
        store.wait()


def last_call(first, soft_q, partial, planes, cross, early, late, own_kv, soft_late, block):
    tok, width = soft_q.shape
    half = tok // 2
    heads = width // HD
    return pl.pallas_call(
        functools.partial(last_kernel, heads, block),
        in_specs=[SMEM] + [ANY] * 8,
        out_specs=ANY,
        out_shape=jax.ShapeDtypeStruct((tok * 2 * heads, HD), BF16),
        scratch_shapes=[
            pltpu.VMEM((half, width), BF16),
            pltpu.VMEM((tok, width), F32),
            pltpu.VMEM((tok, width), BF16),
            pltpu.VMEM((heads, HD, HD), F32),
            pltpu.VMEM((tok, HD), BF16),
            pltpu.VMEM((tok, HD), BF16),
            pltpu.VMEM((tok, HD), BF16),
            pltpu.VMEM((half, width), BF16),
            pltpu.VMEM((tok * 2 * heads, HD), F32),
            pltpu.VMEM((tok * 2 * heads, HD), BF16),
            pltpu.VMEM((3 * tok, HD), F32),
            pltpu.VMEM((tok + half, 2 * HD), BF16),
            pltpu.VMEM((tok + half, 2 * HD), BF16),
            pltpu.SemaphoreType.DMA((8,)),
            pltpu.SemaphoreType.DMA((tok // block,)),
        ],
        compiler_params=PARAMS,
        cost_estimate=pl.CostEstimate(
            flops=8 * half * tok * width, bytes_accessed=14 * tok * width, transcendentals=half * tok * heads
        ),
    )(first, soft_q, partial, planes, cross, early, late, own_kv, soft_late)


def local(lin_qkv, level_weights, soft_q, soft_kv):
    tok = lin_qkv.shape[0]
    heads = lin_qkv.shape[2] // HD
    q_heads = soft_q.shape[1] // HD
    group = HEADS_SM // KV_HEADS
    local_bits = tok.bit_length() - 1
    block = min(256, tok // 2)
    my_seq = lax.axis_index("seq")

    kv_index = lax.axis_index("head") * q_heads // group
    own_kv = lax.dynamic_slice_in_dim(soft_kv, kv_index * HD, HD, 2).reshape(2 * tok, HD)
    late = passed_along(own_kv[tok:], "seq", 1)
    early = passed_along(own_kv[:tok], "seq", 1)

    planes = jnp.transpose(lin_qkv, (1, 0, 2))
    state = states_call(planes)
    group_sum = state
    cross_state = jnp.zeros((heads, HD, HD), F32)
    for bit_pos in range(lax.axis_size("seq").bit_length() - 1):
        sent = group_sum if bit_pos == 0 else group_sum.astype(BF16)
        partner = partner_2(sent, "seq", bit_pos)
        partner = partner.astype(F32)
        upper = jnp.right_shift(my_seq, bit_pos) % 2 == 1
        factor = jnp.where(upper, level_weights[local_bits + bit_pos + 1], 0.0)
        cross_state = cross_state + factor[:, None, None] * partner
        group_sum = group_sum + partner

    first = (my_seq == 0).astype(jnp.int32).reshape(1)
    table = jnp.transpose(level_weights)
    partial = linear_call(table, planes)
    soft_late = late_call(first, soft_q, late, own_kv, block)
    out = last_call(first, soft_q, partial, planes, cross_state, early, late, own_kv, soft_late, block)
    out = out.reshape(tok, q_heads, 2, HD).transpose(0, 2, 1, 3)
    return out.reshape(tok, 2, q_heads * HD)


def solution(mesh):
    in_specs = (
        P(("groups", "seq"), None, "head"),
        P(None, "head"),
        P(("groups", "seq"), "head"),
        P(("groups", "seq"), None, None),
    )
    out_specs = P(("groups", "seq"), None, "head")
    return jax.shard_map(local, mesh=mesh, in_specs=in_specs, out_specs=out_specs, check_vma=False)
```

```python
import functools

import jax
import jax.numpy as jnp
import numpy as np
from jax import lax
from jax.experimental import pallas as pl
from jax.experimental.pallas import tpu as pltpu
from jax.sharding import PartitionSpec as P


HD = 128
HEADS_SM = 16
KV_HEADS = 2
CHUNK = 256
NEG = -1e30
FAR = 1e30
F32 = jnp.float32
BF16 = jnp.bfloat16
SCALE = float(np.log2(np.e) / np.sqrt(HD))
ANY = pl.BlockSpec(memory_space=pl.ANY)
SMEM = pl.BlockSpec(memory_space=pltpu.SMEM)
VMEM = pl.BlockSpec(memory_space=pltpu.VMEM)
HBM = pl.BlockSpec(memory_space=pltpu.HBM)
PARAMS = pltpu.CompilerParams(vmem_limit_bytes=24 * 2**20)


def partner_2(value, axis, distance):
    mask = 2**distance
    pairs = [(source, source ^ mask) for source in range(lax.axis_size(axis))]
    return lax.ppermute(value, axis, pairs)


def passed_along(x, axis, by):
    size = lax.axis_size(axis)
    pairs = [(i, (i + by) % size) for i in range(size)]
    return lax.ppermute(x, axis, pairs)


def nt_dot(a, b):
    return lax.dot_general(a, b, (((1,), (1,)), ((), ())), preferred_element_type=F32)


def tn_dot(a, b):
    return lax.dot_general(a, b, (((0,), (0,)), ((), ())), preferred_element_type=F32)


def lanes(h):
    return slice(h * HD, (h + 1) * HD)


def pick_kernel(index_ref, kv_hbm, out_hbm, sem):
    copy = pltpu.make_async_copy(kv_hbm.at[:, index_ref[0]], out_hbm, sem)
    copy.start()
    copy.wait()


def pick_call(index, kv):
    tok, _, two, hd = kv.shape
    return pl.pallas_call(
        pick_kernel,
        in_specs=[SMEM, HBM],
        out_specs=VMEM,
        out_shape=jax.ShapeDtypeStruct((tok, two, hd), BF16),
        scratch_shapes=[pltpu.SemaphoreType.DMA(())],
        compiler_params=PARAMS,
        cost_estimate=pl.CostEstimate(flops=0, bytes_accessed=8 * tok * hd, transcendentals=0),
    )(index, pltpu.with_memory_space_constraint(kv, pltpu.HBM))


def states_kernel(heads, x_hbm, state_ref, kv_ref, sums, sems):
    half = kv_ref.shape[1] // 2
    pieces = [pl.ds(0, half), pl.ds(half, half)]
    loads = [
        pltpu.make_async_copy(x_hbm.at[pl.ds(1, 2), rows, :], kv_ref.at[:, rows, :], sems.at[i])
        for i, rows in enumerate(pieces)
    ]
    for load in loads:
        load.start()
    loads[0].wait()
    for h in range(heads):
        sums[h] = tn_dot(kv_ref[0, pieces[0], lanes(h)], kv_ref[1, pieces[0], lanes(h)])
    loads[1].wait()
    for h in range(heads):
        total = sums[h] + tn_dot(kv_ref[0, pieces[1], lanes(h)], kv_ref[1, pieces[1], lanes(h)])
        state_ref[h] = total.astype(BF16)


def states_call(planes):
    _, tok, width = planes.shape
    heads = width // HD
    return pl.pallas_call(
        functools.partial(states_kernel, heads),
        in_specs=[HBM],
        out_specs=VMEM,
        out_shape=jax.ShapeDtypeStruct((heads, HD, HD), BF16),
        scratch_shapes=[
            pltpu.VMEM((2, tok, width), BF16),
            pltpu.VMEM((heads, HD, HD), F32),
            pltpu.SemaphoreType.DMA((2,)),
        ],
        compiler_params=PARAMS,
        cost_estimate=pl.CostEstimate(
            flops=2 * tok * width * HD, bytes_accessed=4 * tok * width, transcendentals=0
        ),
    )(pltpu.with_memory_space_constraint(planes, pltpu.HBM))


def linear_kernel(heads, table_ref, x_ref, out_ref, states):
    tok = x_ref.shape[1]
    chunks = tok // CHUNK
    bits = CHUNK.bit_length() - 1
    rows = [pl.ds(c * CHUNK, CHUNK) for c in range(chunks)]
    row = lax.broadcasted_iota(jnp.int32, (CHUNK, CHUNK), 0)
    col = lax.broadcasted_iota(jnp.int32, (CHUNK, CHUNK), 1)
    differ = jnp.bitwise_xor(row, col)
    weights = []
    for h in range(heads):
        weight = jnp.full((CHUNK, CHUNK), table_ref[h, 0], F32)
        for level in range(1, bits + 1):
            weight = jnp.where(differ >= 2 ** (level - 1), table_ref[h, level], weight)
        weights.append(jnp.where(col <= row, weight, 0.0))
    groups = [{} for _ in range(heads)]
    for c in range(chunks):
        for h in range(heads):
            base = h * 2 * chunks
            q, k, v = (x_ref[part, rows[c], lanes(h)] for part in range(3))
            tile = (nt_dot(q, k) * weights[h]).astype(BF16)
            prefix, bit = None, 0
            while (1 << bit) <= c:
                if (c >> bit) & 1:
                    term = table_ref[h, bits + bit + 1] * states[base + groups[h][bit, (c >> bit) - 1]]
                    prefix = term if prefix is None else prefix + term
                bit += 1
            if prefix is None:
                total = jnp.dot(tile, v, preferred_element_type=F32)
            else:
                total = jnp.dot(
                    jnp.concatenate([tile, q], axis=1),
                    jnp.concatenate([v, prefix.astype(BF16)], axis=0),
                    preferred_element_type=F32,
                )
            out_ref[rows[c], lanes(h)] = total
            if c < chunks - 1:
                state, bit, index = tn_dot(k, v), 0, c
                slot = len(groups[h])
                groups[h][0, c] = slot
                states[base + slot] = state
                while index & 1:
                    state = states[base + groups[h][bit, index - 1]] + state
                    bit, index = bit + 1, index >> 1
                    slot = len(groups[h])
                    groups[h][bit, index] = slot
                    states[base + slot] = state


def linear_call(table, planes):
    _, tok, width = planes.shape
    heads = width // HD
    return pl.pallas_call(
        functools.partial(linear_kernel, heads),
        in_specs=[SMEM, VMEM],
        out_specs=VMEM,
        out_shape=jax.ShapeDtypeStruct((tok, width), F32),
        scratch_shapes=[pltpu.VMEM((heads * 2 * (tok // CHUNK), HD, HD), F32)],
        compiler_params=PARAMS,
        cost_estimate=pl.CostEstimate(
            flops=8 * tok * width * CHUNK, bytes_accessed=10 * tok * width, transcendentals=0
        ),
    )(table, planes)


def take_apart(pairs, stage, k_all, v_all, at, count):
    here = pl.ds(at, count)
    rows = pl.ds(2 * at, 2 * count)
    stage[rows, :] = pairs.astype(F32)
    keys = stage[pl.ds(2 * at, count, stride=2), :] * SCALE
    high = keys.astype(BF16)
    k_all[here, 0:HD] = high
    k_all[here, HD : 2 * HD] = (keys - high.astype(F32)).astype(BF16)
    v_all[here, 0:HD] = stage[pl.ds(2 * at + 1, count, stride=2), :].astype(BF16)
    v_all[here, HD : 2 * HD] = jnp.ones((count, HD), BF16)


def edge_masks(block):
    row = lax.broadcasted_iota(jnp.int32, (block, block), 0)
    col = lax.broadcasted_iota(jnp.int32, (block, block), 1)
    low = jnp.where(col >= row, 0.0, NEG).astype(F32)
    high = jnp.where(col <= row, 0.0, NEG).astype(F32)
    return low, high


def softmax_block(q, keys, values, before, masks, first):
    low, high = masks
    block, width = q.shape[0], keys.shape[0]
    scores = nt_dot(jnp.concatenate([q, q], axis=1), keys)
    left = scores[:, :block] + low
    if before > block:
        left = jnp.concatenate([left, scores[:, block:before]], axis=1)
    right = scores[:, width - block :] + high
    if before < width - block:
        right = jnp.concatenate([scores[:, before : width - block], right], axis=1)
    m_left = jnp.max(left, axis=1, keepdims=True)
    m_right = jnp.max(right, axis=1, keepdims=True)
    m = jnp.where(first, m_right, jnp.maximum(m_left, m_right))
    m_left = jnp.where(first, FAR, m)
    probs = jnp.concatenate([jnp.exp2(left - m_left).astype(BF16), jnp.exp2(right - m).astype(BF16)], axis=1)
    out = jnp.dot(probs, values, preferred_element_type=F32)
    return out[:, :HD] / out[:, HD:]


def late_kernel(heads, block, place_ref, q_ref, before_ref, own_ref, out_ref, k_all, v_all, stage):
    half = out_ref.shape[0]
    tok = 2 * half
    first = place_ref[0] == 0
    take_apart(before_ref[...], stage, k_all, v_all, 0, tok)
    take_apart(own_ref[...], stage, k_all, v_all, tok, tok)
    masks = edge_masks(block)
    for start in range(half, tok, block):
        keys = k_all[start : start + tok + block, :]
        values = v_all[start : start + tok + block, :]
        for h in range(heads):
            out = softmax_block(q_ref[start : start + block, lanes(h)], keys, values, tok - start, masks, first)
            out_ref[start - half : start - half + block, lanes(h)] = out.astype(BF16)


def late_call(place, soft_q, before, own_kv, block):
    tok, width = soft_q.shape
    half = tok // 2
    heads = width // HD
    both = jax.ShapeDtypeStruct((2 * tok, 2 * HD), BF16)
    return pl.pallas_call(
        functools.partial(late_kernel, heads, block),
        in_specs=[SMEM, VMEM, VMEM, VMEM],
        out_specs=[VMEM, VMEM, VMEM],
        out_shape=[jax.ShapeDtypeStruct((half, width), BF16), both, both],
        scratch_shapes=[pltpu.VMEM((4 * tok, HD), F32)],
        compiler_params=PARAMS,
        cost_estimate=pl.CostEstimate(
            flops=6 * half * tok * width, bytes_accessed=6 * tok * width, transcendentals=half * tok * heads
        ),
    )(place, soft_q, before, own_kv)


def last_kernel(
    heads, block, others, place_ref, table_ref, q_ref, lin_ref, x_ref, k_all, v_all, soft_ref, *refs
):
    state_refs = refs[: len(others)]
    out_hbm, mixed, packed, cross, out_sems = refs[len(others) :]
    tok = q_ref.shape[0]
    half = tok // 2
    place = place_ref[0]
    first = place == 0
    stride = 2 * heads
    local_bits = tok.bit_length() - 1
    masks = edge_masks(block)
    stores = []
    for h in range(heads):
        total = jnp.zeros((HD, HD), F32)
        for distance, ref in zip(others, state_refs):
            bits = distance.bit_length()
            earlier = jnp.bitwise_and(jnp.right_shift(place, bits - 1), 1) == 1
            factor = jnp.where(earlier, table_ref[h, local_bits + bits], 0.0)
            total = total + factor * ref[h].astype(F32)
        cross[h] = total.astype(BF16)

    def linear_rows(start):
        rows = slice(start, start + block)
        for h in range(heads):
            total = lin_ref[rows, lanes(h)] + jnp.dot(
                x_ref[0, rows, lanes(h)], cross[h], preferred_element_type=F32
            )
            norm = total * lax.rsqrt(jnp.mean(total * total, axis=1, keepdims=True) + 1e-06)
            mixed[pl.ds(start * stride + 2 * h, block, stride=stride), :] = norm

    def send(start):
        rows = pl.ds(start * stride, block * stride)
        packed[rows, :] = mixed[rows, :].astype(BF16)
        store = pltpu.make_async_copy(packed.at[rows, :], out_hbm.at[rows, :], out_sems.at[start // block])
        store.start()
        stores.append(store)

    for start in range(half, tok, block):
        for h in range(heads):
            mixed[pl.ds(start * stride + 2 * h + 1, block, stride=stride), :] = soft_ref[
                start - half : start - half + block, lanes(h)
            ].astype(F32)
        linear_rows(start)
        send(start)
    for start in range(0, half, block):
        keys = k_all[start : start + tok + block, :]
        values = v_all[start : start + tok + block, :]
        linear_rows(start)
        for h in range(heads):
            out = softmax_block(q_ref[start : start + block, lanes(h)], keys, values, tok - start, masks, first)
            mixed[pl.ds(start * stride + 2 * h + 1, block, stride=stride), :] = out
        send(start)
    for store in stores:
        store.wait()


def last_call(place, table, soft_q, partial, planes, k_all, v_all, soft_late, states, block):
    tok, width = soft_q.shape
    heads = width // HD
    others = tuple(distance for distance, _ in states)
    return pl.pallas_call(
        functools.partial(last_kernel, heads, block, others),
        in_specs=[SMEM, SMEM] + [VMEM] * (6 + len(others)),
        out_specs=ANY,
        out_shape=jax.ShapeDtypeStruct((tok * 2 * heads, HD), BF16),
        scratch_shapes=[
            pltpu.VMEM((tok * 2 * heads, HD), F32),
            pltpu.VMEM((tok * 2 * heads, HD), BF16),
            pltpu.VMEM((heads, HD, HD), BF16),
            pltpu.SemaphoreType.DMA((tok // block,)),
        ],
        compiler_params=PARAMS,
        cost_estimate=pl.CostEstimate(
            flops=8 * tok * tok * width // 2, bytes_accessed=14 * tok * width, transcendentals=tok * tok * heads // 2
        ),
    )(place, table, soft_q, partial, planes, k_all, v_all, soft_late, *[state for _, state in states])


def all_states(own):
    have = [(0, own)]
    for bit in reversed(range(lax.axis_size("seq").bit_length() - 1)):
        for distance, state in list(have):
            further = distance + (1 << bit)
            have.append((further, partner_2(state, "seq", bit)))
    return have[1:]


def local(lin_qkv, level_weights, soft_q, soft_kv):
    tok = lin_qkv.shape[0]
    q_heads = soft_q.shape[1] // HD
    group = HEADS_SM // KV_HEADS
    block = min(256, tok // 2)
    my_seq = lax.axis_index("seq")

    kv_index = lax.axis_index("head") * q_heads // group
    kv = soft_kv.reshape(tok, 2, KV_HEADS, HD).transpose(0, 2, 1, 3)
    own_kv = pick_call(kv_index.reshape(1), kv).reshape(2 * tok, HD)
    before = passed_along(own_kv, "seq", 1)

    planes = jnp.transpose(lin_qkv, (1, 0, 2))
    state = states_call(planes)
    states = all_states(state)

    place = my_seq.reshape(1)
    table = jnp.transpose(level_weights)
    partial = linear_call(table, planes)
    soft_late, k_all, v_all = late_call(place, soft_q, before, own_kv, block)
    out = last_call(place, table, soft_q, partial, planes, k_all, v_all, soft_late, states, block)
    out = out.reshape(tok, q_heads, 2, HD).transpose(0, 2, 1, 3)
    return out.reshape(tok, 2, q_heads * HD)


def solution(mesh):
    in_specs = (
        P(("groups", "seq"), None, "head"),
        P(None, "head"),
        P(("groups", "seq"), "head"),
        P(("groups", "seq"), None, None),
    )
    out_specs = P(("groups", "seq"), None, "head")
    return jax.shard_map(local, mesh=mesh, in_specs=in_specs, out_specs=out_specs, check_vma=False)
```

```python
import functools

import jax
import jax.numpy as jnp
import numpy as np
from jax import lax
from jax.experimental import pallas as pl
from jax.experimental.pallas import tpu as pltpu
from jax.sharding import PartitionSpec as P


HD = 128
HEADS_SM = 16
KV_HEADS = 2
CHUNK = 256
NEG = -1e30
FAR = 1e30
F32 = jnp.float32
BF16 = jnp.bfloat16
SCALE = float(np.log2(np.e) / np.sqrt(HD))
ANY = pl.BlockSpec(memory_space=pl.ANY)
SMEM = pl.BlockSpec(memory_space=pltpu.SMEM)
VMEM = pl.BlockSpec(memory_space=pltpu.VMEM)
HBM = pl.BlockSpec(memory_space=pltpu.HBM)
PARAMS = pltpu.CompilerParams(vmem_limit_bytes=24 * 2**20)


def partner_2(value, axis, distance):
    mask = 2**distance
    pairs = [(source, source ^ mask) for source in range(lax.axis_size(axis))]
    return lax.ppermute(value, axis, pairs)


def passed_along(x, axis, by):
    size = lax.axis_size(axis)
    pairs = [(i, (i + by) % size) for i in range(size)]
    return lax.ppermute(x, axis, pairs)


def nt_dot(a, b):
    return lax.dot_general(a, b, (((1,), (1,)), ((), ())), preferred_element_type=F32)


def tn_dot(a, b):
    return lax.dot_general(a, b, (((0,), (0,)), ((), ())), preferred_element_type=F32)


def lanes(h):
    return slice(h * HD, (h + 1) * HD)


def take_apart(pairs, stage, k_out, v_out):
    count = k_out.shape[0]
    stage[...] = pairs.astype(F32)
    keys = stage[pl.ds(0, count, stride=2), :] * SCALE
    high = keys.astype(BF16)
    k_out[:, 0:HD] = high
    k_out[:, HD : 2 * HD] = (keys - high.astype(F32)).astype(BF16)
    v_out[:, 0:HD] = stage[pl.ds(1, count, stride=2), :].astype(BF16)
    v_out[:, HD : 2 * HD] = jnp.ones((count, HD), BF16)


def first_kernel(heads, index_ref, kv_hbm, x_hbm, own_ref, state_ref, x_ref, sums, sems):
    half = x_ref.shape[1] // 2
    pieces = [pl.ds(0, half), pl.ds(half, half)]
    pick = pltpu.make_async_copy(kv_hbm.at[:, index_ref[0]], own_ref, sems.at[2])
    pick.start()
    loads = [
        pltpu.make_async_copy(x_hbm.at[pl.ds(1, 2), rows, :], x_ref.at[:, rows, :], sems.at[i])
        for i, rows in enumerate(pieces)
    ]
    for load in loads:
        load.start()
    loads[0].wait()
    for h in range(heads):
        sums[h] = tn_dot(x_ref[0, pieces[0], lanes(h)], x_ref[1, pieces[0], lanes(h)])
    loads[1].wait()
    for h in range(heads):
        total = sums[h] + tn_dot(x_ref[0, pieces[1], lanes(h)], x_ref[1, pieces[1], lanes(h)])
        state_ref[h] = total.astype(BF16)
    pick.wait()


def first_call(index, kv, planes):
    tok, _, two, hd = kv.shape
    width = planes.shape[2]
    heads = width // HD
    return pl.pallas_call(
        functools.partial(first_kernel, heads),
        in_specs=[SMEM, HBM, HBM],
        out_specs=[VMEM, VMEM],
        out_shape=[pltpu.VMEM((tok, two, hd), BF16), pltpu.VMEM((heads, HD, HD), BF16)],
        scratch_shapes=[
            pltpu.VMEM((2, tok, width), BF16),
            pltpu.VMEM((heads, HD, HD), F32),
            pltpu.SemaphoreType.DMA((3,)),
        ],
        compiler_params=PARAMS,
        cost_estimate=pl.CostEstimate(
            flops=2 * tok * width * HD, bytes_accessed=4 * tok * width, transcendentals=0
        ),
    )(index, pltpu.with_memory_space_constraint(kv, pltpu.HBM), pltpu.with_memory_space_constraint(planes, pltpu.HBM))


def linear_kernel(
    heads, table_ref, x_ref, own_ref, mine_ref, near_ref, out_ref, pair_ref, k_own, v_own, states, stage,
    raw, sem,
):
    load = pltpu.make_async_copy(own_ref, raw, sem)
    load.start()
    tok = x_ref.shape[1]
    chunks = tok // CHUNK
    bits = CHUNK.bit_length() - 1
    rows = [pl.ds(c * CHUNK, CHUNK) for c in range(chunks)]
    row = lax.broadcasted_iota(jnp.int32, (CHUNK, CHUNK), 0)
    col = lax.broadcasted_iota(jnp.int32, (CHUNK, CHUNK), 1)
    differ = jnp.bitwise_xor(row, col)
    weights = []
    for h in range(heads):
        weight = jnp.full((CHUNK, CHUNK), table_ref[h, 0], F32)
        for level in range(1, bits + 1):
            weight = jnp.where(differ >= 2 ** (level - 1), table_ref[h, level], weight)
        weights.append(jnp.where(col <= row, weight, 0.0))
    pair_ref[...] = (mine_ref[...].astype(F32) + near_ref[...].astype(F32)).astype(BF16)
    groups = [{} for _ in range(heads)]
    for c in range(chunks):
        for h in range(heads):
            base = h * 2 * chunks
            q, k, v = (x_ref[part, rows[c], lanes(h)] for part in range(3))
            tile = (nt_dot(q, k) * weights[h]).astype(BF16)
            prefix, bit = None, 0
            while (1 << bit) <= c:
                if (c >> bit) & 1:
                    term = table_ref[h, bits + bit + 1] * states[base + groups[h][bit, (c >> bit) - 1]]
                    prefix = term if prefix is None else prefix + term
                bit += 1
            if prefix is None:
                total = jnp.dot(tile, v, preferred_element_type=F32)
            else:
                total = jnp.dot(
                    jnp.concatenate([tile, q], axis=1),
                    jnp.concatenate([v, prefix.astype(BF16)], axis=0),
                    preferred_element_type=F32,
                )
            out_ref[rows[c], lanes(h)] = total
            if c < chunks - 1:
                state, bit, index = tn_dot(k, v), 0, c
                slot = len(groups[h])
                groups[h][0, c] = slot
                states[base + slot] = state
                while index & 1:
                    state = states[base + groups[h][bit, index - 1]] + state
                    bit, index = bit + 1, index >> 1
                    slot = len(groups[h])
                    groups[h][bit, index] = slot
                    states[base + slot] = state
    load.wait()
    take_apart(raw[...], stage, k_own, v_own)


def linear_call(table, planes, own_kv, mine, near):
    _, tok, width = planes.shape
    heads = width // HD
    keys = pltpu.VMEM((tok, 2 * HD), BF16)
    return pl.pallas_call(
        functools.partial(linear_kernel, heads),
        in_specs=[SMEM, VMEM, ANY, VMEM, VMEM],
        out_specs=[VMEM] * 4,
        out_shape=[pltpu.VMEM((tok, width), F32), pltpu.VMEM(mine.shape, BF16), keys, keys],
        scratch_shapes=[
            pltpu.VMEM((heads * 2 * (tok // CHUNK), HD, HD), F32),
            pltpu.VMEM((2 * tok, HD), F32),
            pltpu.VMEM((2 * tok, HD), BF16),
            pltpu.SemaphoreType.DMA(()),
        ],
        compiler_params=PARAMS,
        cost_estimate=pl.CostEstimate(
            flops=8 * tok * width * CHUNK, bytes_accessed=10 * tok * width, transcendentals=0
        ),
    )(table, planes, own_kv, mine, near)


def edge_masks(block):
    row = lax.broadcasted_iota(jnp.int32, (block, block), 0)
    col = lax.broadcasted_iota(jnp.int32, (block, block), 1)
    low = jnp.where(col >= row, 0.0, NEG).astype(F32)
    high = jnp.where(col <= row, 0.0, NEG).astype(F32)
    return low, high


def softmax_block(q, start, before, own, masks, first):
    low, high = masks
    block = q.shape[0]
    end = start + block
    twice = jnp.concatenate([q, q], axis=1)
    left = nt_dot(twice, before[0][start:, :])
    right = nt_dot(twice, own[0][:end, :])
    edge = left[:, :block] + low
    left = jnp.concatenate([edge, left[:, block:]], axis=1) if left.shape[1] > block else edge
    edge = right[:, start:] + high
    right = jnp.concatenate([right[:, :start], edge], axis=1) if start else edge
    m_left = jnp.max(left, axis=1, keepdims=True)
    m_right = jnp.max(right, axis=1, keepdims=True)
    m = jnp.where(first, m_right, jnp.maximum(m_left, m_right))
    m_left = jnp.where(first, FAR, m)
    out = jnp.dot(jnp.exp2(left - m_left).astype(BF16), before[1][start:, :], preferred_element_type=F32)
    out = out + jnp.dot(jnp.exp2(right - m).astype(BF16), own[1][:end, :], preferred_element_type=F32)
    return out[:, :HD] / out[:, HD:]


def late_kernel(
    heads, block, place_ref, q_ref, before_ref, k_own, v_own, out_ref, k_before, v_before, stage, raw, sem
):
    load = pltpu.make_async_copy(before_ref, raw, sem)
    load.start()
    half = out_ref.shape[0]
    tok = 2 * half
    first = place_ref[0] == 0
    masks = edge_masks(block)
    load.wait()
    take_apart(raw[...], stage, k_before, v_before)
    for start in range(half, tok, block):
        for h in range(heads):
            q = q_ref[start : start + block, lanes(h)]
            out = softmax_block(q, start, (k_before, v_before), (k_own, v_own), masks, first)
            out_ref[start - half : start - half + block, lanes(h)] = out.astype(BF16)


def late_call(place, soft_q, before, k_own, v_own, block):
    tok, width = soft_q.shape
    half = tok // 2
    heads = width // HD
    keys = pltpu.VMEM((tok, 2 * HD), BF16)
    return pl.pallas_call(
        functools.partial(late_kernel, heads, block),
        in_specs=[SMEM, VMEM, ANY, VMEM, VMEM],
        out_specs=[VMEM] * 3,
        out_shape=[pltpu.VMEM((half, width), BF16), keys, keys],
        scratch_shapes=[
            pltpu.VMEM((2 * tok, HD), F32),
            pltpu.VMEM((2 * tok, HD), BF16),
            pltpu.SemaphoreType.DMA(()),
        ],
        compiler_params=PARAMS,
        cost_estimate=pl.CostEstimate(
            flops=6 * half * tok * width, bytes_accessed=6 * tok * width, transcendentals=half * tok * heads
        ),
    )(place, soft_q, before, k_own, v_own)


def last_kernel(
    heads, block, rounds, place_ref, table_ref, q_ref, lin_ref, x_ref, k_before, v_before, k_own, v_own, soft_ref, *refs
):
    state_refs = refs[:rounds]
    out_hbm, mixed, packed, cross, out_sems = refs[rounds:]
    tok = q_ref.shape[0]
    half = tok // 2
    place = place_ref[0]
    first = place == 0
    stride = 2 * heads
    local_bits = tok.bit_length() - 1
    masks = edge_masks(block)
    stores = []
    for h in range(heads):
        total = jnp.zeros((HD, HD), F32)
        for bit, ref in enumerate(state_refs):
            earlier = jnp.bitwise_and(jnp.right_shift(place, bit), 1) == 1
            factor = jnp.where(earlier, table_ref[h, local_bits + bit + 1], 0.0)
            total = total + factor * ref[h].astype(F32)
        cross[h] = total.astype(BF16)

    def linear_rows(start):
        rows = slice(start, start + block)
        for h in range(heads):
            total = lin_ref[rows, lanes(h)] + jnp.dot(
                x_ref[0, rows, lanes(h)], cross[h], preferred_element_type=F32
            )
            norm = total * lax.rsqrt(jnp.mean(total * total, axis=1, keepdims=True) + 1e-06)
            mixed[pl.ds(start * stride + 2 * h, block, stride=stride), :] = norm

    def send(start):
        rows = pl.ds(start * stride, block * stride)
        packed[rows, :] = mixed[rows, :].astype(BF16)
        store = pltpu.make_async_copy(packed.at[rows, :], out_hbm.at[rows, :], out_sems.at[start // block])
        store.start()
        stores.append(store)

    for start in range(half, tok, block):
        for h in range(heads):
            mixed[pl.ds(start * stride + 2 * h + 1, block, stride=stride), :] = soft_ref[
                start - half : start - half + block, lanes(h)
            ].astype(F32)
        linear_rows(start)
        send(start)
    for start in range(0, half, block):
        linear_rows(start)
        for h in range(heads):
            q = q_ref[start : start + block, lanes(h)]
            out = softmax_block(q, start, (k_before, v_before), (k_own, v_own), masks, first)
            mixed[pl.ds(start * stride + 2 * h + 1, block, stride=stride), :] = out
        send(start)
    for store in stores:
        store.wait()


def last_call(place, table, soft_q, partial, planes, before, own, soft_late, states, block):
    tok, width = soft_q.shape
    heads = width // HD
    return pl.pallas_call(
        functools.partial(last_kernel, heads, block, len(states)),
        in_specs=[SMEM, SMEM] + [VMEM] * (8 + len(states)),
        out_specs=ANY,
        out_shape=jax.ShapeDtypeStruct((tok * 2 * heads, HD), BF16),
        scratch_shapes=[
            pltpu.VMEM((tok * 2 * heads, HD), F32),
            pltpu.VMEM((tok * 2 * heads, HD), BF16),
            pltpu.VMEM((heads, HD, HD), BF16),
            pltpu.SemaphoreType.DMA((tok // block,)),
        ],
        compiler_params=PARAMS,
        cost_estimate=pl.CostEstimate(
            flops=8 * tok * tok * width // 2, bytes_accessed=14 * tok * width, transcendentals=tok * tok * heads // 2
        ),
    )(place, table, soft_q, partial, planes, *before, *own, soft_late, *states)


def local(lin_qkv, level_weights, soft_q, soft_kv):
    tok = lin_qkv.shape[0]
    q_heads = soft_q.shape[1] // HD
    group = HEADS_SM // KV_HEADS
    block = min(256, tok // 2)
    my_seq = lax.axis_index("seq")

    kv_index = lax.axis_index("head") * q_heads // group
    kv = soft_kv.reshape(tok, 2, KV_HEADS, HD).transpose(0, 2, 1, 3)
    planes = jnp.transpose(lin_qkv, (1, 0, 2))
    place = my_seq.reshape(1)
    table = jnp.transpose(level_weights)
    own_kv, state = first_call(kv_index.reshape(1), kv, planes)
    own_kv = own_kv.reshape(2 * tok, HD)
    before = passed_along(own_kv, "seq", 1)
    near = partner_2(state, "seq", 0)
    partial, group_sum, *own = linear_call(table, planes, own_kv, state, near)
    states = [near]
    for bit in range(1, lax.axis_size("seq").bit_length() - 1):
        if bit > 1:
            group_sum = (group_sum.astype(F32) + states[-1].astype(F32)).astype(BF16)
        states.append(partner_2(group_sum, "seq", bit))
    soft_late, *earlier = late_call(place, soft_q, before, *own, block)
    out = last_call(place, table, soft_q, partial, planes, earlier, own, soft_late, states, block)
    out = out.reshape(tok, q_heads, 2, HD).transpose(0, 2, 1, 3)
    return out.reshape(tok, 2, q_heads * HD)


def solution(mesh):
    in_specs = (
        P(("groups", "seq"), None, "head"),
        P(None, "head"),
        P(("groups", "seq"), "head"),
        P(("groups", "seq"), None, None),
    )
    out_specs = P(("groups", "seq"), None, "head")
    return jax.shard_map(local, mesh=mesh, in_specs=in_specs, out_specs=out_specs, check_vma=False)
```

```python
import functools

import jax
import jax.numpy as jnp
import numpy as np
from jax import lax
from jax.experimental import pallas as pl
from jax.experimental.pallas import tpu as pltpu
from jax.sharding import PartitionSpec as P


HD = 128
HEADS_SM = 16
KV_HEADS = 2
CHUNK = 256
NEG = -1e30
FAR = 1e30
F32 = jnp.float32
BF16 = jnp.bfloat16
SCALE = float(np.log2(np.e) / np.sqrt(HD))
ANY = pl.BlockSpec(memory_space=pl.ANY)
SMEM = pl.BlockSpec(memory_space=pltpu.SMEM)
VMEM = pl.BlockSpec(memory_space=pltpu.VMEM)
HBM = pl.BlockSpec(memory_space=pltpu.HBM)
PARAMS = pltpu.CompilerParams(vmem_limit_bytes=24 * 2**20)


def partner_2(value, axis, distance):
    mask = 2**distance
    pairs = [(source, source ^ mask) for source in range(lax.axis_size(axis))]
    return lax.ppermute(value, axis, pairs)


def passed_along(x, axis, by):
    size = lax.axis_size(axis)
    pairs = [(i, (i + by) % size) for i in range(size)]
    return lax.ppermute(x, axis, pairs)


def nt_dot(a, b):
    return lax.dot_general(a, b, (((1,), (1,)), ((), ())), preferred_element_type=F32)


def tn_dot(a, b):
    return lax.dot_general(a, b, (((0,), (0,)), ((), ())), preferred_element_type=F32)


def lanes(h):
    return slice(h * HD, (h + 1) * HD)


def take_apart(pairs, stage, k_out, v_out):
    count = k_out.shape[0]
    stage[...] = pairs.astype(F32)
    keys = stage[pl.ds(0, count, stride=2), :] * SCALE
    high = keys.astype(BF16)
    k_out[:, 0:HD] = high
    k_out[:, HD : 2 * HD] = (keys - high.astype(F32)).astype(BF16)
    v_out[:, 0:HD] = stage[pl.ds(1, count, stride=2), :].astype(BF16)
    v_out[:, HD : 2 * HD] = jnp.ones((count, HD), BF16)


def first_kernel(heads, index_ref, kv_hbm, x_hbm, own_ref, state_ref, x_ref, sums, sems):
    half = x_ref.shape[1] // 2
    pieces = [pl.ds(0, half), pl.ds(half, half)]
    pick = pltpu.make_async_copy(kv_hbm.at[:, index_ref[0]], own_ref, sems.at[2])
    pick.start()
    loads = [
        pltpu.make_async_copy(x_hbm.at[pl.ds(1, 2), rows, :], x_ref.at[pl.ds(1, 2), rows, :], sems.at[i])
        for i, rows in enumerate(pieces)
    ]
    loads.append(pltpu.make_async_copy(x_hbm.at[0], x_ref.at[0], sems.at[3]))
    for load in loads:
        load.start()
    loads[0].wait()
    for h in range(heads):
        sums[h] = tn_dot(x_ref[1, pieces[0], lanes(h)], x_ref[2, pieces[0], lanes(h)])
    loads[1].wait()
    for h in range(heads):
        total = sums[h] + tn_dot(x_ref[1, pieces[1], lanes(h)], x_ref[2, pieces[1], lanes(h)])
        state_ref[h] = total.astype(BF16)
    pick.wait()
    loads[2].wait()


def first_call(index, kv, planes):
    tok, _, two, hd = kv.shape
    width = planes.shape[2]
    heads = width // HD
    return pl.pallas_call(
        functools.partial(first_kernel, heads),
        in_specs=[SMEM, HBM, HBM],
        out_specs=[VMEM] * 3,
        out_shape=[
            pltpu.VMEM((tok, two, hd), BF16),
            pltpu.VMEM((heads, HD, HD), BF16),
            pltpu.VMEM(planes.shape, BF16),
        ],
        scratch_shapes=[
            pltpu.VMEM((heads, HD, HD), F32),
            pltpu.SemaphoreType.DMA((4,)),
        ],
        compiler_params=PARAMS,
        cost_estimate=pl.CostEstimate(
            flops=2 * tok * width * HD, bytes_accessed=4 * tok * width, transcendentals=0
        ),
    )(index, pltpu.with_memory_space_constraint(kv, pltpu.HBM), pltpu.with_memory_space_constraint(planes, pltpu.HBM))


def linear_kernel(
    heads, table_ref, x_ref, own_ref, mine_ref, near_ref, out_ref, pair_ref, k_own, v_own, states, stage,
    raw, sem,
):
    load = pltpu.make_async_copy(own_ref, raw, sem)
    load.start()
    tok = x_ref.shape[1]
    chunks = tok // CHUNK
    bits = CHUNK.bit_length() - 1
    rows = [pl.ds(c * CHUNK, CHUNK) for c in range(chunks)]
    row = lax.broadcasted_iota(jnp.int32, (CHUNK, CHUNK), 0)
    col = lax.broadcasted_iota(jnp.int32, (CHUNK, CHUNK), 1)
    differ = jnp.bitwise_xor(row, col)
    weights = []
    for h in range(heads):
        weight = jnp.full((CHUNK, CHUNK), table_ref[h, 0], F32)
        for level in range(1, bits + 1):
            weight = jnp.where(differ >= 2 ** (level - 1), table_ref[h, level], weight)
        weights.append(jnp.where(col <= row, weight, 0.0))
    pair_ref[...] = (mine_ref[...].astype(F32) + near_ref[...].astype(F32)).astype(BF16)
    groups = [{} for _ in range(heads)]
    for c in range(chunks):
        for h in range(heads):
            base = h * 2 * chunks
            q, k, v = (x_ref[part, rows[c], lanes(h)] for part in range(3))
            tile = (nt_dot(q, k) * weights[h]).astype(BF16)
            prefix, bit = None, 0
            while (1 << bit) <= c:
                if (c >> bit) & 1:
                    term = table_ref[h, bits + bit + 1] * states[base + groups[h][bit, (c >> bit) - 1]]
                    prefix = term if prefix is None else prefix + term
                bit += 1
            if prefix is None:
                total = jnp.dot(tile, v, preferred_element_type=F32)
            else:
                total = jnp.dot(
                    jnp.concatenate([tile, q], axis=1),
                    jnp.concatenate([v, prefix.astype(BF16)], axis=0),
                    preferred_element_type=F32,
                )
            out_ref[rows[c], lanes(h)] = total
            if c < chunks - 1:
                state, bit, index = tn_dot(k, v), 0, c
                slot = len(groups[h])
                groups[h][0, c] = slot
                states[base + slot] = state
                while index & 1:
                    state = states[base + groups[h][bit, index - 1]] + state
                    bit, index = bit + 1, index >> 1
                    slot = len(groups[h])
                    groups[h][bit, index] = slot
                    states[base + slot] = state
    load.wait()
    take_apart(raw[...], stage, k_own, v_own)


def linear_call(table, planes, own_kv, mine, near):
    _, tok, width = planes.shape
    heads = width // HD
    keys = pltpu.VMEM((tok, 2 * HD), BF16)
    return pl.pallas_call(
        functools.partial(linear_kernel, heads),
        in_specs=[SMEM, VMEM, ANY, VMEM, VMEM],
        out_specs=[VMEM] * 4,
        out_shape=[pltpu.VMEM((tok, width), F32), pltpu.VMEM(mine.shape, BF16), keys, keys],
        scratch_shapes=[
            pltpu.VMEM((heads * 2 * (tok // CHUNK), HD, HD), F32),
            pltpu.VMEM((2 * tok, HD), F32),
            pltpu.VMEM((2 * tok, HD), BF16),
            pltpu.SemaphoreType.DMA(()),
        ],
        compiler_params=PARAMS,
        cost_estimate=pl.CostEstimate(
            flops=8 * tok * width * CHUNK, bytes_accessed=10 * tok * width, transcendentals=0
        ),
    )(table, planes, own_kv, mine, near)


def edge_masks(block):
    row = lax.broadcasted_iota(jnp.int32, (block, block), 0)
    col = lax.broadcasted_iota(jnp.int32, (block, block), 1)
    low = jnp.where(col >= row, 0.0, NEG).astype(F32)
    high = jnp.where(col <= row, 0.0, NEG).astype(F32)
    return low, high


def softmax_block(q, start, before, own, masks, first):
    low, high = masks
    block = q.shape[0]
    end = start + block
    twice = jnp.concatenate([q, q], axis=1)
    left = nt_dot(twice, before[0][start:, :])
    right = nt_dot(twice, own[0][:end, :])
    edge = left[:, :block] + low
    left = jnp.concatenate([edge, left[:, block:]], axis=1) if left.shape[1] > block else edge
    edge = right[:, start:] + high
    right = jnp.concatenate([right[:, :start], edge], axis=1) if start else edge
    m_left = jnp.max(left, axis=1, keepdims=True)
    m_right = jnp.max(right, axis=1, keepdims=True)
    m = jnp.where(first, m_right, jnp.maximum(m_left, m_right))
    m_left = jnp.where(first, FAR, m)
    out = jnp.dot(jnp.exp2(left - m_left).astype(BF16), before[1][start:, :], preferred_element_type=F32)
    out = out + jnp.dot(jnp.exp2(right - m).astype(BF16), own[1][:end, :], preferred_element_type=F32)
    return out[:, :HD] / out[:, HD:]


def late_kernel(
    heads, block, place_ref, q_ref, before_ref, k_own, v_own, out_ref, k_before, v_before, stage, raw, sem
):
    load = pltpu.make_async_copy(before_ref, raw, sem)
    load.start()
    half = out_ref.shape[0]
    tok = 2 * half
    first = place_ref[0] == 0
    masks = edge_masks(block)
    load.wait()
    take_apart(raw[...], stage, k_before, v_before)
    for start in range(half, tok, block):
        for h in range(heads):
            q = q_ref[start : start + block, lanes(h)]
            out = softmax_block(q, start, (k_before, v_before), (k_own, v_own), masks, first)
            out_ref[start - half : start - half + block, lanes(h)] = out.astype(BF16)


def late_call(place, soft_q, before, k_own, v_own, block):
    tok, width = soft_q.shape
    half = tok // 2
    heads = width // HD
    keys = pltpu.VMEM((tok, 2 * HD), BF16)
    return pl.pallas_call(
        functools.partial(late_kernel, heads, block),
        in_specs=[SMEM, VMEM, ANY, VMEM, VMEM],
        out_specs=[VMEM] * 3,
        out_shape=[pltpu.VMEM((half, width), BF16), keys, keys],
        scratch_shapes=[
            pltpu.VMEM((2 * tok, HD), F32),
            pltpu.VMEM((2 * tok, HD), BF16),
            pltpu.SemaphoreType.DMA(()),
        ],
        compiler_params=PARAMS,
        cost_estimate=pl.CostEstimate(
            flops=6 * half * tok * width, bytes_accessed=6 * tok * width, transcendentals=half * tok * heads
        ),
    )(place, soft_q, before, k_own, v_own)


def last_kernel(
    heads, block, rounds, place_ref, table_ref, q_ref, lin_ref, x_ref, k_before, v_before, k_own, v_own, soft_ref, *refs
):
    state_refs = refs[:rounds]
    out_hbm, mixed, packed, cross, out_sems = refs[rounds:]
    pairs = heads // 2 if heads % 2 == 0 else heads
    together = heads // pairs
    cross[...] = jnp.zeros_like(cross)
    tok = q_ref.shape[0]
    half = tok // 2
    place = place_ref[0]
    first = place == 0
    stride = 2 * heads
    local_bits = tok.bit_length() - 1
    masks = edge_masks(block)
    stores = []
    for h in range(heads):
        total = jnp.zeros((HD, HD), F32)
        for bit, ref in enumerate(state_refs):
            earlier = jnp.bitwise_and(jnp.right_shift(place, bit), 1) == 1
            factor = jnp.where(earlier, table_ref[h, local_bits + bit + 1], 0.0)
            total = total + factor * ref[h].astype(F32)
        at = slice(h % together * HD, (h % together + 1) * HD)
        cross[h // together, at, at] = total.astype(BF16)

    def linear_rows(start):
        rows = slice(start, start + block)
        for pair in range(pairs):
            wide = slice(pair * together * HD, (pair + 1) * together * HD)
            both = jnp.dot(x_ref[0, rows, wide], cross[pair], preferred_element_type=F32) + lin_ref[rows, wide]
            for i in range(together):
                total = both[:, lanes(i)]
                norm = total * lax.rsqrt(jnp.mean(total * total, axis=1, keepdims=True) + 1e-06)
                mixed[2 * (pair * together + i)] = norm

    def send(start):
        rows = pl.ds(start * stride, block * stride)
        packed[rows, :] = jnp.swapaxes(mixed[...], 0, 1).reshape(block * stride, HD).astype(BF16)
        store = pltpu.make_async_copy(packed.at[rows, :], out_hbm.at[rows, :], out_sems.at[start // block])
        store.start()
        stores.append(store)

    for start in range(half, tok, block):
        for h in range(heads):
            mixed[2 * h + 1] = soft_ref[start - half : start - half + block, lanes(h)].astype(F32)
        linear_rows(start)
        send(start)
    for start in range(0, half, block):
        linear_rows(start)
        for h in range(heads):
            q = q_ref[start : start + block, lanes(h)]
            mixed[2 * h + 1] = softmax_block(q, start, (k_before, v_before), (k_own, v_own), masks, first)
        send(start)
    for store in stores:
        store.wait()


def last_call(place, table, soft_q, partial, planes, before, own, soft_late, states, block):
    tok, width = soft_q.shape
    heads = width // HD
    return pl.pallas_call(
        functools.partial(last_kernel, heads, block, len(states)),
        in_specs=[SMEM, SMEM] + [VMEM] * (8 + len(states)),
        out_specs=ANY,
        out_shape=jax.ShapeDtypeStruct((tok * 2 * heads, HD), BF16),
        scratch_shapes=[
            pltpu.VMEM((2 * heads, block, HD), F32),
            pltpu.VMEM((tok * 2 * heads, HD), BF16),
            pltpu.VMEM((heads // 2, 2 * HD, 2 * HD) if heads % 2 == 0 else (heads, HD, HD), BF16),
            pltpu.SemaphoreType.DMA((tok // block,)),
        ],
        compiler_params=PARAMS,
        cost_estimate=pl.CostEstimate(
            flops=8 * tok * tok * width // 2, bytes_accessed=14 * tok * width, transcendentals=tok * tok * heads // 2
        ),
    )(place, table, soft_q, partial, planes, *before, *own, soft_late, *states)


def local(lin_qkv, level_weights, soft_q, soft_kv):
    tok = lin_qkv.shape[0]
    q_heads = soft_q.shape[1] // HD
    group = HEADS_SM // KV_HEADS
    block = min(256, tok // 2)
    my_seq = lax.axis_index("seq")

    kv_index = lax.axis_index("head") * q_heads // group
    kv = soft_kv.reshape(tok, 2, KV_HEADS, HD).transpose(0, 2, 1, 3)
    planes = jnp.transpose(lin_qkv, (1, 0, 2))
    place = my_seq.reshape(1)
    table = jnp.transpose(level_weights)
    own_kv, state, planes = first_call(kv_index.reshape(1), kv, planes)
    own_kv = own_kv.reshape(2 * tok, HD)
    before = passed_along(own_kv, "seq", 1)
    near = partner_2(state, "seq", 0)
    partial, group_sum, *own = linear_call(table, planes, own_kv, state, near)
    states = [near]
    for bit in range(1, lax.axis_size("seq").bit_length() - 1):
        if bit > 1:
            group_sum = (group_sum.astype(F32) + states[-1].astype(F32)).astype(BF16)
        states.append(partner_2(group_sum, "seq", bit))
    soft_late, *earlier = late_call(place, soft_q, before, *own, block)
    out = last_call(place, table, soft_q, partial, planes, earlier, own, soft_late, states, block)
    out = out.reshape(tok, q_heads, 2, HD).transpose(0, 2, 1, 3)
    return out.reshape(tok, 2, q_heads * HD)


def solution(mesh):
    in_specs = (
        P(("groups", "seq"), None, "head"),
        P(None, "head"),
        P(("groups", "seq"), "head"),
        P(("groups", "seq"), None, None),
    )
    out_specs = P(("groups", "seq"), None, "head")
    return jax.shard_map(local, mesh=mesh, in_specs=in_specs, out_specs=out_specs, check_vma=False)
```

```python
import functools

import jax
import jax.numpy as jnp
import numpy as np
from jax import lax
from jax.experimental import pallas as pl
from jax.experimental.pallas import tpu as pltpu
from jax.sharding import PartitionSpec as P


HD = 128
HEADS_SM = 16
KV_HEADS = 2
CHUNK = 256
NEG = -1e30
FAR = 1e30
F32 = jnp.float32
BF16 = jnp.bfloat16
SCALE = float(np.log2(np.e) / np.sqrt(HD))
ANY = pl.BlockSpec(memory_space=pl.ANY)
SMEM = pl.BlockSpec(memory_space=pltpu.SMEM)
VMEM = pl.BlockSpec(memory_space=pltpu.VMEM)
HBM = pl.BlockSpec(memory_space=pltpu.HBM)
PARAMS = pltpu.CompilerParams(vmem_limit_bytes=24 * 2**20)


def partner_2(value, axis, distance):
    mask = 2**distance
    pairs = [(source, source ^ mask) for source in range(lax.axis_size(axis))]
    return lax.ppermute(value, axis, pairs)


def passed_along(x, axis, by):
    size = lax.axis_size(axis)
    pairs = [(i, (i + by) % size) for i in range(size)]
    return lax.ppermute(x, axis, pairs)


def nt_dot(a, b):
    return lax.dot_general(a, b, (((1,), (1,)), ((), ())), preferred_element_type=F32)


def tn_dot(a, b):
    return lax.dot_general(a, b, (((0,), (0,)), ((), ())), preferred_element_type=F32)


def lanes(h):
    return slice(h * HD, (h + 1) * HD)


def take_apart(pairs, stage, k_out, v_out):
    count = k_out.shape[0]
    stage[...] = pairs.astype(F32)
    keys = stage[pl.ds(0, count, stride=2), :] * SCALE
    high = keys.astype(BF16)
    k_out[:, 0:HD] = high
    k_out[:, HD : 2 * HD] = (keys - high.astype(F32)).astype(BF16)
    v_out[:, 0:HD] = stage[pl.ds(1, count, stride=2), :].astype(BF16)
    v_out[:, HD : 2 * HD] = jnp.ones((count, HD), BF16)


def first_kernel(heads, index_ref, kv_hbm, x_hbm, own_ref, state_ref, x_ref, sums, sems):
    half = x_ref.shape[1] // 2
    pieces = [pl.ds(0, half), pl.ds(half, half)]
    pick = pltpu.make_async_copy(kv_hbm.at[:, index_ref[0]], own_ref, sems.at[2])
    pick.start()
    loads = [
        pltpu.make_async_copy(x_hbm.at[pl.ds(1, 2), rows, :], x_ref.at[pl.ds(1, 2), rows, :], sems.at[i])
        for i, rows in enumerate(pieces)
    ]
    loads.append(pltpu.make_async_copy(x_hbm.at[0], x_ref.at[0], sems.at[3]))
    for load in loads:
        load.start()
    loads[0].wait()
    for h in range(heads):
        sums[h] = tn_dot(x_ref[1, pieces[0], lanes(h)], x_ref[2, pieces[0], lanes(h)])
    loads[1].wait()
    for h in range(heads):
        total = sums[h] + tn_dot(x_ref[1, pieces[1], lanes(h)], x_ref[2, pieces[1], lanes(h)])
        state_ref[h] = total.astype(BF16)
    pick.wait()
    loads[2].wait()


def first_call(index, kv, planes):
    tok, _, two, hd = kv.shape
    width = planes.shape[2]
    heads = width // HD
    return pl.pallas_call(
        functools.partial(first_kernel, heads),
        in_specs=[SMEM, HBM, HBM],
        out_specs=[VMEM] * 3,
        out_shape=[
            pltpu.VMEM((tok, two, hd), BF16),
            pltpu.VMEM((heads, HD, HD), BF16),
            pltpu.VMEM(planes.shape, BF16),
        ],
        scratch_shapes=[
            pltpu.VMEM((heads, HD, HD), F32),
            pltpu.SemaphoreType.DMA((4,)),
        ],
        compiler_params=PARAMS,
        cost_estimate=pl.CostEstimate(
            flops=2 * tok * width * HD, bytes_accessed=4 * tok * width, transcendentals=0
        ),
    )(index, pltpu.with_memory_space_constraint(kv, pltpu.HBM), pltpu.with_memory_space_constraint(planes, pltpu.HBM))


def linear_kernel(
    heads, table_ref, x_ref, own_ref, mine_ref, near_ref, out_ref, pair_ref, k_own, v_own, states, stage,
    raw, sem,
):
    load = pltpu.make_async_copy(own_ref, raw, sem)
    load.start()
    tok = x_ref.shape[1]
    chunks = tok // CHUNK
    bits = CHUNK.bit_length() - 1
    rows = [pl.ds(c * CHUNK, CHUNK) for c in range(chunks)]
    row = lax.broadcasted_iota(jnp.int32, (CHUNK, CHUNK), 0)
    col = lax.broadcasted_iota(jnp.int32, (CHUNK, CHUNK), 1)
    differ = jnp.bitwise_xor(row, col)
    weights = []
    for h in range(heads):
        weight = jnp.full((CHUNK, CHUNK), table_ref[h, 0], F32)
        for level in range(1, bits + 1):
            weight = jnp.where(differ >= 2 ** (level - 1), table_ref[h, level], weight)
        weights.append(jnp.where(col <= row, weight, 0.0))
    pair_ref[...] = (mine_ref[...].astype(F32) + near_ref[...].astype(F32)).astype(BF16)
    groups = [{} for _ in range(heads)]
    for c in range(chunks):
        for h in range(heads):
            base = h * 2 * chunks
            q, k, v = (x_ref[part, rows[c], lanes(h)] for part in range(3))
            tile = (nt_dot(q, k) * weights[h]).astype(BF16)
            prefix, bit = None, 0
            while (1 << bit) <= c:
                if (c >> bit) & 1:
                    term = table_ref[h, bits + bit + 1] * states[base + groups[h][bit, (c >> bit) - 1]]
                    prefix = term if prefix is None else prefix + term
                bit += 1
            if prefix is None:
                total = jnp.dot(tile, v, preferred_element_type=F32)
            else:
                total = jnp.dot(
                    jnp.concatenate([tile, q], axis=1),
                    jnp.concatenate([v, prefix.astype(BF16)], axis=0),
                    preferred_element_type=F32,
                )
            out_ref[rows[c], lanes(h)] = total
            if c < chunks - 1:
                state, bit, index = tn_dot(k, v), 0, c
                slot = len(groups[h])
                groups[h][0, c] = slot
                states[base + slot] = state
                while index & 1:
                    state = states[base + groups[h][bit, index - 1]] + state
                    bit, index = bit + 1, index >> 1
                    slot = len(groups[h])
                    groups[h][bit, index] = slot
                    states[base + slot] = state
    load.wait()
    take_apart(raw[...], stage, k_own, v_own)


def linear_call(table, planes, own_kv, mine, near):
    _, tok, width = planes.shape
    heads = width // HD
    keys = pltpu.VMEM((tok, 2 * HD), BF16)
    return pl.pallas_call(
        functools.partial(linear_kernel, heads),
        in_specs=[SMEM, VMEM, ANY, VMEM, VMEM],
        out_specs=[VMEM] * 4,
        out_shape=[pltpu.VMEM((tok, width), F32), pltpu.VMEM(mine.shape, BF16), keys, keys],
        scratch_shapes=[
            pltpu.VMEM((heads * 2 * (tok // CHUNK), HD, HD), F32),
            pltpu.VMEM((2 * tok, HD), F32),
            pltpu.VMEM((2 * tok, HD), BF16),
            pltpu.SemaphoreType.DMA(()),
        ],
        compiler_params=PARAMS,
        cost_estimate=pl.CostEstimate(
            flops=8 * tok * width * CHUNK, bytes_accessed=10 * tok * width, transcendentals=0
        ),
    )(table, planes, own_kv, mine, near)


def own_kernel(heads, block, q_ref, k_own, v_own, sums_ref, top_ref):
    tok = q_ref.shape[0]
    row = lax.broadcasted_iota(jnp.int32, (block, block), 0)
    col = lax.broadcasted_iota(jnp.int32, (block, block), 1)
    mask = jnp.where(col <= row, 0.0, NEG).astype(F32)
    for start in range(0, tok, block):
        end = start + block
        for h in range(heads):
            q = q_ref[start:end, lanes(h)]
            scores = nt_dot(jnp.concatenate([q, q], axis=1), k_own[:end, :])
            edge = scores[:, start:] + mask
            scores = jnp.concatenate([scores[:, :start], edge], axis=1) if start else edge
            top = jnp.max(scores, axis=1, keepdims=True)
            sums_ref[h, start:end, :] = jnp.dot(
                jnp.exp2(scores - top).astype(BF16), v_own[:end, :], preferred_element_type=F32
            )
            top_ref[h, start:end, :] = jnp.broadcast_to(top, (block, HD))


def own_call(soft_q, k_own, v_own, block):
    tok, width = soft_q.shape
    heads = width // HD
    return pl.pallas_call(
        functools.partial(own_kernel, heads, block),
        in_specs=[VMEM] * 3,
        out_specs=[VMEM] * 2,
        out_shape=[pltpu.VMEM((heads, tok, 2 * HD), F32), pltpu.VMEM((heads, tok, HD), F32)],
        compiler_params=PARAMS,
        cost_estimate=pl.CostEstimate(
            flops=3 * tok * tok * width, bytes_accessed=6 * tok * width, transcendentals=tok * tok * heads // 2
        ),
    )(soft_q, k_own, v_own)


def last_kernel(
    heads, block, rounds, place_ref, table_ref, q_ref, lin_ref, x_ref, before_ref, sums_ref, top_ref, *refs
):
    state_refs = refs[:rounds]
    out_hbm, mixed, packed, cross, k_before, v_before, stage, raw, in_sem, out_sems = refs[rounds:]
    tok = q_ref.shape[0]
    load = pltpu.make_async_copy(before_ref, raw, in_sem)
    load.start()
    place = place_ref[0]
    first = place == 0
    stride = 2 * heads
    local_bits = tok.bit_length() - 1
    pairs = heads // 2 if heads % 2 == 0 else heads
    together = heads // pairs
    cross[...] = jnp.zeros_like(cross)
    for h in range(heads):
        total = jnp.zeros((HD, HD), F32)
        for bit, ref in enumerate(state_refs):
            earlier = jnp.bitwise_and(jnp.right_shift(place, bit), 1) == 1
            factor = jnp.where(earlier, table_ref[h, local_bits + bit + 1], 0.0)
            total = total + factor * ref[h].astype(F32)
        at = lanes(h % together)
        cross[h // together, at, at] = total.astype(BF16)
    for start in range(0, tok, block):
        rows = slice(start, start + block)
        for pair in range(pairs):
            wide = slice(pair * together * HD, (pair + 1) * together * HD)
            both = jnp.dot(x_ref[0, rows, wide], cross[pair], preferred_element_type=F32) + lin_ref[rows, wide]
            for i in range(together):
                total = both[:, lanes(i)]
                norm = total * lax.rsqrt(jnp.mean(total * total, axis=1, keepdims=True) + 1e-06)
                mixed[start // block, 2 * (pair * together + i)] = norm

    load.wait()
    take_apart(raw[...], stage, k_before, v_before)
    row = lax.broadcasted_iota(jnp.int32, (block, block), 0)
    col = lax.broadcasted_iota(jnp.int32, (block, block), 1)
    mask = jnp.where(col >= row, 0.0, NEG).astype(F32)
    stores = []
    for start in range(0, tok, block):
        index = start // block
        for h in range(heads):
            q = q_ref[start : start + block, lanes(h)]
            scores = nt_dot(jnp.concatenate([q, q], axis=1), k_before[start:, :])
            edge = scores[:, :block] + mask
            scores = jnp.concatenate([edge, scores[:, block:]], axis=1) if start + block < tok else edge
            top = jnp.max(scores, axis=1, keepdims=True)
            top_own = top_ref[h, start : start + block, 0:1]
            both = jnp.where(first, top_own, jnp.maximum(top, top_own))
            probs = jnp.exp2(scores - jnp.where(first, FAR, both)).astype(BF16)
            sums = jnp.dot(probs, v_before[start:, :], preferred_element_type=F32)
            sums = sums + sums_ref[h, start : start + block, :] * jnp.exp2(top_own - both)
            mixed[index, 2 * h + 1] = sums[:, :HD] / sums[:, HD:]
        rows = pl.ds(start * stride, block * stride)
        packed[rows, :] = jnp.swapaxes(mixed[index], 0, 1).reshape(block * stride, HD).astype(BF16)
        store = pltpu.make_async_copy(packed.at[rows, :], out_hbm.at[rows, :], out_sems.at[index])
        store.start()
        stores.append(store)
    for store in stores:
        store.wait()


def last_call(place, table, soft_q, partial, planes, before, sums, top, states, block):
    tok, width = soft_q.shape
    heads = width // HD
    return pl.pallas_call(
        functools.partial(last_kernel, heads, block, len(states)),
        in_specs=[SMEM, SMEM, VMEM, VMEM, VMEM, ANY, VMEM, VMEM] + [VMEM] * len(states),
        out_specs=ANY,
        out_shape=jax.ShapeDtypeStruct((tok * 2 * heads, HD), BF16),
        scratch_shapes=[
            pltpu.VMEM((tok // block, 2 * heads, block, HD), F32),
            pltpu.VMEM((tok * 2 * heads, HD), BF16),
            pltpu.VMEM((heads // 2, 2 * HD, 2 * HD) if heads % 2 == 0 else (heads, HD, HD), BF16),
            pltpu.VMEM((tok, 2 * HD), BF16),
            pltpu.VMEM((tok, 2 * HD), BF16),
            pltpu.VMEM((2 * tok, HD), F32),
            pltpu.VMEM((2 * tok, HD), BF16),
            pltpu.SemaphoreType.DMA(()),
            pltpu.SemaphoreType.DMA((tok // block,)),
        ],
        compiler_params=PARAMS,
        cost_estimate=pl.CostEstimate(
            flops=4 * tok * tok * width, bytes_accessed=14 * tok * width, transcendentals=tok * tok * heads // 2
        ),
    )(place, table, soft_q, partial, planes, before, sums, top, *states)


def local(lin_qkv, level_weights, soft_q, soft_kv):
    tok = lin_qkv.shape[0]
    q_heads = soft_q.shape[1] // HD
    group = HEADS_SM // KV_HEADS
    block = min(256, tok // 2)
    my_seq = lax.axis_index("seq")

    kv_index = lax.axis_index("head") * q_heads // group
    kv = soft_kv.reshape(tok, 2, KV_HEADS, HD).transpose(0, 2, 1, 3)
    planes = jnp.transpose(lin_qkv, (1, 0, 2))
    place = my_seq.reshape(1)
    table = jnp.transpose(level_weights)
    own_kv, state, planes = first_call(kv_index.reshape(1), kv, planes)
    own_kv = own_kv.reshape(2 * tok, HD)
    before = passed_along(own_kv, "seq", 1)
    near = partner_2(state, "seq", 0)
    partial, group_sum, *own = linear_call(table, planes, own_kv, state, near)
    states = [near]
    for bit in range(1, lax.axis_size("seq").bit_length() - 1):
        if bit > 1:
            group_sum = (group_sum.astype(F32) + states[-1].astype(F32)).astype(BF16)
        states.append(partner_2(group_sum, "seq", bit))
    sums, top = own_call(soft_q, *own, block)
    out = last_call(place, table, soft_q, partial, planes, before, sums, top, states, block)
    out = out.reshape(tok, q_heads, 2, HD).transpose(0, 2, 1, 3)
    return out.reshape(tok, 2, q_heads * HD)


def solution(mesh):
    in_specs = (
        P(("groups", "seq"), None, "head"),
        P(None, "head"),
        P(("groups", "seq"), "head"),
        P(("groups", "seq"), None, None),
    )
    out_specs = P(("groups", "seq"), None, "head")
    return jax.shard_map(local, mesh=mesh, in_specs=in_specs, out_specs=out_specs, check_vma=False)
```

```python
import functools

import jax
import jax.numpy as jnp
import numpy as np
from jax import lax
from jax.experimental import pallas as pl
from jax.experimental.pallas import tpu as pltpu
from jax.sharding import PartitionSpec as P


HD = 128
HEADS_SM = 16
KV_HEADS = 2
CHUNK = 256
NEG = -1e30
FAR = 1e30
F32 = jnp.float32
BF16 = jnp.bfloat16
SCALE = float(np.log2(np.e) / np.sqrt(HD))
ANY = pl.BlockSpec(memory_space=pl.ANY)
SMEM = pl.BlockSpec(memory_space=pltpu.SMEM)
VMEM = pl.BlockSpec(memory_space=pltpu.VMEM)
HBM = pl.BlockSpec(memory_space=pltpu.HBM)
PARAMS = pltpu.CompilerParams(vmem_limit_bytes=24 * 2**20)


def partner_2(value, axis, distance):
    mask = 2**distance
    pairs = [(source, source ^ mask) for source in range(lax.axis_size(axis))]
    return lax.ppermute(value, axis, pairs)


def passed_along(x, axis, by):
    size = lax.axis_size(axis)
    pairs = [(i, (i + by) % size) for i in range(size)]
    return lax.ppermute(x, axis, pairs)


def nt_dot(a, b):
    return lax.dot_general(a, b, (((1,), (1,)), ((), ())), preferred_element_type=F32)


def tn_dot(a, b):
    return lax.dot_general(a, b, (((0,), (0,)), ((), ())), preferred_element_type=F32)


def lanes(h):
    return slice(h * HD, (h + 1) * HD)


def take_apart(pairs, stage, k_out, v_out):
    count = k_out.shape[0]
    stage[...] = pairs.astype(F32)
    keys = stage[pl.ds(0, count, stride=2), :] * SCALE
    high = keys.astype(BF16)
    k_out[:, 0:HD] = high
    k_out[:, HD : 2 * HD] = (keys - high.astype(F32)).astype(BF16)
    v_out[:, 0:HD] = stage[pl.ds(1, count, stride=2), :].astype(BF16)
    v_out[:, HD : 2 * HD] = jnp.ones((count, HD), BF16)


def first_kernel(heads, index_ref, kv_hbm, x_hbm, own_ref, state_ref, x_ref, sums, sems):
    half = x_ref.shape[1] // 2
    pieces = [pl.ds(0, half), pl.ds(half, half)]
    pick = pltpu.make_async_copy(kv_hbm.at[:, index_ref[0]], own_ref, sems.at[2])
    pick.start()
    loads = [
        pltpu.make_async_copy(x_hbm.at[pl.ds(1, 2), rows, :], x_ref.at[pl.ds(1, 2), rows, :], sems.at[i])
        for i, rows in enumerate(pieces)
    ]
    loads.append(pltpu.make_async_copy(x_hbm.at[0], x_ref.at[0], sems.at[3]))
    for load in loads:
        load.start()
    loads[0].wait()
    for h in range(heads):
        sums[h] = tn_dot(x_ref[1, pieces[0], lanes(h)], x_ref[2, pieces[0], lanes(h)])
    loads[1].wait()
    for h in range(heads):
        total = sums[h] + tn_dot(x_ref[1, pieces[1], lanes(h)], x_ref[2, pieces[1], lanes(h)])
        state_ref[h] = total.astype(BF16)
    pick.wait()
    loads[2].wait()


def first_call(index, kv, planes):
    tok, _, two, hd = kv.shape
    width = planes.shape[2]
    heads = width // HD
    return pl.pallas_call(
        functools.partial(first_kernel, heads),
        in_specs=[SMEM, HBM, HBM],
        out_specs=[VMEM] * 3,
        out_shape=[
            pltpu.VMEM((tok, two, hd), BF16),
            pltpu.VMEM((heads, HD, HD), BF16),
            pltpu.VMEM(planes.shape, BF16),
        ],
        scratch_shapes=[
            pltpu.VMEM((heads, HD, HD), F32),
            pltpu.SemaphoreType.DMA((4,)),
        ],
        compiler_params=PARAMS,
        cost_estimate=pl.CostEstimate(
            flops=2 * tok * width * HD, bytes_accessed=4 * tok * width, transcendentals=0
        ),
    )(index, pltpu.with_memory_space_constraint(kv, pltpu.HBM), pltpu.with_memory_space_constraint(planes, pltpu.HBM))


def linear_kernel(
    heads, table_ref, x_ref, own_ref, mine_ref, near_ref, out_ref, pair_ref, k_own, v_own, states, stage,
    raw, sem,
):
    load = pltpu.make_async_copy(own_ref, raw, sem)
    load.start()
    tok = x_ref.shape[1]
    chunks = tok // CHUNK
    bits = CHUNK.bit_length() - 1
    rows = [pl.ds(c * CHUNK, CHUNK) for c in range(chunks)]
    row = lax.broadcasted_iota(jnp.int32, (CHUNK, CHUNK), 0)
    col = lax.broadcasted_iota(jnp.int32, (CHUNK, CHUNK), 1)
    differ = jnp.bitwise_xor(row, col)
    weights = []
    for h in range(heads):
        weight = jnp.full((CHUNK, CHUNK), table_ref[h, 0], F32)
        for level in range(1, bits + 1):
            weight = jnp.where(differ >= 2 ** (level - 1), table_ref[h, level], weight)
        weights.append(jnp.where(col <= row, weight, 0.0))
    pair_ref[...] = (mine_ref[...].astype(F32) + near_ref[...].astype(F32)).astype(BF16)
    groups = [{} for _ in range(heads)]
    for c in range(chunks):
        for h in range(heads):
            base = h * 2 * chunks
            q, k, v = (x_ref[part, rows[c], lanes(h)] for part in range(3))
            tile = (nt_dot(q, k) * weights[h]).astype(BF16)
            prefix, bit = None, 0
            while (1 << bit) <= c:
                if (c >> bit) & 1:
                    term = table_ref[h, bits + bit + 1] * states[base + groups[h][bit, (c >> bit) - 1]]
                    prefix = term if prefix is None else prefix + term
                bit += 1
            if prefix is None:
                total = jnp.dot(tile, v, preferred_element_type=F32)
            else:
                total = jnp.dot(
                    jnp.concatenate([tile, q], axis=1),
                    jnp.concatenate([v, prefix.astype(BF16)], axis=0),
                    preferred_element_type=F32,
                )
            out_ref[rows[c], lanes(h)] = total
            if c < chunks - 1:
                state, bit, index = tn_dot(k, v), 0, c
                slot = len(groups[h])
                groups[h][0, c] = slot
                states[base + slot] = state
                while index & 1:
                    state = states[base + groups[h][bit, index - 1]] + state
                    bit, index = bit + 1, index >> 1
                    slot = len(groups[h])
                    groups[h][bit, index] = slot
                    states[base + slot] = state
    load.wait()
    take_apart(raw[...], stage, k_own, v_own)


def linear_call(table, planes, own_kv, mine, near):
    _, tok, width = planes.shape
    heads = width // HD
    keys = pltpu.VMEM((tok, 2 * HD), BF16)
    return pl.pallas_call(
        functools.partial(linear_kernel, heads),
        in_specs=[SMEM, VMEM, ANY, VMEM, VMEM],
        out_specs=[VMEM] * 4,
        out_shape=[pltpu.VMEM((tok, width), F32), pltpu.VMEM(mine.shape, BF16), keys, keys],
        scratch_shapes=[
            pltpu.VMEM((heads * 2 * (tok // CHUNK), HD, HD), F32),
            pltpu.VMEM((2 * tok, HD), F32),
            pltpu.VMEM((2 * tok, HD), BF16),
            pltpu.SemaphoreType.DMA(()),
        ],
        compiler_params=PARAMS,
        cost_estimate=pl.CostEstimate(
            flops=8 * tok * width * CHUNK, bytes_accessed=10 * tok * width, transcendentals=0
        ),
    )(table, planes, own_kv, mine, near)


def attend_own(q_ref, k_own, v_own, start, block, h, sums_ref, top_ref, at):
    row = lax.broadcasted_iota(jnp.int32, (block, block), 0)
    col = lax.broadcasted_iota(jnp.int32, (block, block), 1)
    mask = jnp.where(col <= row, 0.0, NEG).astype(F32)
    end = start + block
    q = q_ref[start:end, lanes(h)]
    scores = nt_dot(jnp.concatenate([q, q], axis=1), k_own[:end, :])
    edge = scores[:, start:] + mask
    scores = jnp.concatenate([scores[:, :start], edge], axis=1) if start else edge
    top = jnp.max(scores, axis=1, keepdims=True)
    sums_ref[h, at : at + block, :] = jnp.dot(
        jnp.exp2(scores - top).astype(BF16), v_own[:end, :], preferred_element_type=F32
    )
    top_ref[h, at : at + block, :] = jnp.broadcast_to(top, (block, HD))


def own_kernel(heads, block, q_ref, k_own, v_own, sums_ref, top_ref):
    for start in range(0, sums_ref.shape[1], block):
        for h in range(heads):
            attend_own(q_ref, k_own, v_own, start, block, h, sums_ref, top_ref, start)


def own_call(soft_q, k_own, v_own, block):
    tok, width = soft_q.shape
    heads = width // HD
    rows = tok - block
    return pl.pallas_call(
        functools.partial(own_kernel, heads, block),
        in_specs=[VMEM] * 3,
        out_specs=[VMEM] * 2,
        out_shape=[pltpu.VMEM((heads, rows, 2 * HD), F32), pltpu.VMEM((heads, rows, HD), F32)],
        compiler_params=PARAMS,
        cost_estimate=pl.CostEstimate(
            flops=2 * tok * tok * width, bytes_accessed=6 * tok * width, transcendentals=tok * tok * heads // 2
        ),
    )(soft_q, k_own, v_own)


def last_kernel(
    heads, block, rounds, place_ref, table_ref, q_ref, lin_ref, x_ref, before_ref, k_own, v_own, sums_ref, top_ref, *refs
):
    state_refs = refs[:rounds]
    out_hbm, mixed, packed, cross, k_before, v_before, stage, raw, sums_end, top_end, in_sem, out_sems = refs[rounds:]
    tok = q_ref.shape[0]
    load = pltpu.make_async_copy(before_ref, raw, in_sem)
    load.start()
    place = place_ref[0]
    first = place == 0
    stride = 2 * heads
    local_bits = tok.bit_length() - 1
    pairs = heads // 2 if heads % 2 == 0 else heads
    together = heads // pairs
    cross[...] = jnp.zeros_like(cross)
    for h in range(heads):
        total = jnp.zeros((HD, HD), F32)
        for bit, ref in enumerate(state_refs):
            earlier = jnp.bitwise_and(jnp.right_shift(place, bit), 1) == 1
            factor = jnp.where(earlier, table_ref[h, local_bits + bit + 1], 0.0)
            total = total + factor * ref[h].astype(F32)
        at = lanes(h % together)
        cross[h // together, at, at] = total.astype(BF16)

    def linear_rows(start):
        rows = slice(start, start + block)
        for pair in range(pairs):
            wide = slice(pair * together * HD, (pair + 1) * together * HD)
            both = jnp.dot(x_ref[0, rows, wide], cross[pair], preferred_element_type=F32) + lin_ref[rows, wide]
            for i in range(together):
                total = both[:, lanes(i)]
                norm = total * lax.rsqrt(jnp.mean(total * total, axis=1, keepdims=True) + 1e-06)
                at = start * stride + 2 * (pair * together + i)
                mixed[pl.ds(at, block, stride=stride), :] = norm

    for h in range(heads):
        attend_own(q_ref, k_own, v_own, tok - block, block, h, sums_end, top_end, 0)
    load.wait()
    take_apart(raw[...], stage, k_before, v_before)
    row = lax.broadcasted_iota(jnp.int32, (block, block), 0)
    col = lax.broadcasted_iota(jnp.int32, (block, block), 1)
    mask = jnp.where(col >= row, 0.0, NEG).astype(F32)

    def copy_out(start):
        rows = pl.ds(start * stride, block * stride)
        return pltpu.make_async_copy(packed.at[rows, :], out_hbm.at[rows, :], out_sems.at[start // block])

    def send(start):
        rows = pl.ds(start * stride, block * stride)
        packed[rows, :] = mixed[rows, :].astype(BF16)
        copy_out(start).start()

    def attend(start):
        linear_rows(start)
        for h in range(heads):
            q = q_ref[start : start + block, lanes(h)]
            scores = nt_dot(jnp.concatenate([q, q], axis=1), k_before[start:, :])
            edge = scores[:, :block] + mask
            scores = jnp.concatenate([edge, scores[:, block:]], axis=1) if start + block < tok else edge
            top = jnp.max(scores, axis=1, keepdims=True)
            sums_own, top_own = (sums_end, top_end) if start + block == tok else (sums_ref, top_ref)
            at = 0 if start + block == tok else start
            sums_own, top_own = sums_own[h, at : at + block, :], top_own[h, at : at + block, :]
            both = jnp.where(first, top_own, jnp.maximum(top, top_own))
            off = jnp.where(first, FAR, both)
            probs = jnp.exp2(scores - jnp.concatenate([off] * (scores.shape[1] // HD), axis=1)).astype(BF16)
            sums = jnp.dot(probs, v_before[start:, :], preferred_element_type=F32)
            factor = jnp.exp2(top_own - both)
            sums = sums + sums_own * jnp.concatenate([factor, factor], axis=1)
            mixed[pl.ds(start * stride + 2 * h + 1, block, stride=stride), :] = sums[:, :HD] / sums[:, HD:]

    for start in range(0, tok, block):

        if start:
            send(start - block)
        attend(start)

    send(tok - block)
    for start in range(0, tok, block):
        copy_out(start).wait()


def last_call(place, table, soft_q, partial, planes, before, own, sums, top, states, block):
    tok, width = soft_q.shape
    heads = width // HD
    return pl.pallas_call(
        functools.partial(last_kernel, heads, block, len(states)),
        in_specs=[SMEM, SMEM, VMEM, VMEM, VMEM, ANY] + [VMEM] * (4 + len(states)),
        out_specs=ANY,
        out_shape=jax.ShapeDtypeStruct((tok * 2 * heads, HD), BF16),
        scratch_shapes=[
            pltpu.VMEM((tok * 2 * heads, HD), F32),
            pltpu.VMEM((tok * 2 * heads, HD), BF16),
            pltpu.VMEM((heads // 2, 2 * HD, 2 * HD) if heads % 2 == 0 else (heads, HD, HD), BF16),
            pltpu.VMEM((tok, 2 * HD), BF16),
            pltpu.VMEM((tok, 2 * HD), BF16),
            pltpu.VMEM((2 * tok, HD), F32),
            pltpu.VMEM((2 * tok, HD), BF16),
            pltpu.VMEM((heads, block, 2 * HD), F32),
            pltpu.VMEM((heads, block, HD), F32),
            pltpu.SemaphoreType.DMA(()),
            pltpu.SemaphoreType.DMA((tok // block,)),
        ],
        compiler_params=PARAMS,
        cost_estimate=pl.CostEstimate(
            flops=4 * tok * tok * width, bytes_accessed=14 * tok * width, transcendentals=tok * tok * heads // 2
        ),
    )(place, table, soft_q, partial, planes, before, *own, sums, top, *states)


def local(lin_qkv, level_weights, soft_q, soft_kv):
    tok = lin_qkv.shape[0]
    q_heads = soft_q.shape[1] // HD
    group = HEADS_SM // KV_HEADS
    block = min(256, tok // 2)
    my_seq = lax.axis_index("seq")

    kv_index = lax.axis_index("head") * q_heads // group
    kv = soft_kv.reshape(tok, 2, KV_HEADS, HD).transpose(0, 2, 1, 3)
    planes = jnp.transpose(lin_qkv, (1, 0, 2))
    place = my_seq.reshape(1)
    table = jnp.transpose(level_weights)
    own_kv, state, planes = first_call(kv_index.reshape(1), kv, planes)
    own_kv = own_kv.reshape(2 * tok, HD)
    before = passed_along(own_kv, "seq", 1)
    near = partner_2(state, "seq", 0)
    partial, group_sum, *own = linear_call(table, planes, own_kv, state, near)
    states = [near]
    for bit in range(1, lax.axis_size("seq").bit_length() - 1):
        if bit > 1:
            group_sum = (group_sum.astype(F32) + states[-1].astype(F32)).astype(BF16)
        states.append(partner_2(group_sum, "seq", bit))
    sums, top = own_call(soft_q, *own, block)
    out = last_call(place, table, soft_q, partial, planes, before, own, sums, top, states, block)
    out = out.reshape(tok, q_heads, 2, HD).transpose(0, 2, 1, 3)
    return out.reshape(tok, 2, q_heads * HD)


def solution(mesh):
    in_specs = (
        P(("groups", "seq"), None, "head"),
        P(None, "head"),
        P(("groups", "seq"), "head"),
        P(("groups", "seq"), None, None),
    )
    out_specs = P(("groups", "seq"), None, "head")
    return jax.shard_map(local, mesh=mesh, in_specs=in_specs, out_specs=out_specs, check_vma=False)
```

```python
import functools

import jax
import jax.numpy as jnp
import numpy as np
from jax import lax
from jax.experimental import pallas as pl
from jax.experimental.pallas import tpu as pltpu
from jax.sharding import PartitionSpec as P


HD = 128
HEADS_SM = 16
KV_HEADS = 2
CHUNK = 256
NEG = -1e30
FAR = 1e30
F32 = jnp.float32
BF16 = jnp.bfloat16
SCALE = float(np.log2(np.e) / np.sqrt(HD))
ANY = pl.BlockSpec(memory_space=pl.ANY)
SMEM = pl.BlockSpec(memory_space=pltpu.SMEM)
VMEM = pl.BlockSpec(memory_space=pltpu.VMEM)
HBM = pl.BlockSpec(memory_space=pltpu.HBM)
PARAMS = pltpu.CompilerParams(vmem_limit_bytes=24 * 2**20)


def partner_2(value, axis, distance):
    mask = 2**distance
    pairs = [(source, source ^ mask) for source in range(lax.axis_size(axis))]
    return lax.ppermute(value, axis, pairs)


def passed_along(x, axis, by):
    size = lax.axis_size(axis)
    pairs = [(i, (i + by) % size) for i in range(size)]
    return lax.ppermute(x, axis, pairs)


def nt_dot(a, b):
    return lax.dot_general(a, b, (((1,), (1,)), ((), ())), preferred_element_type=F32)


def tn_dot(a, b):
    return lax.dot_general(a, b, (((0,), (0,)), ((), ())), preferred_element_type=F32)


def lanes(h):
    return slice(h * HD, (h + 1) * HD)


def take_apart(pairs, stage, k_out, v_out):
    count = k_out.shape[0]
    stage[...] = pairs.astype(F32)
    keys = stage[pl.ds(0, count, stride=2), :] * SCALE
    high = keys.astype(BF16)
    k_out[:, 0:HD] = high
    k_out[:, HD : 2 * HD] = (keys - high.astype(F32)).astype(BF16)
    v_out[:, 0:HD] = stage[pl.ds(1, count, stride=2), :].astype(BF16)
    v_out[:, HD : 2 * HD] = jnp.ones((count, HD), BF16)


def first_kernel(heads, index_ref, kv_hbm, x_hbm, own_ref, state_ref, x_ref, sums, sems):
    half = x_ref.shape[1] // 2
    pieces = [pl.ds(0, half), pl.ds(half, half)]
    pick = pltpu.make_async_copy(kv_hbm.at[:, index_ref[0]], own_ref, sems.at[2])
    pick.start()
    loads = [
        pltpu.make_async_copy(x_hbm.at[pl.ds(1, 2), rows, :], x_ref.at[pl.ds(1, 2), rows, :], sems.at[i])
        for i, rows in enumerate(pieces)
    ]
    loads.append(pltpu.make_async_copy(x_hbm.at[0], x_ref.at[0], sems.at[3]))
    for load in loads:
        load.start()
    loads[0].wait()
    for h in range(heads):
        sums[h] = tn_dot(x_ref[1, pieces[0], lanes(h)], x_ref[2, pieces[0], lanes(h)])
    loads[1].wait()
    for h in range(heads):
        total = sums[h] + tn_dot(x_ref[1, pieces[1], lanes(h)], x_ref[2, pieces[1], lanes(h)])
        state_ref[h] = total.astype(BF16)
    pick.wait()
    loads[2].wait()


def first_call(index, kv, planes):
    tok, _, two, hd = kv.shape
    width = planes.shape[2]
    heads = width // HD
    return pl.pallas_call(
        functools.partial(first_kernel, heads),
        in_specs=[SMEM, HBM, HBM],
        out_specs=[VMEM] * 3,
        out_shape=[
            pltpu.VMEM((tok, two, hd), BF16),
            pltpu.VMEM((heads, HD, HD), BF16),
            pltpu.VMEM(planes.shape, BF16),
        ],
        scratch_shapes=[
            pltpu.VMEM((heads, HD, HD), F32),
            pltpu.SemaphoreType.DMA((4,)),
        ],
        compiler_params=PARAMS,
        cost_estimate=pl.CostEstimate(
            flops=2 * tok * width * HD, bytes_accessed=4 * tok * width, transcendentals=0
        ),
    )(index, pltpu.with_memory_space_constraint(kv, pltpu.HBM), pltpu.with_memory_space_constraint(planes, pltpu.HBM))


def linear_kernel(
    heads, table_ref, x_ref, own_ref, mine_ref, near_ref, out_ref, pair_ref, k_own, v_own, states, stage,
    raw, sem,
):
    load = pltpu.make_async_copy(own_ref, raw, sem)
    load.start()
    tok = x_ref.shape[1]
    chunks = tok // CHUNK
    bits = CHUNK.bit_length() - 1
    rows = [pl.ds(c * CHUNK, CHUNK) for c in range(chunks)]
    row = lax.broadcasted_iota(jnp.int32, (CHUNK, CHUNK), 0)
    col = lax.broadcasted_iota(jnp.int32, (CHUNK, CHUNK), 1)
    differ = jnp.bitwise_xor(row, col)
    weights = []
    for h in range(heads):
        weight = jnp.full((CHUNK, CHUNK), table_ref[h, 0], F32)
        for level in range(1, bits + 1):
            weight = jnp.where(differ >= 2 ** (level - 1), table_ref[h, level], weight)
        weights.append(jnp.where(col <= row, weight, 0.0))
    pair_ref[...] = (mine_ref[...].astype(F32) + near_ref[...].astype(F32)).astype(BF16)
    groups = [{} for _ in range(heads)]
    for c in range(chunks):
        for h in range(heads):
            base = h * 2 * chunks
            q, k, v = (x_ref[part, rows[c], lanes(h)] for part in range(3))
            tile = (nt_dot(q, k) * weights[h]).astype(BF16)
            prefix, bit = None, 0
            while (1 << bit) <= c:
                if (c >> bit) & 1:
                    term = table_ref[h, bits + bit + 1] * states[base + groups[h][bit, (c >> bit) - 1]]
                    prefix = term if prefix is None else prefix + term
                bit += 1
            if prefix is None:
                total = jnp.dot(tile, v, preferred_element_type=F32)
            else:
                total = jnp.dot(
                    jnp.concatenate([tile, q], axis=1),
                    jnp.concatenate([v, prefix.astype(BF16)], axis=0),
                    preferred_element_type=F32,
                )
            out_ref[rows[c], lanes(h)] = total
            if c < chunks - 1:
                state, bit, index = tn_dot(k, v), 0, c
                slot = len(groups[h])
                groups[h][0, c] = slot
                states[base + slot] = state
                while index & 1:
                    state = states[base + groups[h][bit, index - 1]] + state
                    bit, index = bit + 1, index >> 1
                    slot = len(groups[h])
                    groups[h][bit, index] = slot
                    states[base + slot] = state
    load.wait()
    take_apart(raw[...], stage, k_own, v_own)


def linear_call(table, planes, own_kv, mine, near):
    _, tok, width = planes.shape
    heads = width // HD
    keys = pltpu.VMEM((tok, 2 * HD), BF16)
    return pl.pallas_call(
        functools.partial(linear_kernel, heads),
        in_specs=[SMEM, VMEM, ANY, VMEM, VMEM],
        out_specs=[VMEM] * 4,
        out_shape=[pltpu.VMEM((tok, width), F32), pltpu.VMEM(mine.shape, BF16), keys, keys],
        scratch_shapes=[
            pltpu.VMEM((heads * 2 * (tok // CHUNK), HD, HD), F32),
            pltpu.VMEM((2 * tok, HD), F32),
            pltpu.VMEM((2 * tok, HD), BF16),
            pltpu.SemaphoreType.DMA(()),
        ],
        compiler_params=PARAMS,
        cost_estimate=pl.CostEstimate(
            flops=8 * tok * width * CHUNK, bytes_accessed=10 * tok * width, transcendentals=0
        ),
    )(table, planes, own_kv, mine, near)


def own_kernel(heads, block, q_ref, k_own, v_own, sums_ref, top_ref):
    tok = q_ref.shape[0]
    row = lax.broadcasted_iota(jnp.int32, (block, block), 0)
    col = lax.broadcasted_iota(jnp.int32, (block, block), 1)
    mask = jnp.where(col <= row, 0.0, NEG).astype(F32)
    for start in range(0, tok, block):
        end = start + block
        for h in range(heads):
            q = q_ref[start:end, lanes(h)]
            scores = nt_dot(jnp.concatenate([q, q], axis=1), k_own[:end, :])
            edge = scores[:, start:] + mask
            scores = jnp.concatenate([scores[:, :start], edge], axis=1) if start else edge
            top = jnp.max(scores, axis=1, keepdims=True)
            sums_ref[h, start:end, :] = jnp.dot(
                jnp.exp2(scores - top).astype(BF16), v_own[:end, :], preferred_element_type=F32
            )
            top_ref[h, start:end, :] = jnp.broadcast_to(top, (block, HD))


def own_call(soft_q, k_own, v_own, block):
    tok, width = soft_q.shape
    heads = width // HD
    return pl.pallas_call(
        functools.partial(own_kernel, heads, block),
        in_specs=[VMEM] * 3,
        out_specs=[VMEM] * 2,
        out_shape=[pltpu.VMEM((heads, tok, 2 * HD), F32), pltpu.VMEM((heads, tok, HD), F32)],
        compiler_params=PARAMS,
        cost_estimate=pl.CostEstimate(
            flops=3 * tok * tok * width, bytes_accessed=6 * tok * width, transcendentals=tok * tok * heads // 2
        ),
    )(soft_q, k_own, v_own)


def last_kernel(
    heads, block, rounds, place_ref, table_ref, q_ref, lin_ref, x_ref, before_ref, sums_ref, top_ref, *refs
):
    state_refs = refs[:rounds]
    out_hbm, mixed, packed, cross, k_before, v_before, stage, raw, in_sem, out_sems = refs[rounds:]
    tok = q_ref.shape[0]
    load = pltpu.make_async_copy(before_ref, raw, in_sem)
    load.start()
    place = place_ref[0]
    first = place == 0
    stride = 2 * heads
    local_bits = tok.bit_length() - 1
    pairs = heads // 2 if heads % 2 == 0 else heads
    together = heads // pairs
    cross[...] = jnp.zeros_like(cross)
    for h in range(heads):
        total = jnp.zeros((HD, HD), F32)
        for bit, ref in enumerate(state_refs):
            earlier = jnp.bitwise_and(jnp.right_shift(place, bit), 1) == 1
            factor = jnp.where(earlier, table_ref[h, local_bits + bit + 1], 0.0)
            total = total + factor * ref[h].astype(F32)
        at = lanes(h % together)
        cross[h // together, at, at] = total.astype(BF16)

    def linear_rows(start):
        rows = slice(start, start + block)
        for pair in range(pairs):
            wide = slice(pair * together * HD, (pair + 1) * together * HD)
            both = jnp.dot(x_ref[0, rows, wide], cross[pair], preferred_element_type=F32) + lin_ref[rows, wide]
            for i in range(together):
                total = both[:, lanes(i)]
                norm = total * lax.rsqrt(jnp.mean(total * total, axis=1, keepdims=True) + 1e-06)
                at = start * stride + 2 * (pair * together + i)
                mixed[pl.ds(at, block, stride=stride), :] = norm

    for start in range(0, tok // 2, block):
        linear_rows(start)

    load.wait()
    take_apart(raw[...], stage, k_before, v_before)
    row = lax.broadcasted_iota(jnp.int32, (block, block), 0)
    col = lax.broadcasted_iota(jnp.int32, (block, block), 1)
    mask = jnp.where(col >= row, 0.0, NEG).astype(F32)

    def copy_out(start):
        rows = pl.ds(start * stride, block * stride)
        return pltpu.make_async_copy(packed.at[rows, :], out_hbm.at[rows, :], out_sems.at[start // block])

    def send(start):
        rows = pl.ds(start * stride, block * stride)
        packed[rows, :] = mixed[rows, :].astype(BF16)
        copy_out(start).start()

    def attend(start):
        if start >= tok // 2:
            linear_rows(start)
        for h in range(heads):
            q = q_ref[start : start + block, lanes(h)]
            scores = nt_dot(jnp.concatenate([q, q], axis=1), k_before[start:, :])
            edge = scores[:, :block] + mask
            scores = jnp.concatenate([edge, scores[:, block:]], axis=1) if start + block < tok else edge
            top = jnp.max(scores, axis=1, keepdims=True)
            top_own = top_ref[h, start : start + block, :]
            both = jnp.where(first, top_own, jnp.maximum(top, top_own))
            off = jnp.where(first, FAR, both)
            probs = jnp.exp2(scores - jnp.concatenate([off] * (scores.shape[1] // HD), axis=1)).astype(BF16)
            sums = jnp.dot(probs, v_before[start:, :], preferred_element_type=F32)
            factor = jnp.exp2(top_own - both)
            sums = sums + sums_ref[h, start : start + block, :] * jnp.concatenate([factor, factor], axis=1)
            mixed[pl.ds(start * stride + 2 * h + 1, block, stride=stride), :] = sums[:, :HD] / sums[:, HD:]

    for start in range(0, tok, block):

        if start:
            send(start - block)
        attend(start)

    send(tok - block)
    for start in range(0, tok, block):
        copy_out(start).wait()


def last_call(place, table, soft_q, partial, planes, before, sums, top, states, block):
    tok, width = soft_q.shape
    heads = width // HD
    return pl.pallas_call(
        functools.partial(last_kernel, heads, block, len(states)),
        in_specs=[SMEM, SMEM, VMEM, VMEM, VMEM, ANY, VMEM, VMEM] + [VMEM] * len(states),
        out_specs=ANY,
        out_shape=jax.ShapeDtypeStruct((tok * 2 * heads, HD), BF16),
        scratch_shapes=[
            pltpu.VMEM((tok * 2 * heads, HD), F32),
            pltpu.VMEM((tok * 2 * heads, HD), BF16),
            pltpu.VMEM((heads // 2, 2 * HD, 2 * HD) if heads % 2 == 0 else (heads, HD, HD), BF16),
            pltpu.VMEM((tok, 2 * HD), BF16),
            pltpu.VMEM((tok, 2 * HD), BF16),
            pltpu.VMEM((2 * tok, HD), F32),
            pltpu.VMEM((2 * tok, HD), BF16),
            pltpu.SemaphoreType.DMA(()),
            pltpu.SemaphoreType.DMA((tok // block,)),
        ],
        compiler_params=PARAMS,
        cost_estimate=pl.CostEstimate(
            flops=4 * tok * tok * width, bytes_accessed=14 * tok * width, transcendentals=tok * tok * heads // 2
        ),
    )(place, table, soft_q, partial, planes, before, sums, top, *states)


def local(lin_qkv, level_weights, soft_q, soft_kv):
    tok = lin_qkv.shape[0]
    q_heads = soft_q.shape[1] // HD
    group = HEADS_SM // KV_HEADS
    block = min(256, tok // 2)
    my_seq = lax.axis_index("seq")

    kv_index = lax.axis_index("head") * q_heads // group
    kv = soft_kv.reshape(tok, 2, KV_HEADS, HD).transpose(0, 2, 1, 3)
    planes = jnp.transpose(lin_qkv, (1, 0, 2))
    place = my_seq.reshape(1)
    table = jnp.transpose(level_weights)
    own_kv, state, planes = first_call(kv_index.reshape(1), kv, planes)
    own_kv = own_kv.reshape(2 * tok, HD)
    before = passed_along(own_kv, "seq", 1)
    near = partner_2(state, "seq", 0)
    partial, group_sum, *own = linear_call(table, planes, own_kv, state, near)
    states = [near]
    for bit in range(1, lax.axis_size("seq").bit_length() - 1):
        if bit > 1:
            group_sum = (group_sum.astype(F32) + states[-1].astype(F32)).astype(BF16)
        states.append(partner_2(group_sum, "seq", bit))
    sums, top = own_call(soft_q, *own, block)
    out = last_call(place, table, soft_q, partial, planes, before, sums, top, states, block)
    out = out.reshape(tok, q_heads, 2, HD).transpose(0, 2, 1, 3)
    return out.reshape(tok, 2, q_heads * HD)


def solution(mesh):
    in_specs = (
        P(("groups", "seq"), None, "head"),
        P(None, "head"),
        P(("groups", "seq"), "head"),
        P(("groups", "seq"), None, None),
    )
    out_specs = P(("groups", "seq"), None, "head")
    return jax.shard_map(local, mesh=mesh, in_specs=in_specs, out_specs=out_specs, check_vma=False)
```

```python
import functools

import jax
import jax.numpy as jnp
import numpy as np
from jax import lax
from jax.experimental import pallas as pl
from jax.experimental.pallas import tpu as pltpu
from jax.sharding import PartitionSpec as P


HD = 128
HEADS_SM = 16
KV_HEADS = 2
CHUNK = 256
NEG = -1e30
FAR = 1e30
F32 = jnp.float32
BF16 = jnp.bfloat16
SCALE = float(np.log2(np.e) / np.sqrt(HD))
ANY = pl.BlockSpec(memory_space=pl.ANY)
SMEM = pl.BlockSpec(memory_space=pltpu.SMEM)
VMEM = pl.BlockSpec(memory_space=pltpu.VMEM)
HBM = pl.BlockSpec(memory_space=pltpu.HBM)
PARAMS = pltpu.CompilerParams(vmem_limit_bytes=24 * 2**20)


def partner_2(value, axis, distance):
    mask = 2**distance
    pairs = [(source, source ^ mask) for source in range(lax.axis_size(axis))]
    return lax.ppermute(value, axis, pairs)


def passed_along(x, axis, by):
    size = lax.axis_size(axis)
    pairs = [(i, (i + by) % size) for i in range(size)]
    return lax.ppermute(x, axis, pairs)


def nt_dot(a, b):
    return lax.dot_general(a, b, (((1,), (1,)), ((), ())), preferred_element_type=F32)


def tn_dot(a, b):
    return lax.dot_general(a, b, (((0,), (0,)), ((), ())), preferred_element_type=F32)


def lanes(h):
    return slice(h * HD, (h + 1) * HD)


def take_apart(pairs, stage, k_out, v_out):
    count = k_out.shape[0]
    stage[...] = pairs.astype(F32)
    keys = stage[pl.ds(0, count, stride=2), :] * SCALE
    high = keys.astype(BF16)
    k_out[:, 0:HD] = high
    k_out[:, HD : 2 * HD] = (keys - high.astype(F32)).astype(BF16)
    v_out[:, 0:HD] = stage[pl.ds(1, count, stride=2), :].astype(BF16)
    v_out[:, HD : 2 * HD] = jnp.ones((count, HD), BF16)


def first_kernel(heads, index_ref, kv_hbm, x_hbm, own_hbm, state_ref, x_ref, raw, sums, sems):
    half = x_ref.shape[1] // 2
    pieces = [pl.ds(0, half), pl.ds(half, half)]
    pick = pltpu.make_async_copy(kv_hbm.at[:, index_ref[0]], raw, sems.at[2])
    hand_on = pltpu.make_async_copy(raw, own_hbm, sems.at[4])
    pick.start()
    loads = [
        pltpu.make_async_copy(x_hbm.at[pl.ds(1, 2), rows, :], x_ref.at[pl.ds(1, 2), rows, :], sems.at[i])
        for i, rows in enumerate(pieces)
    ]
    loads.append(pltpu.make_async_copy(x_hbm.at[0], x_ref.at[0], sems.at[3]))
    for load in loads:
        load.start()
    pick.wait()
    hand_on.start()
    loads[0].wait()
    for h in range(heads):
        sums[h] = tn_dot(x_ref[1, pieces[0], lanes(h)], x_ref[2, pieces[0], lanes(h)])
    loads[1].wait()
    for h in range(heads):
        total = sums[h] + tn_dot(x_ref[1, pieces[1], lanes(h)], x_ref[2, pieces[1], lanes(h)])
        state_ref[h] = total.astype(BF16)
    loads[2].wait()
    hand_on.wait()


def first_call(index, kv, planes):
    tok, _, two, hd = kv.shape
    width = planes.shape[2]
    heads = width // HD
    return pl.pallas_call(
        functools.partial(first_kernel, heads),
        in_specs=[SMEM, HBM, HBM],
        out_specs=[ANY, VMEM, VMEM],
        out_shape=[
            jax.ShapeDtypeStruct((tok, two, hd), BF16),
            pltpu.VMEM((heads, HD, HD), BF16),
            pltpu.VMEM(planes.shape, BF16),
        ],
        scratch_shapes=[
            pltpu.VMEM((tok, two, hd), BF16),
            pltpu.VMEM((heads, HD, HD), F32),
            pltpu.SemaphoreType.DMA((5,)),
        ],
        compiler_params=PARAMS,
        cost_estimate=pl.CostEstimate(
            flops=2 * tok * width * HD, bytes_accessed=4 * tok * width, transcendentals=0
        ),
    )(index, pltpu.with_memory_space_constraint(kv, pltpu.HBM), pltpu.with_memory_space_constraint(planes, pltpu.HBM))


def linear_kernel(
    heads, table_ref, x_ref, own_ref, mine_ref, near_ref, out_ref, pair_ref, k_own, v_own, states, stage,
    raw, sem,
):
    load = pltpu.make_async_copy(own_ref, raw, sem)
    load.start()
    tok = x_ref.shape[1]
    chunks = tok // CHUNK
    bits = CHUNK.bit_length() - 1
    rows = [pl.ds(c * CHUNK, CHUNK) for c in range(chunks)]
    row = lax.broadcasted_iota(jnp.int32, (CHUNK, CHUNK), 0)
    col = lax.broadcasted_iota(jnp.int32, (CHUNK, CHUNK), 1)
    differ = jnp.bitwise_xor(row, col)
    weights = []
    for h in range(heads):
        weight = jnp.full((CHUNK, CHUNK), table_ref[h, 0], F32)
        for level in range(1, bits + 1):
            weight = jnp.where(differ >= 2 ** (level - 1), table_ref[h, level], weight)
        weights.append(jnp.where(col <= row, weight, 0.0))
    pair_ref[...] = (mine_ref[...].astype(F32) + near_ref[...].astype(F32)).astype(BF16)
    groups = [{} for _ in range(heads)]
    for c in range(chunks):
        for h in range(heads):
            base = h * 2 * chunks
            q, k, v = (x_ref[part, rows[c], lanes(h)] for part in range(3))
            tile = (nt_dot(q, k) * weights[h]).astype(BF16)
            prefix, bit = None, 0
            while (1 << bit) <= c:
                if (c >> bit) & 1:
                    term = table_ref[h, bits + bit + 1] * states[base + groups[h][bit, (c >> bit) - 1]]
                    prefix = term if prefix is None else prefix + term
                bit += 1
            if prefix is None:
                total = jnp.dot(tile, v, preferred_element_type=F32)
            else:
                total = jnp.dot(
                    jnp.concatenate([tile, q], axis=1),
                    jnp.concatenate([v, prefix.astype(BF16)], axis=0),
                    preferred_element_type=F32,
                )
            out_ref[rows[c], lanes(h)] = total
            if c < chunks - 1:
                state, bit, index = tn_dot(k, v), 0, c
                slot = len(groups[h])
                groups[h][0, c] = slot
                states[base + slot] = state
                while index & 1:
                    state = states[base + groups[h][bit, index - 1]] + state
                    bit, index = bit + 1, index >> 1
                    slot = len(groups[h])
                    groups[h][bit, index] = slot
                    states[base + slot] = state
    load.wait()
    take_apart(raw[...], stage, k_own, v_own)


def linear_call(table, planes, own_kv, mine, near):
    _, tok, width = planes.shape
    heads = width // HD
    keys = pltpu.VMEM((tok, 2 * HD), BF16)
    return pl.pallas_call(
        functools.partial(linear_kernel, heads),
        in_specs=[SMEM, VMEM, ANY, VMEM, VMEM],
        out_specs=[VMEM] * 4,
        out_shape=[pltpu.VMEM((tok, width), F32), pltpu.VMEM(mine.shape, BF16), keys, keys],
        scratch_shapes=[
            pltpu.VMEM((heads * 2 * (tok // CHUNK), HD, HD), F32),
            pltpu.VMEM((2 * tok, HD), F32),
            pltpu.VMEM((2 * tok, HD), BF16),
            pltpu.SemaphoreType.DMA(()),
        ],
        compiler_params=PARAMS,
        cost_estimate=pl.CostEstimate(
            flops=8 * tok * width * CHUNK, bytes_accessed=10 * tok * width, transcendentals=0
        ),
    )(table, planes, own_kv, mine, near)


def own_kernel(heads, block, q_ref, k_own, v_own, sums_ref, top_ref):
    tok = q_ref.shape[0]
    row = lax.broadcasted_iota(jnp.int32, (block, block), 0)
    col = lax.broadcasted_iota(jnp.int32, (block, block), 1)
    mask = jnp.where(col <= row, 0.0, NEG).astype(F32)
    for start in range(0, tok, block):
        end = start + block
        for h in range(heads):
            q = q_ref[start:end, lanes(h)]
            scores = nt_dot(jnp.concatenate([q, q], axis=1), k_own[:end, :])
            edge = scores[:, start:] + mask
            scores = jnp.concatenate([scores[:, :start], edge], axis=1) if start else edge
            top = jnp.max(scores, axis=1, keepdims=True)
            sums_ref[h, start:end, :] = jnp.dot(
                jnp.exp2(scores - top).astype(BF16), v_own[:end, :], preferred_element_type=F32
            )
            top_ref[h, start:end, :] = jnp.broadcast_to(top, (block, HD))


def own_call(soft_q, k_own, v_own, block):
    tok, width = soft_q.shape
    heads = width // HD
    return pl.pallas_call(
        functools.partial(own_kernel, heads, block),
        in_specs=[VMEM] * 3,
        out_specs=[VMEM] * 2,
        out_shape=[pltpu.VMEM((heads, tok, 2 * HD), F32), pltpu.VMEM((heads, tok, HD), F32)],
        compiler_params=PARAMS,
        cost_estimate=pl.CostEstimate(
            flops=3 * tok * tok * width, bytes_accessed=6 * tok * width, transcendentals=tok * tok * heads // 2
        ),
    )(soft_q, k_own, v_own)


def last_kernel(
    heads, block, rounds, place_ref, table_ref, q_ref, lin_ref, x_ref, before_ref, sums_ref, top_ref, *refs
):
    state_refs = refs[:rounds]
    out_hbm, mixed, packed, cross, k_before, v_before, stage, raw, in_sem, out_sems = refs[rounds:]
    tok = q_ref.shape[0]
    load = pltpu.make_async_copy(before_ref, raw, in_sem)
    load.start()
    place = place_ref[0]
    first = place == 0
    stride = 2 * heads
    local_bits = tok.bit_length() - 1
    pairs = heads // 2 if heads % 2 == 0 else heads
    together = heads // pairs
    cross[...] = jnp.zeros_like(cross)
    for h in range(heads):
        total = jnp.zeros((HD, HD), F32)
        for bit, ref in enumerate(state_refs):
            earlier = jnp.bitwise_and(jnp.right_shift(place, bit), 1) == 1
            factor = jnp.where(earlier, table_ref[h, local_bits + bit + 1], 0.0)
            total = total + factor * ref[h].astype(F32)
        at = lanes(h % together)
        cross[h // together, at, at] = total.astype(BF16)

    def linear_rows(start):
        rows = slice(start, start + block)
        for pair in range(pairs):
            wide = slice(pair * together * HD, (pair + 1) * together * HD)
            both = jnp.dot(x_ref[0, rows, wide], cross[pair], preferred_element_type=F32) + lin_ref[rows, wide]
            for i in range(together):
                total = both[:, lanes(i)]
                norm = total * lax.rsqrt(jnp.mean(total * total, axis=1, keepdims=True) + 1e-06)
                at = start * stride + 2 * (pair * together + i)
                mixed[pl.ds(at, block, stride=stride), :] = norm

    for start in range(0, tok // 2, block):
        linear_rows(start)

    load.wait()
    take_apart(raw[...], stage, k_before, v_before)
    row = lax.broadcasted_iota(jnp.int32, (block, block), 0)
    col = lax.broadcasted_iota(jnp.int32, (block, block), 1)
    mask = jnp.where(col >= row, 0.0, NEG).astype(F32)

    def copy_out(start):
        rows = pl.ds(start * stride, block * stride)
        return pltpu.make_async_copy(packed.at[rows, :], out_hbm.at[rows, :], out_sems.at[start // block])

    def send(start):
        rows = pl.ds(start * stride, block * stride)
        packed[rows, :] = mixed[rows, :].astype(BF16)
        copy_out(start).start()

    def attend(start):
        if start >= tok // 2:
            linear_rows(start)
        for h in range(heads):
            q = q_ref[start : start + block, lanes(h)]
            scores = nt_dot(jnp.concatenate([q, q], axis=1), k_before[start:, :])
            edge = scores[:, :block] + mask
            scores = jnp.concatenate([edge, scores[:, block:]], axis=1) if start + block < tok else edge
            top = jnp.max(scores, axis=1, keepdims=True)
            top_own = top_ref[h, start : start + block, :]
            both = jnp.where(first, top_own, jnp.maximum(top, top_own))
            off = jnp.where(first, FAR, both)
            probs = jnp.exp2(scores - jnp.concatenate([off] * (scores.shape[1] // HD), axis=1)).astype(BF16)
            sums = jnp.dot(probs, v_before[start:, :], preferred_element_type=F32)
            factor = jnp.exp2(top_own - both)
            sums = sums + sums_ref[h, start : start + block, :] * jnp.concatenate([factor, factor], axis=1)
            mixed[pl.ds(start * stride + 2 * h + 1, block, stride=stride), :] = sums[:, :HD] / sums[:, HD:]

    for start in range(0, tok, block):

        if start:
            send(start - block)
        attend(start)

    send(tok - block)
    for start in range(0, tok, block):
        copy_out(start).wait()


def last_call(place, table, soft_q, partial, planes, before, sums, top, states, block):
    tok, width = soft_q.shape
    heads = width // HD
    return pl.pallas_call(
        functools.partial(last_kernel, heads, block, len(states)),
        in_specs=[SMEM, SMEM, VMEM, VMEM, VMEM, ANY, VMEM, VMEM] + [VMEM] * len(states),
        out_specs=ANY,
        out_shape=jax.ShapeDtypeStruct((tok * 2 * heads, HD), BF16),
        scratch_shapes=[
            pltpu.VMEM((tok * 2 * heads, HD), F32),
            pltpu.VMEM((tok * 2 * heads, HD), BF16),
            pltpu.VMEM((heads // 2, 2 * HD, 2 * HD) if heads % 2 == 0 else (heads, HD, HD), BF16),
            pltpu.VMEM((tok, 2 * HD), BF16),
            pltpu.VMEM((tok, 2 * HD), BF16),
            pltpu.VMEM((2 * tok, HD), F32),
            pltpu.VMEM((2 * tok, HD), BF16),
            pltpu.SemaphoreType.DMA(()),
            pltpu.SemaphoreType.DMA((tok // block,)),
        ],
        compiler_params=PARAMS,
        cost_estimate=pl.CostEstimate(
            flops=4 * tok * tok * width, bytes_accessed=14 * tok * width, transcendentals=tok * tok * heads // 2
        ),
    )(place, table, soft_q, partial, planes, before, sums, top, *states)


def local(lin_qkv, level_weights, soft_q, soft_kv):
    tok = lin_qkv.shape[0]
    q_heads = soft_q.shape[1] // HD
    group = HEADS_SM // KV_HEADS
    block = min(256, tok // 2)
    my_seq = lax.axis_index("seq")

    kv_index = lax.axis_index("head") * q_heads // group
    kv = soft_kv.reshape(tok, 2, KV_HEADS, HD).transpose(0, 2, 1, 3)
    planes = jnp.transpose(lin_qkv, (1, 0, 2))
    place = my_seq.reshape(1)
    table = jnp.transpose(level_weights)
    own_kv, state, planes = first_call(kv_index.reshape(1), kv, planes)
    own_kv = own_kv.reshape(2 * tok, HD)
    before = passed_along(own_kv, "seq", 1)
    near = partner_2(state, "seq", 0)
    partial, group_sum, *own = linear_call(table, planes, own_kv, state, near)
    states = [near]
    for bit in range(1, lax.axis_size("seq").bit_length() - 1):
        if bit > 1:
            group_sum = (group_sum.astype(F32) + states[-1].astype(F32)).astype(BF16)
        states.append(partner_2(group_sum, "seq", bit))
    sums, top = own_call(soft_q, *own, block)
    out = last_call(place, table, soft_q, partial, planes, before, sums, top, states, block)
    out = out.reshape(tok, q_heads, 2, HD).transpose(0, 2, 1, 3)
    return out.reshape(tok, 2, q_heads * HD)


def solution(mesh):
    in_specs = (
        P(("groups", "seq"), None, "head"),
        P(None, "head"),
        P(("groups", "seq"), "head"),
        P(("groups", "seq"), None, None),
    )
    out_specs = P(("groups", "seq"), None, "head")
    return jax.shard_map(local, mesh=mesh, in_specs=in_specs, out_specs=out_specs, check_vma=False)
```

```python
import functools

import jax
import jax.numpy as jnp
import numpy as np
from jax import lax
from jax.experimental import pallas as pl
from jax.experimental.pallas import tpu as pltpu
from jax.sharding import PartitionSpec as P


HD = 128
HEADS_SM = 16
KV_HEADS = 2
CHUNK = 256
NEG = -1e30
FAR = 1e30
F32 = jnp.float32
BF16 = jnp.bfloat16
SCALE = float(np.log2(np.e) / np.sqrt(HD))
ANY = pl.BlockSpec(memory_space=pl.ANY)
SMEM = pl.BlockSpec(memory_space=pltpu.SMEM)
VMEM = pl.BlockSpec(memory_space=pltpu.VMEM)
HBM = pl.BlockSpec(memory_space=pltpu.HBM)
PARAMS = pltpu.CompilerParams(vmem_limit_bytes=24 * 2**20)


def partner_2(value, axis, distance):
    mask = 2**distance
    pairs = [(source, source ^ mask) for source in range(lax.axis_size(axis))]
    return lax.ppermute(value, axis, pairs)


def passed_along(x, axis, by):
    size = lax.axis_size(axis)
    pairs = [(i, (i + by) % size) for i in range(size)]
    return lax.ppermute(x, axis, pairs)


def nt_dot(a, b):
    return lax.dot_general(a, b, (((1,), (1,)), ((), ())), preferred_element_type=F32)


def tn_dot(a, b):
    return lax.dot_general(a, b, (((0,), (0,)), ((), ())), preferred_element_type=F32)


def lanes(h):
    return slice(h * HD, (h + 1) * HD)


def take_apart(pairs, stage, k_out, v_out):
    count = k_out.shape[0]
    stage[...] = pairs.astype(F32)
    keys = stage[pl.ds(0, count, stride=2), :] * SCALE
    high = keys.astype(BF16)
    k_out[:, 0:HD] = high
    k_out[:, HD : 2 * HD] = (keys - high.astype(F32)).astype(BF16)
    v_out[:, 0:HD] = stage[pl.ds(1, count, stride=2), :].astype(BF16)
    v_out[:, HD : 2 * HD] = jnp.ones((count, HD), BF16)


def first_kernel(heads, index_ref, kv_hbm, x_hbm, own_hbm, state_ref, x_ref, raw, sums, sems):
    half = x_ref.shape[1] // 2
    pieces = [pl.ds(0, half), pl.ds(half, half)]
    pick = pltpu.make_async_copy(kv_hbm.at[:, index_ref[0]], raw, sems.at[2])
    hand_on = pltpu.make_async_copy(raw, own_hbm, sems.at[4])
    pick.start()
    loads = [
        pltpu.make_async_copy(x_hbm.at[pl.ds(1, 2), rows, :], x_ref.at[pl.ds(1, 2), rows, :], sems.at[i])
        for i, rows in enumerate(pieces)
    ]
    loads.append(pltpu.make_async_copy(x_hbm.at[0], x_ref.at[0], sems.at[3]))
    for load in loads:
        load.start()
    pick.wait()
    hand_on.start()
    loads[0].wait()
    for h in range(heads):
        sums[h] = tn_dot(x_ref[1, pieces[0], lanes(h)], x_ref[2, pieces[0], lanes(h)])
    loads[1].wait()
    for h in range(heads):
        total = sums[h] + tn_dot(x_ref[1, pieces[1], lanes(h)], x_ref[2, pieces[1], lanes(h)])
        state_ref[h] = total.astype(BF16)
    loads[2].wait()
    hand_on.wait()


def first_call(index, kv, planes):
    tok, _, two, hd = kv.shape
    width = planes.shape[2]
    heads = width // HD
    return pl.pallas_call(
        functools.partial(first_kernel, heads),
        in_specs=[SMEM, HBM, HBM],
        out_specs=[ANY, VMEM, VMEM],
        out_shape=[
            jax.ShapeDtypeStruct((tok, two, hd), BF16),
            pltpu.VMEM((heads, HD, HD), BF16),
            pltpu.VMEM(planes.shape, BF16),
        ],
        scratch_shapes=[
            pltpu.VMEM((tok, two, hd), BF16),
            pltpu.VMEM((heads, HD, HD), F32),
            pltpu.SemaphoreType.DMA((5,)),
        ],
        compiler_params=PARAMS,
        cost_estimate=pl.CostEstimate(
            flops=2 * tok * width * HD, bytes_accessed=4 * tok * width, transcendentals=0
        ),
    )(index, pltpu.with_memory_space_constraint(kv, pltpu.HBM), pltpu.with_memory_space_constraint(planes, pltpu.HBM))


def linear_kernel(
    heads, table_ref, x_ref, own_ref, mine_ref, near_ref, out_ref, pair_ref, k_own, v_own, states, stage,
    raw, sem,
):
    load = pltpu.make_async_copy(own_ref, raw, sem)
    load.start()
    tok = x_ref.shape[1]
    chunks = tok // CHUNK
    bits = CHUNK.bit_length() - 1
    rows = [pl.ds(c * CHUNK, CHUNK) for c in range(chunks)]
    row = lax.broadcasted_iota(jnp.int32, (CHUNK, CHUNK), 0)
    col = lax.broadcasted_iota(jnp.int32, (CHUNK, CHUNK), 1)
    differ = jnp.bitwise_xor(row, col)
    weights = []
    for h in range(heads):
        weight = jnp.full((CHUNK, CHUNK), table_ref[h, 0], F32)
        for level in range(1, bits + 1):
            weight = jnp.where(differ >= 2 ** (level - 1), table_ref[h, level], weight)
        weights.append(jnp.where(col <= row, weight, 0.0))
    pair_ref[...] = (mine_ref[...].astype(F32) + near_ref[...].astype(F32)).astype(BF16)
    groups = [{} for _ in range(heads)]
    for c in range(chunks):
        for h in range(heads):
            base = h * 2 * chunks
            q, k, v = (x_ref[part, rows[c], lanes(h)] for part in range(3))
            tile = (nt_dot(q, k) * weights[h]).astype(BF16)
            prefix, bit = None, 0
            while (1 << bit) <= c:
                if (c >> bit) & 1:
                    term = table_ref[h, bits + bit + 1] * states[base + groups[h][bit, (c >> bit) - 1]]
                    prefix = term if prefix is None else prefix + term
                bit += 1
            if prefix is None:
                total = jnp.dot(tile, v, preferred_element_type=F32)
            else:
                total = jnp.dot(
                    jnp.concatenate([tile, q], axis=1),
                    jnp.concatenate([v, prefix.astype(BF16)], axis=0),
                    preferred_element_type=F32,
                )
            out_ref[rows[c], lanes(h)] = total
            if c < chunks - 1:
                state, bit, index = tn_dot(k, v), 0, c
                slot = len(groups[h])
                groups[h][0, c] = slot
                states[base + slot] = state
                while index & 1:
                    state = states[base + groups[h][bit, index - 1]] + state
                    bit, index = bit + 1, index >> 1
                    slot = len(groups[h])
                    groups[h][bit, index] = slot
                    states[base + slot] = state
    load.wait()
    take_apart(raw[...], stage, k_own, v_own)


def linear_call(table, planes, own_kv, mine, near):
    _, tok, width = planes.shape
    heads = width // HD
    keys = pltpu.VMEM((tok, 2 * HD), BF16)
    return pl.pallas_call(
        functools.partial(linear_kernel, heads),
        in_specs=[SMEM, VMEM, ANY, VMEM, VMEM],
        out_specs=[VMEM] * 4,
        out_shape=[pltpu.VMEM((tok, width), F32), pltpu.VMEM(mine.shape, BF16), keys, keys],
        scratch_shapes=[
            pltpu.VMEM((heads * 2 * (tok // CHUNK), HD, HD), F32),
            pltpu.VMEM((2 * tok, HD), F32),
            pltpu.VMEM((2 * tok, HD), BF16),
            pltpu.SemaphoreType.DMA(()),
        ],
        compiler_params=PARAMS,
        cost_estimate=pl.CostEstimate(
            flops=8 * tok * width * CHUNK, bytes_accessed=10 * tok * width, transcendentals=0
        ),
    )(table, planes, own_kv, mine, near)


def own_kernel(heads, block, q_ref, k_own, v_own, sums_ref, top_ref):
    tok = q_ref.shape[0]
    row = lax.broadcasted_iota(jnp.int32, (block, block), 0)
    col = lax.broadcasted_iota(jnp.int32, (block, block), 1)
    mask = jnp.where(col <= row, 0.0, NEG).astype(F32)
    mask = jnp.concatenate([mask] * heads, axis=0)
    for start in reversed(range(0, tok, block)):
        end = start + block
        q = jnp.concatenate([q_ref[start:end, lanes(h)] for h in range(heads)], axis=0)
        scores = nt_dot(jnp.concatenate([q, q], axis=1), k_own[:end, :])
        edge = scores[:, start:] + mask
        scores = jnp.concatenate([scores[:, :start], edge], axis=1) if start else edge
        top = jnp.max(scores, axis=1, keepdims=True)
        sums = jnp.dot(jnp.exp2(scores - top).astype(BF16), v_own[:end, :], preferred_element_type=F32)
        top = jnp.broadcast_to(top, (heads * block, HD))
        for h in range(heads):
            rows = slice(h * block, (h + 1) * block)
            sums_ref[h, start:end, :] = sums[rows]
            top_ref[h, start:end, :] = top[rows]


def own_call(soft_q, k_own, v_own, block):
    tok, width = soft_q.shape
    heads = width // HD
    return pl.pallas_call(
        functools.partial(own_kernel, heads, block),
        in_specs=[VMEM] * 3,
        out_specs=[VMEM] * 2,
        out_shape=[pltpu.VMEM((heads, tok, 2 * HD), F32), pltpu.VMEM((heads, tok, HD), F32)],
        compiler_params=PARAMS,
        cost_estimate=pl.CostEstimate(
            flops=3 * tok * tok * width, bytes_accessed=6 * tok * width, transcendentals=tok * tok * heads // 2
        ),
    )(soft_q, k_own, v_own)


def last_kernel(
    heads, block, rounds, place_ref, table_ref, q_ref, lin_ref, x_ref, before_ref, sums_ref, top_ref, *refs
):
    state_refs = refs[:rounds]
    out_hbm, mixed, packed, cross, k_before, v_before, stage, raw, in_sem, out_sems = refs[rounds:]
    tok = q_ref.shape[0]
    load = pltpu.make_async_copy(before_ref, raw, in_sem)
    load.start()
    place = place_ref[0]
    first = place == 0
    stride = 2 * heads
    local_bits = tok.bit_length() - 1
    pairs = heads // 2 if heads % 2 == 0 else heads
    together = heads // pairs
    cross[...] = jnp.zeros_like(cross)
    for h in range(heads):
        total = jnp.zeros((HD, HD), F32)
        for bit, ref in enumerate(state_refs):
            earlier = jnp.bitwise_and(jnp.right_shift(place, bit), 1) == 1
            factor = jnp.where(earlier, table_ref[h, local_bits + bit + 1], 0.0)
            total = total + factor * ref[h].astype(F32)
        at = lanes(h % together)
        cross[h // together, at, at] = total.astype(BF16)

    def linear_rows(start):
        rows = slice(start, start + block)
        for pair in range(pairs):
            wide = slice(pair * together * HD, (pair + 1) * together * HD)
            both = jnp.dot(x_ref[0, rows, wide], cross[pair], preferred_element_type=F32) + lin_ref[rows, wide]
            for i in range(together):
                total = both[:, lanes(i)]
                norm = total * lax.rsqrt(jnp.mean(total * total, axis=1, keepdims=True) + 1e-06)
                at = start * stride + 2 * (pair * together + i)
                mixed[pl.ds(at, block, stride=stride), :] = norm

    for start in range(0, tok // 2, block):
        linear_rows(start)

    load.wait()
    take_apart(raw[...], stage, k_before, v_before)
    row = lax.broadcasted_iota(jnp.int32, (block, block), 0)
    col = lax.broadcasted_iota(jnp.int32, (block, block), 1)
    mask = jnp.where(col >= row, 0.0, NEG).astype(F32)

    def copy_out(start):
        rows = pl.ds(start * stride, block * stride)
        return pltpu.make_async_copy(packed.at[rows, :], out_hbm.at[rows, :], out_sems.at[start // block])

    def send(start):
        rows = pl.ds(start * stride, block * stride)
        packed[rows, :] = mixed[rows, :].astype(BF16)
        copy_out(start).start()

    def attend(start):
        if start >= tok // 2:
            linear_rows(start)
        for h in range(heads):
            q = q_ref[start : start + block, lanes(h)]
            scores = nt_dot(jnp.concatenate([q, q], axis=1), k_before[start:, :])
            edge = scores[:, :block] + mask
            scores = jnp.concatenate([edge, scores[:, block:]], axis=1) if start + block < tok else edge
            top = jnp.max(scores, axis=1, keepdims=True)
            top_own = top_ref[h, start : start + block, :]
            both = jnp.where(first, top_own, jnp.maximum(top, top_own))
            off = jnp.where(first, FAR, both)
            probs = jnp.exp2(scores - jnp.concatenate([off] * (scores.shape[1] // HD), axis=1)).astype(BF16)
            sums = jnp.dot(probs, v_before[start:, :], preferred_element_type=F32)
            factor = jnp.exp2(top_own - both)
            sums = sums + sums_ref[h, start : start + block, :] * jnp.concatenate([factor, factor], axis=1)
            mixed[pl.ds(start * stride + 2 * h + 1, block, stride=stride), :] = sums[:, :HD] / sums[:, HD:]

    for start in range(0, tok, block):

        if start:
            send(start - block)
        attend(start)

    send(tok - block)
    for start in range(0, tok, block):
        copy_out(start).wait()


def last_call(place, table, soft_q, partial, planes, before, sums, top, states, block):
    tok, width = soft_q.shape
    heads = width // HD
    return pl.pallas_call(
        functools.partial(last_kernel, heads, block, len(states)),
        in_specs=[SMEM, SMEM, VMEM, VMEM, VMEM, ANY, VMEM, VMEM] + [VMEM] * len(states),
        out_specs=ANY,
        out_shape=jax.ShapeDtypeStruct((tok * 2 * heads, HD), BF16),
        scratch_shapes=[
            pltpu.VMEM((tok * 2 * heads, HD), F32),
            pltpu.VMEM((tok * 2 * heads, HD), BF16),
            pltpu.VMEM((heads // 2, 2 * HD, 2 * HD) if heads % 2 == 0 else (heads, HD, HD), BF16),
            pltpu.VMEM((tok, 2 * HD), BF16),
            pltpu.VMEM((tok, 2 * HD), BF16),
            pltpu.VMEM((2 * tok, HD), F32),
            pltpu.VMEM((2 * tok, HD), BF16),
            pltpu.SemaphoreType.DMA(()),
            pltpu.SemaphoreType.DMA((tok // block,)),
        ],
        compiler_params=PARAMS,
        cost_estimate=pl.CostEstimate(
            flops=4 * tok * tok * width, bytes_accessed=14 * tok * width, transcendentals=tok * tok * heads // 2
        ),
    )(place, table, soft_q, partial, planes, before, sums, top, *states)


def local(lin_qkv, level_weights, soft_q, soft_kv):
    tok = lin_qkv.shape[0]
    q_heads = soft_q.shape[1] // HD
    group = HEADS_SM // KV_HEADS
    block = min(256, tok // 2)
    my_seq = lax.axis_index("seq")

    kv_index = lax.axis_index("head") * q_heads // group
    kv = soft_kv.reshape(tok, 2, KV_HEADS, HD).transpose(0, 2, 1, 3)
    planes = jnp.transpose(lin_qkv, (1, 0, 2))
    place = my_seq.reshape(1)
    table = jnp.transpose(level_weights)
    own_kv, state, planes = first_call(kv_index.reshape(1), kv, planes)
    own_kv = own_kv.reshape(2 * tok, HD)
    before = passed_along(own_kv, "seq", 1)
    near = partner_2(state, "seq", 0)
    partial, group_sum, *own = linear_call(table, planes, own_kv, state, near)
    states = [near]
    for bit in range(1, lax.axis_size("seq").bit_length() - 1):
        if bit > 1:
            group_sum = (group_sum.astype(F32) + states[-1].astype(F32)).astype(BF16)
        states.append(partner_2(group_sum, "seq", bit))
    sums, top = own_call(soft_q, *own, block)
    out = last_call(place, table, soft_q, partial, planes, before, sums, top, states, block)
    out = out.reshape(tok, q_heads, 2, HD).transpose(0, 2, 1, 3)
    return out.reshape(tok, 2, q_heads * HD)


def solution(mesh):
    in_specs = (
        P(("groups", "seq"), None, "head"),
        P(None, "head"),
        P(("groups", "seq"), "head"),
        P(("groups", "seq"), None, None),
    )
    out_specs = P(("groups", "seq"), None, "head")
    return jax.shard_map(local, mesh=mesh, in_specs=in_specs, out_specs=out_specs, check_vma=False)
```

```python
import functools

import jax
import jax.numpy as jnp
import numpy as np
from jax import lax
from jax.experimental import pallas as pl
from jax.experimental.pallas import tpu as pltpu
from jax.sharding import PartitionSpec as P


HD = 128
HEADS_SM = 16
KV_HEADS = 2
CHUNK = 256
NEG = -1e30
FAR = 1e30
F32 = jnp.float32
BF16 = jnp.bfloat16
SCALE = float(np.log2(np.e) / np.sqrt(HD))
ANY = pl.BlockSpec(memory_space=pl.ANY)
SMEM = pl.BlockSpec(memory_space=pltpu.SMEM)
VMEM = pl.BlockSpec(memory_space=pltpu.VMEM)
HBM = pl.BlockSpec(memory_space=pltpu.HBM)
PARAMS = pltpu.CompilerParams(vmem_limit_bytes=24 * 2**20)


def partner_2(value, axis, distance):
    mask = 2**distance
    pairs = [(source, source ^ mask) for source in range(lax.axis_size(axis))]
    return lax.ppermute(value, axis, pairs)


def passed_along(x, axis, by):
    size = lax.axis_size(axis)
    pairs = [(i, (i + by) % size) for i in range(size)]
    return lax.ppermute(x, axis, pairs)


def nt_dot(a, b):
    return lax.dot_general(a, b, (((1,), (1,)), ((), ())), preferred_element_type=F32)


def tn_dot(a, b):
    return lax.dot_general(a, b, (((0,), (0,)), ((), ())), preferred_element_type=F32)


def lanes(h):
    return slice(h * HD, (h + 1) * HD)


def take_apart(pairs, stage, k_out, v_out):
    count = k_out.shape[0]
    stage[...] = pairs.astype(F32)
    keys = stage[pl.ds(0, count, stride=2), :] * SCALE
    high = keys.astype(BF16)
    k_out[:, 0:HD] = high
    k_out[:, HD : 2 * HD] = (keys - high.astype(F32)).astype(BF16)
    v_out[:, 0:HD] = stage[pl.ds(1, count, stride=2), :].astype(BF16)
    v_out[:, HD : 2 * HD] = jnp.ones((count, HD), BF16)


def first_kernel(heads, index_ref, kv_hbm, x_hbm, own_hbm, state_ref, x_ref, raw, sums, sems):
    half = x_ref.shape[1] // 2
    pieces = [pl.ds(0, half), pl.ds(half, half)]
    pick = pltpu.make_async_copy(kv_hbm.at[:, index_ref[0]], raw, sems.at[2])
    hand_on = pltpu.make_async_copy(raw, own_hbm, sems.at[4])
    pick.start()
    loads = [
        pltpu.make_async_copy(x_hbm.at[pl.ds(1, 2), rows, :], x_ref.at[pl.ds(1, 2), rows, :], sems.at[i])
        for i, rows in enumerate(pieces)
    ]
    loads.append(pltpu.make_async_copy(x_hbm.at[0], x_ref.at[0], sems.at[3]))
    for load in loads:
        load.start()
    pick.wait()
    hand_on.start()
    loads[0].wait()
    for h in range(heads):
        sums[h] = tn_dot(x_ref[1, pieces[0], lanes(h)], x_ref[2, pieces[0], lanes(h)])
    loads[1].wait()
    for h in range(heads):
        total = sums[h] + tn_dot(x_ref[1, pieces[1], lanes(h)], x_ref[2, pieces[1], lanes(h)])
        state_ref[h] = total.astype(BF16)
    loads[2].wait()
    hand_on.wait()


def first_call(index, kv, planes):
    tok, _, two, hd = kv.shape
    width = planes.shape[2]
    heads = width // HD
    return pl.pallas_call(
        functools.partial(first_kernel, heads),
        in_specs=[SMEM, HBM, HBM],
        out_specs=[ANY, VMEM, VMEM],
        out_shape=[
            jax.ShapeDtypeStruct((tok, two, hd), BF16),
            pltpu.VMEM((heads, HD, HD), BF16),
            pltpu.VMEM(planes.shape, BF16),
        ],
        scratch_shapes=[
            pltpu.VMEM((tok, two, hd), BF16),
            pltpu.VMEM((heads, HD, HD), F32),
            pltpu.SemaphoreType.DMA((5,)),
        ],
        compiler_params=PARAMS,
        cost_estimate=pl.CostEstimate(
            flops=2 * tok * width * HD, bytes_accessed=4 * tok * width, transcendentals=0
        ),
    )(index, pltpu.with_memory_space_constraint(kv, pltpu.HBM), pltpu.with_memory_space_constraint(planes, pltpu.HBM))


def linear_kernel(
    heads, table_ref, x_ref, own_ref, mine_ref, near_ref, out_ref, pair_ref, k_own, v_own, states, stage,
    raw, sem,
):
    load = pltpu.make_async_copy(own_ref, raw, sem)
    load.start()
    tok = x_ref.shape[1]
    chunks = tok // CHUNK
    bits = CHUNK.bit_length() - 1
    rows = [pl.ds(c * CHUNK, CHUNK) for c in range(chunks)]
    row = lax.broadcasted_iota(jnp.int32, (CHUNK, CHUNK), 0)
    col = lax.broadcasted_iota(jnp.int32, (CHUNK, CHUNK), 1)
    differ = jnp.bitwise_xor(row, col)
    weights = []
    for h in range(heads):
        weight = jnp.full((CHUNK, CHUNK), table_ref[h, 0], F32)
        for level in range(1, bits + 1):
            weight = jnp.where(differ >= 2 ** (level - 1), table_ref[h, level], weight)
        weights.append(jnp.where(col <= row, weight, 0.0))
    pair_ref[...] = (mine_ref[...].astype(F32) + near_ref[...].astype(F32)).astype(BF16)
    groups = [{} for _ in range(heads)]
    for c in range(chunks):
        for h in range(heads):
            base = h * 2 * chunks
            q, k, v = (x_ref[part, rows[c], lanes(h)] for part in range(3))
            tile = (nt_dot(q, k) * weights[h]).astype(BF16)
            prefix, bit = None, 0
            while (1 << bit) <= c:
                if (c >> bit) & 1:
                    term = table_ref[h, bits + bit + 1] * states[base + groups[h][bit, (c >> bit) - 1]]
                    prefix = term if prefix is None else prefix + term
                bit += 1
            if prefix is None:
                total = jnp.dot(tile, v, preferred_element_type=F32)
            else:
                total = jnp.dot(
                    jnp.concatenate([tile, q], axis=1),
                    jnp.concatenate([v, prefix.astype(BF16)], axis=0),
                    preferred_element_type=F32,
                )
            out_ref[rows[c], lanes(h)] = total
            if c < chunks - 1:
                state, bit, index = tn_dot(k, v), 0, c
                slot = len(groups[h])
                groups[h][0, c] = slot
                states[base + slot] = state
                while index & 1:
                    state = states[base + groups[h][bit, index - 1]] + state
                    bit, index = bit + 1, index >> 1
                    slot = len(groups[h])
                    groups[h][bit, index] = slot
                    states[base + slot] = state
    load.wait()
    take_apart(raw[...], stage, k_own, v_own)


def linear_call(table, planes, own_kv, mine, near):
    _, tok, width = planes.shape
    heads = width // HD
    keys = pltpu.VMEM((tok, 2 * HD), BF16)
    return pl.pallas_call(
        functools.partial(linear_kernel, heads),
        in_specs=[SMEM, VMEM, ANY, VMEM, VMEM],
        out_specs=[VMEM] * 4,
        out_shape=[pltpu.VMEM((tok, width), F32), pltpu.VMEM(mine.shape, BF16), keys, keys],
        scratch_shapes=[
            pltpu.VMEM((heads * 2 * (tok // CHUNK), HD, HD), F32),
            pltpu.VMEM((2 * tok, HD), F32),
            pltpu.VMEM((2 * tok, HD), BF16),
            pltpu.SemaphoreType.DMA(()),
        ],
        compiler_params=PARAMS,
        cost_estimate=pl.CostEstimate(
            flops=8 * tok * width * CHUNK, bytes_accessed=10 * tok * width, transcendentals=0
        ),
    )(table, planes, own_kv, mine, near)


def own_kernel(heads, block, q_ref, k_own, v_own, sums_ref, top_ref):
    tok = q_ref.shape[0]
    row = lax.broadcasted_iota(jnp.int32, (block, block), 0)
    col = lax.broadcasted_iota(jnp.int32, (block, block), 1)
    mask = jnp.where(col <= row, 0.0, NEG).astype(F32)
    mask = jnp.concatenate([mask] * heads, axis=0)
    for start in reversed(range(0, tok, block)):
        end = start + block
        q = jnp.concatenate([q_ref[start:end, lanes(h)] for h in range(heads)], axis=0)
        scores = nt_dot(jnp.concatenate([q, q], axis=1), k_own[:end, :])
        edge = scores[:, start:] + mask
        scores = jnp.concatenate([scores[:, :start], edge], axis=1) if start else edge
        top = jnp.max(scores, axis=1, keepdims=True)
        sums = jnp.dot(jnp.exp2(scores - top).astype(BF16), v_own[:end, :], preferred_element_type=F32)
        top = jnp.broadcast_to(top, (heads * block, HD))
        for h in range(heads):
            rows = slice(h * block, (h + 1) * block)
            sums_ref[h, start:end, :] = sums[rows]
            top_ref[h, start:end, :] = top[rows]


def own_call(soft_q, k_own, v_own, block):
    tok, width = soft_q.shape
    heads = width // HD
    return pl.pallas_call(
        functools.partial(own_kernel, heads, block),
        in_specs=[VMEM] * 3,
        out_specs=[VMEM] * 2,
        out_shape=[pltpu.VMEM((heads, tok, 2 * HD), F32), pltpu.VMEM((heads, tok, HD), F32)],
        compiler_params=PARAMS,
        cost_estimate=pl.CostEstimate(
            flops=3 * tok * tok * width, bytes_accessed=6 * tok * width, transcendentals=tok * tok * heads // 2
        ),
    )(soft_q, k_own, v_own)


def unpack_kernel(before_ref, k_out, v_out, stage, raw, sem):
    load = pltpu.make_async_copy(before_ref, raw, sem)
    load.start()
    load.wait()
    take_apart(raw[...], stage, k_out, v_out)


def unpack_call(before):
    rows = before.shape[0]
    keys = pltpu.VMEM((rows // 2, 2 * HD), BF16)
    return pl.pallas_call(
        unpack_kernel,
        in_specs=[ANY],
        out_specs=[VMEM] * 2,
        out_shape=[keys, keys],
        scratch_shapes=[
            pltpu.VMEM((rows, HD), F32),
            pltpu.VMEM((rows, HD), BF16),
            pltpu.SemaphoreType.DMA(()),
        ],
        compiler_params=PARAMS,
        cost_estimate=pl.CostEstimate(flops=0, bytes_accessed=8 * rows * HD, transcendentals=0),
    )(before)


def last_kernel(
    heads, block, rounds, place_ref, table_ref, q_ref, lin_ref, x_ref, k_before, v_before, sums_ref, top_ref, *refs
):
    state_refs = refs[:rounds]
    out_hbm, mixed, packed, cross, out_sems = refs[rounds:]
    tok = q_ref.shape[0]
    place = place_ref[0]
    first = place == 0
    stride = 2 * heads
    local_bits = tok.bit_length() - 1
    pairs = heads // 2 if heads % 2 == 0 else heads
    together = heads // pairs
    cross[...] = jnp.zeros_like(cross)
    for h in range(heads):
        total = jnp.zeros((HD, HD), F32)
        for bit, ref in enumerate(state_refs):
            earlier = jnp.bitwise_and(jnp.right_shift(place, bit), 1) == 1
            factor = jnp.where(earlier, table_ref[h, local_bits + bit + 1], 0.0)
            total = total + factor * ref[h].astype(F32)
        at = lanes(h % together)
        cross[h // together, at, at] = total.astype(BF16)

    def linear_rows(start):
        rows = slice(start, start + block)
        for pair in range(pairs):
            wide = slice(pair * together * HD, (pair + 1) * together * HD)
            both = jnp.dot(x_ref[0, rows, wide], cross[pair], preferred_element_type=F32) + lin_ref[rows, wide]
            for i in range(together):
                total = both[:, lanes(i)]
                norm = total * lax.rsqrt(jnp.mean(total * total, axis=1, keepdims=True) + 1e-06)
                at = start * stride + 2 * (pair * together + i)
                mixed[pl.ds(at, block, stride=stride), :] = norm

    row = lax.broadcasted_iota(jnp.int32, (block, block), 0)
    col = lax.broadcasted_iota(jnp.int32, (block, block), 1)
    mask = jnp.where(col >= row, 0.0, NEG).astype(F32)

    def copy_out(start):
        rows = pl.ds(start * stride, block * stride)
        return pltpu.make_async_copy(packed.at[rows, :], out_hbm.at[rows, :], out_sems.at[start // block])

    def send(start):
        rows = pl.ds(start * stride, block * stride)
        packed[rows, :] = mixed[rows, :].astype(BF16)
        copy_out(start).start()

    def attend(start):
        linear_rows(start)
        for h in range(heads):
            q = q_ref[start : start + block, lanes(h)]
            scores = nt_dot(jnp.concatenate([q, q], axis=1), k_before[start:, :])
            edge = scores[:, :block] + mask
            scores = jnp.concatenate([edge, scores[:, block:]], axis=1) if start + block < tok else edge
            top = jnp.max(scores, axis=1, keepdims=True)
            top_own = top_ref[h, start : start + block, :]
            both = jnp.where(first, top_own, jnp.maximum(top, top_own))
            off = jnp.where(first, FAR, both)
            probs = jnp.exp2(scores - jnp.concatenate([off] * (scores.shape[1] // HD), axis=1)).astype(BF16)
            sums = jnp.dot(probs, v_before[start:, :], preferred_element_type=F32)
            factor = jnp.exp2(top_own - both)
            sums = sums + sums_ref[h, start : start + block, :] * jnp.concatenate([factor, factor], axis=1)
            mixed[pl.ds(start * stride + 2 * h + 1, block, stride=stride), :] = sums[:, :HD] / sums[:, HD:]

    for start in range(0, tok, block):

        if start:
            send(start - block)
        attend(start)

    send(tok - block)
    for start in range(0, tok, block):
        copy_out(start).wait()


def last_call(place, table, soft_q, partial, planes, earlier, sums, top, states, block):
    tok, width = soft_q.shape
    heads = width // HD
    return pl.pallas_call(
        functools.partial(last_kernel, heads, block, len(states)),
        in_specs=[SMEM, SMEM] + [VMEM] * (7 + len(states)),
        out_specs=ANY,
        out_shape=jax.ShapeDtypeStruct((tok * 2 * heads, HD), BF16),
        scratch_shapes=[
            pltpu.VMEM((tok * 2 * heads, HD), F32),
            pltpu.VMEM((tok * 2 * heads, HD), BF16),
            pltpu.VMEM((heads // 2, 2 * HD, 2 * HD) if heads % 2 == 0 else (heads, HD, HD), BF16),
            pltpu.SemaphoreType.DMA((tok // block,)),
        ],
        compiler_params=PARAMS,
        cost_estimate=pl.CostEstimate(
            flops=4 * tok * tok * width, bytes_accessed=14 * tok * width, transcendentals=tok * tok * heads // 2
        ),
    )(place, table, soft_q, partial, planes, *earlier, sums, top, *states)


def local(lin_qkv, level_weights, soft_q, soft_kv):
    tok = lin_qkv.shape[0]
    q_heads = soft_q.shape[1] // HD
    group = HEADS_SM // KV_HEADS
    block = min(256, tok // 2)
    my_seq = lax.axis_index("seq")

    kv_index = lax.axis_index("head") * q_heads // group
    kv = soft_kv.reshape(tok, 2, KV_HEADS, HD).transpose(0, 2, 1, 3)
    planes = jnp.transpose(lin_qkv, (1, 0, 2))
    place = my_seq.reshape(1)
    table = jnp.transpose(level_weights)
    own_kv, state, planes = first_call(kv_index.reshape(1), kv, planes)
    own_kv = own_kv.reshape(2 * tok, HD)
    before = passed_along(own_kv, "seq", 1)
    near = partner_2(state, "seq", 0)
    partial, group_sum, *own = linear_call(table, planes, own_kv, state, near)
    states = [near]
    for bit in range(1, lax.axis_size("seq").bit_length() - 1):
        if bit > 1:
            group_sum = (group_sum.astype(F32) + states[-1].astype(F32)).astype(BF16)
        states.append(partner_2(group_sum, "seq", bit))
    sums, top = own_call(soft_q, *own, block)
    earlier = unpack_call(before)
    out = last_call(place, table, soft_q, partial, planes, earlier, sums, top, states, block)
    out = out.reshape(tok, q_heads, 2, HD).transpose(0, 2, 1, 3)
    return out.reshape(tok, 2, q_heads * HD)


def solution(mesh):
    in_specs = (
        P(("groups", "seq"), None, "head"),
        P(None, "head"),
        P(("groups", "seq"), "head"),
        P(("groups", "seq"), None, None),
    )
    out_specs = P(("groups", "seq"), None, "head")
    return jax.shard_map(local, mesh=mesh, in_specs=in_specs, out_specs=out_specs, check_vma=False)
```

```python
import functools

import jax
import jax.numpy as jnp
import numpy as np
from jax import lax
from jax.experimental import pallas as pl
from jax.experimental.pallas import tpu as pltpu
from jax.sharding import PartitionSpec as P


HD = 128
HEADS_SM = 16
KV_HEADS = 2
CHUNK = 256
NEG = -1e30
FAR = 1e30
F32 = jnp.float32
BF16 = jnp.bfloat16
SCALE = float(np.log2(np.e) / np.sqrt(HD))
ANY = pl.BlockSpec(memory_space=pl.ANY)
SMEM = pl.BlockSpec(memory_space=pltpu.SMEM)
VMEM = pl.BlockSpec(memory_space=pltpu.VMEM)
HBM = pl.BlockSpec(memory_space=pltpu.HBM)
PARAMS = pltpu.CompilerParams(vmem_limit_bytes=24 * 2**20)


def partner_2(value, axis, distance):
    mask = 2**distance
    pairs = [(source, source ^ mask) for source in range(lax.axis_size(axis))]
    return lax.ppermute(value, axis, pairs)


def passed_along(x, axis, by):
    size = lax.axis_size(axis)
    pairs = [(i, (i + by) % size) for i in range(size)]
    return lax.ppermute(x, axis, pairs)


def nt_dot(a, b):
    return lax.dot_general(a, b, (((1,), (1,)), ((), ())), preferred_element_type=F32)


def tn_dot(a, b):
    return lax.dot_general(a, b, (((0,), (0,)), ((), ())), preferred_element_type=F32)


def lanes(h):
    return slice(h * HD, (h + 1) * HD)


def take_apart(pairs, stage, k_out, v_out):
    count = k_out.shape[0]
    stage[...] = pairs.astype(F32)
    keys = stage[pl.ds(0, count, stride=2), :] * SCALE
    high = keys.astype(BF16)
    k_out[:, 0:HD] = high
    k_out[:, HD : 2 * HD] = (keys - high.astype(F32)).astype(BF16)
    v_out[:, 0:HD] = stage[pl.ds(1, count, stride=2), :].astype(BF16)
    v_out[:, HD : 2 * HD] = jnp.ones((count, HD), BF16)


def first_kernel(heads, index_ref, kv_hbm, x_hbm, own_hbm, state_ref, x_ref, raw, sums, sems):
    count = 4
    step = x_ref.shape[1] // count
    pieces = [pl.ds(i * step, step) for i in range(count)]
    pick = pltpu.make_async_copy(kv_hbm.at[:, index_ref[0]], raw, sems.at[count])
    hand_on = pltpu.make_async_copy(raw, own_hbm, sems.at[count + 1])
    pick.start()
    loads = [
        pltpu.make_async_copy(x_hbm.at[pl.ds(1, 2), rows, :], x_ref.at[pl.ds(1, 2), rows, :], sems.at[i])
        for i, rows in enumerate(pieces)
    ]
    loads.append(pltpu.make_async_copy(x_hbm.at[0], x_ref.at[0], sems.at[count + 2]))
    for load in loads:
        load.start()
    pick.wait()
    hand_on.start()
    for i, rows in enumerate(pieces):
        loads[i].wait()
        for h in range(heads):
            total = tn_dot(x_ref[1, rows, lanes(h)], x_ref[2, rows, lanes(h)])
            total = total if i == 0 else sums[h] + total
            if i < count - 1:
                sums[h] = total
            else:
                state_ref[h] = total.astype(BF16)
    loads[count].wait()
    hand_on.wait()


def first_call(index, kv, planes):
    tok, _, two, hd = kv.shape
    width = planes.shape[2]
    heads = width // HD
    return pl.pallas_call(
        functools.partial(first_kernel, heads),
        in_specs=[SMEM, HBM, HBM],
        out_specs=[ANY, VMEM, VMEM],
        out_shape=[
            jax.ShapeDtypeStruct((tok, two, hd), BF16),
            pltpu.VMEM((heads, HD, HD), BF16),
            pltpu.VMEM(planes.shape, BF16),
        ],
        scratch_shapes=[
            pltpu.VMEM((tok, two, hd), BF16),
            pltpu.VMEM((heads, HD, HD), F32),
            pltpu.SemaphoreType.DMA((7,)),
        ],
        compiler_params=PARAMS,
        cost_estimate=pl.CostEstimate(
            flops=2 * tok * width * HD, bytes_accessed=4 * tok * width, transcendentals=0
        ),
    )(index, pltpu.with_memory_space_constraint(kv, pltpu.HBM), pltpu.with_memory_space_constraint(planes, pltpu.HBM))


def linear_kernel(
    heads, table_ref, x_ref, own_ref, mine_ref, near_ref, out_ref, pair_ref, k_own, v_own, states, stage,
    raw, sem,
):
    load = pltpu.make_async_copy(own_ref, raw, sem)
    load.start()
    tok = x_ref.shape[1]
    chunks = tok // CHUNK
    bits = CHUNK.bit_length() - 1
    rows = [pl.ds(c * CHUNK, CHUNK) for c in range(chunks)]
    row = lax.broadcasted_iota(jnp.int32, (CHUNK, CHUNK), 0)
    col = lax.broadcasted_iota(jnp.int32, (CHUNK, CHUNK), 1)
    differ = jnp.bitwise_xor(row, col)
    weights = []
    for h in range(heads):
        weight = jnp.full((CHUNK, CHUNK), table_ref[h, 0], F32)
        for level in range(1, bits + 1):
            weight = jnp.where(differ >= 2 ** (level - 1), table_ref[h, level], weight)
        weights.append(jnp.where(col <= row, weight, 0.0))
    pair_ref[...] = (mine_ref[...].astype(F32) + near_ref[...].astype(F32)).astype(BF16)
    groups = [{} for _ in range(heads)]
    for c in range(chunks):
        for h in range(heads):
            base = h * 2 * chunks
            q, k, v = (x_ref[part, rows[c], lanes(h)] for part in range(3))
            tile = (nt_dot(q, k) * weights[h]).astype(BF16)
            prefix, bit = None, 0
            while (1 << bit) <= c:
                if (c >> bit) & 1:
                    term = table_ref[h, bits + bit + 1] * states[base + groups[h][bit, (c >> bit) - 1]]
                    prefix = term if prefix is None else prefix + term
                bit += 1
            if prefix is None:
                total = jnp.dot(tile, v, preferred_element_type=F32)
            else:
                total = jnp.dot(
                    jnp.concatenate([tile, q], axis=1),
                    jnp.concatenate([v, prefix.astype(BF16)], axis=0),
                    preferred_element_type=F32,
                )
            out_ref[rows[c], lanes(h)] = total
            if c < chunks - 1:
                state, bit, index = tn_dot(k, v), 0, c
                slot = len(groups[h])
                groups[h][0, c] = slot
                states[base + slot] = state
                while index & 1:
                    state = states[base + groups[h][bit, index - 1]] + state
                    bit, index = bit + 1, index >> 1
                    slot = len(groups[h])
                    groups[h][bit, index] = slot
                    states[base + slot] = state
    load.wait()
    take_apart(raw[...], stage, k_own, v_own)


def linear_call(table, planes, own_kv, mine, near):
    _, tok, width = planes.shape
    heads = width // HD
    keys = pltpu.VMEM((tok, 2 * HD), BF16)
    return pl.pallas_call(
        functools.partial(linear_kernel, heads),
        in_specs=[SMEM, VMEM, ANY, VMEM, VMEM],
        out_specs=[VMEM] * 4,
        out_shape=[pltpu.VMEM((tok, width), F32), pltpu.VMEM(mine.shape, BF16), keys, keys],
        scratch_shapes=[
            pltpu.VMEM((heads * 2 * (tok // CHUNK), HD, HD), F32),
            pltpu.VMEM((2 * tok, HD), F32),
            pltpu.VMEM((2 * tok, HD), BF16),
            pltpu.SemaphoreType.DMA(()),
        ],
        compiler_params=PARAMS,
        cost_estimate=pl.CostEstimate(
            flops=8 * tok * width * CHUNK, bytes_accessed=10 * tok * width, transcendentals=0
        ),
    )(table, planes, own_kv, mine, near)


def own_kernel(heads, block, q_ref, k_own, v_own, sums_ref, top_ref):
    tok = q_ref.shape[0]
    row = lax.broadcasted_iota(jnp.int32, (block, block), 0)
    col = lax.broadcasted_iota(jnp.int32, (block, block), 1)
    mask = jnp.where(col <= row, 0.0, NEG).astype(F32)
    mask = jnp.concatenate([mask] * heads, axis=0)
    for start in reversed(range(0, tok, block)):
        end = start + block
        q = jnp.concatenate([q_ref[start:end, lanes(h)] for h in range(heads)], axis=0)
        scores = nt_dot(jnp.concatenate([q, q], axis=1), k_own[:end, :])
        edge = scores[:, start:] + mask
        scores = jnp.concatenate([scores[:, :start], edge], axis=1) if start else edge
        top = jnp.max(scores, axis=1, keepdims=True)
        sums = jnp.dot(jnp.exp2(scores - top).astype(BF16), v_own[:end, :], preferred_element_type=F32)
        top = jnp.broadcast_to(top, (heads * block, HD))
        for h in range(heads):
            rows = slice(h * block, (h + 1) * block)
            sums_ref[h, start:end, :] = sums[rows]
            top_ref[h, start:end, :] = top[rows]


def own_call(soft_q, k_own, v_own, block):
    tok, width = soft_q.shape
    heads = width // HD
    return pl.pallas_call(
        functools.partial(own_kernel, heads, block),
        in_specs=[VMEM] * 3,
        out_specs=[VMEM] * 2,
        out_shape=[pltpu.VMEM((heads, tok, 2 * HD), F32), pltpu.VMEM((heads, tok, HD), F32)],
        compiler_params=PARAMS,
        cost_estimate=pl.CostEstimate(
            flops=3 * tok * tok * width, bytes_accessed=6 * tok * width, transcendentals=tok * tok * heads // 2
        ),
    )(soft_q, k_own, v_own)


def unpack_kernel(before_ref, k_out, v_out, stage, raw, sem):
    load = pltpu.make_async_copy(before_ref, raw, sem)
    load.start()
    load.wait()
    take_apart(raw[...], stage, k_out, v_out)


def unpack_call(before):
    rows = before.shape[0]
    keys = pltpu.VMEM((rows // 2, 2 * HD), BF16)
    return pl.pallas_call(
        unpack_kernel,
        in_specs=[ANY],
        out_specs=[VMEM] * 2,
        out_shape=[keys, keys],
        scratch_shapes=[
            pltpu.VMEM((rows, HD), F32),
            pltpu.VMEM((rows, HD), BF16),
            pltpu.SemaphoreType.DMA(()),
        ],
        compiler_params=PARAMS,
        cost_estimate=pl.CostEstimate(flops=0, bytes_accessed=8 * rows * HD, transcendentals=0),
    )(before)


def last_kernel(
    heads, block, rounds, place_ref, table_ref, q_ref, lin_ref, x_ref, k_before, v_before, sums_ref, top_ref, *refs
):
    state_refs = refs[:rounds]
    out_hbm, mixed, packed, cross, out_sems = refs[rounds:]
    tok = q_ref.shape[0]
    place = place_ref[0]
    first = place == 0
    stride = 2 * heads
    local_bits = tok.bit_length() - 1
    pairs = heads // 2 if heads % 2 == 0 else heads
    together = heads // pairs
    cross[...] = jnp.zeros_like(cross)
    for h in range(heads):
        total = jnp.zeros((HD, HD), F32)
        for bit, ref in enumerate(state_refs):
            earlier = jnp.bitwise_and(jnp.right_shift(place, bit), 1) == 1
            factor = jnp.where(earlier, table_ref[h, local_bits + bit + 1], 0.0)
            total = total + factor * ref[h].astype(F32)
        at = lanes(h % together)
        cross[h // together, at, at] = total.astype(BF16)

    def linear_rows(start):
        rows = slice(start, start + block)
        for pair in range(pairs):
            wide = slice(pair * together * HD, (pair + 1) * together * HD)
            both = jnp.dot(x_ref[0, rows, wide], cross[pair], preferred_element_type=F32) + lin_ref[rows, wide]
            for i in range(together):
                total = both[:, lanes(i)]
                norm = total * lax.rsqrt(jnp.mean(total * total, axis=1, keepdims=True) + 1e-06)
                at = start * stride + 2 * (pair * together + i)
                mixed[pl.ds(at, block, stride=stride), :] = norm

    row = lax.broadcasted_iota(jnp.int32, (block, block), 0)
    col = lax.broadcasted_iota(jnp.int32, (block, block), 1)
    mask = jnp.where(col >= row, 0.0, NEG).astype(F32)

    def copy_out(start):
        rows = pl.ds(start * stride, block * stride)
        return pltpu.make_async_copy(packed.at[rows, :], out_hbm.at[rows, :], out_sems.at[start // block])

    def send(start):
        rows = pl.ds(start * stride, block * stride)
        packed[rows, :] = mixed[rows, :].astype(BF16)
        copy_out(start).start()

    def attend(start):
        for pair in range(pairs):
            group = range(pair * together, (pair + 1) * together)
            here = slice(start, start + block)
            q = jnp.concatenate([q_ref[here, lanes(h)] for h in group], axis=0)
            scores = nt_dot(jnp.concatenate([q, q], axis=1), k_before[start:, :])
            edge = scores[:, :block] + jnp.concatenate([mask] * len(group), axis=0)
            scores = jnp.concatenate([edge, scores[:, block:]], axis=1) if start + block < tok else edge
            top = jnp.max(scores, axis=1, keepdims=True)
            top_own = jnp.concatenate([top_ref[h, here, :] for h in group], axis=0)
            both = jnp.where(first, top_own, jnp.maximum(top, top_own))
            off = jnp.where(first, FAR, both)
            probs = jnp.exp2(scores - jnp.concatenate([off] * (scores.shape[1] // HD), axis=1)).astype(BF16)
            sums = jnp.dot(probs, v_before[start:, :], preferred_element_type=F32)
            factor = jnp.exp2(top_own - both)
            own = jnp.concatenate([sums_ref[h, here, :] for h in group], axis=0)
            sums = sums + own * jnp.concatenate([factor, factor], axis=1)
            out = sums[:, :HD] / sums[:, HD:]
            for i, h in enumerate(group):
                at = start * stride + 2 * h + 1
                mixed[pl.ds(at, block, stride=stride), :] = out[i * block : (i + 1) * block]

    for start in range(0, tok, block):

        if start:
            send(start - block)
        attend(start)
        linear_rows(start)

    send(tok - block)
    for start in range(0, tok, block):
        copy_out(start).wait()


def last_call(place, table, soft_q, partial, planes, earlier, sums, top, states, block):
    tok, width = soft_q.shape
    heads = width // HD
    return pl.pallas_call(
        functools.partial(last_kernel, heads, block, len(states)),
        in_specs=[SMEM, SMEM] + [VMEM] * (7 + len(states)),
        out_specs=ANY,
        out_shape=jax.ShapeDtypeStruct((tok * 2 * heads, HD), BF16),
        scratch_shapes=[
            pltpu.VMEM((tok * 2 * heads, HD), F32),
            pltpu.VMEM((tok * 2 * heads, HD), BF16),
            pltpu.VMEM((heads // 2, 2 * HD, 2 * HD) if heads % 2 == 0 else (heads, HD, HD), BF16),
            pltpu.SemaphoreType.DMA((tok // block,)),
        ],
        compiler_params=PARAMS,
        cost_estimate=pl.CostEstimate(
            flops=4 * tok * tok * width, bytes_accessed=14 * tok * width, transcendentals=tok * tok * heads // 2
        ),
    )(place, table, soft_q, partial, planes, *earlier, sums, top, *states)


def local(lin_qkv, level_weights, soft_q, soft_kv):
    tok = lin_qkv.shape[0]
    q_heads = soft_q.shape[1] // HD
    group = HEADS_SM // KV_HEADS
    block = min(256, tok // 2)
    my_seq = lax.axis_index("seq")

    kv_index = lax.axis_index("head") * q_heads // group
    kv = soft_kv.reshape(tok, 2, KV_HEADS, HD).transpose(0, 2, 1, 3)
    planes = jnp.transpose(lin_qkv, (1, 0, 2))
    place = my_seq.reshape(1)
    table = jnp.transpose(level_weights)
    own_kv, state, planes = first_call(kv_index.reshape(1), kv, planes)
    own_kv = own_kv.reshape(2 * tok, HD)
    before = passed_along(own_kv, "seq", 1)
    near = partner_2(state, "seq", 0)
    partial, group_sum, *own = linear_call(table, planes, own_kv, state, near)
    states = [near]
    for bit in range(1, lax.axis_size("seq").bit_length() - 1):
        if bit > 1:
            group_sum = (group_sum.astype(F32) + states[-1].astype(F32)).astype(BF16)
        states.append(partner_2(group_sum, "seq", bit))
    sums, top = own_call(soft_q, *own, block)
    earlier = unpack_call(before)
    out = last_call(place, table, soft_q, partial, planes, earlier, sums, top, states, block)
    out = out.reshape(tok, q_heads, 2, HD).transpose(0, 2, 1, 3)
    return out.reshape(tok, 2, q_heads * HD)


def solution(mesh):
    in_specs = (
        P(("groups", "seq"), None, "head"),
        P(None, "head"),
        P(("groups", "seq"), "head"),
        P(("groups", "seq"), None, None),
    )
    out_specs = P(("groups", "seq"), None, "head")
    return jax.shard_map(local, mesh=mesh, in_specs=in_specs, out_specs=out_specs, check_vma=False)
```

```python
import functools

import jax
import jax.numpy as jnp
import numpy as np
from jax import lax
from jax.experimental import pallas as pl
from jax.experimental.pallas import tpu as pltpu
from jax.sharding import PartitionSpec as P


HD = 128
HEADS_SM = 16
KV_HEADS = 2
CHUNK = 256
NEG = -1e30
FAR = 1e30
F32 = jnp.float32
BF16 = jnp.bfloat16
SCALE = float(np.log2(np.e) / np.sqrt(HD))
ANY = pl.BlockSpec(memory_space=pl.ANY)
SMEM = pl.BlockSpec(memory_space=pltpu.SMEM)
VMEM = pl.BlockSpec(memory_space=pltpu.VMEM)
HBM = pl.BlockSpec(memory_space=pltpu.HBM)
PARAMS = pltpu.CompilerParams(vmem_limit_bytes=24 * 2**20)


def partner_2(value, axis, distance):
    mask = 2**distance
    pairs = [(source, source ^ mask) for source in range(lax.axis_size(axis))]
    return lax.ppermute(value, axis, pairs)


def passed_along(x, axis, by):
    size = lax.axis_size(axis)
    pairs = [(i, (i + by) % size) for i in range(size)]
    return lax.ppermute(x, axis, pairs)


def nt_dot(a, b):
    return lax.dot_general(a, b, (((1,), (1,)), ((), ())), preferred_element_type=F32)


def tn_dot(a, b):
    return lax.dot_general(a, b, (((0,), (0,)), ((), ())), preferred_element_type=F32)


def lanes(h):
    return slice(h * HD, (h + 1) * HD)


def take_apart(pairs, stage, k_out, v_out):
    count = k_out.shape[0]
    stage[...] = pairs.astype(F32)
    keys = stage[pl.ds(0, count, stride=2), :] * SCALE
    high = keys.astype(BF16)
    k_out[:, 0:HD] = high
    k_out[:, HD : 2 * HD] = (keys - high.astype(F32)).astype(BF16)
    v_out[:, 0:HD] = stage[pl.ds(1, count, stride=2), :].astype(BF16)
    v_out[:, HD : 2 * HD] = jnp.ones((count, HD), BF16)


def first_kernel(heads, index_ref, kv_hbm, x_hbm, own_hbm, state_ref, x_ref, raw, sums, sems):
    half = x_ref.shape[1] // 2
    pieces = [pl.ds(0, half), pl.ds(half, half)]
    pick = pltpu.make_async_copy(kv_hbm.at[:, index_ref[0]], raw, sems.at[2])
    hand_on = pltpu.make_async_copy(raw, own_hbm, sems.at[4])
    pick.start()
    loads = [
        pltpu.make_async_copy(x_hbm.at[pl.ds(1, 2), rows, :], x_ref.at[pl.ds(1, 2), rows, :], sems.at[i])
        for i, rows in enumerate(pieces)
    ]
    loads.append(pltpu.make_async_copy(x_hbm.at[0], x_ref.at[0], sems.at[3]))
    for load in loads:
        load.start()
    pick.wait()
    hand_on.start()
    loads[0].wait()
    for h in range(heads):
        sums[h] = tn_dot(x_ref[1, pieces[0], lanes(h)], x_ref[2, pieces[0], lanes(h)])
    loads[1].wait()
    for h in range(heads):
        total = sums[h] + tn_dot(x_ref[1, pieces[1], lanes(h)], x_ref[2, pieces[1], lanes(h)])
        state_ref[h] = total.astype(BF16)
    loads[2].wait()
    hand_on.wait()


def first_call(index, kv, planes):
    tok, _, two, hd = kv.shape
    width = planes.shape[2]
    heads = width // HD
    return pl.pallas_call(
        functools.partial(first_kernel, heads),
        in_specs=[SMEM, HBM, HBM],
        out_specs=[ANY, VMEM, VMEM],
        out_shape=[
            jax.ShapeDtypeStruct((tok, two, hd), BF16),
            pltpu.VMEM((heads, HD, HD), BF16),
            pltpu.VMEM(planes.shape, BF16),
        ],
        scratch_shapes=[
            pltpu.VMEM((tok, two, hd), BF16),
            pltpu.VMEM((heads, HD, HD), F32),
            pltpu.SemaphoreType.DMA((5,)),
        ],
        compiler_params=PARAMS,
        cost_estimate=pl.CostEstimate(
            flops=2 * tok * width * HD, bytes_accessed=4 * tok * width, transcendentals=0
        ),
    )(index, pltpu.with_memory_space_constraint(kv, pltpu.HBM), pltpu.with_memory_space_constraint(planes, pltpu.HBM))


def linear_kernel(
    heads, table_ref, x_ref, own_ref, mine_ref, near_ref, out_ref, pair_ref, k_own, v_own, states, stage,
    raw, sem,
):
    load = pltpu.make_async_copy(own_ref, raw, sem)
    load.start()
    tok = x_ref.shape[1]
    chunks = tok // CHUNK
    bits = CHUNK.bit_length() - 1
    rows = [pl.ds(c * CHUNK, CHUNK) for c in range(chunks)]
    row = lax.broadcasted_iota(jnp.int32, (CHUNK, CHUNK), 0)
    col = lax.broadcasted_iota(jnp.int32, (CHUNK, CHUNK), 1)
    differ = jnp.bitwise_xor(row, col)
    weights = []
    for h in range(heads):
        weight = jnp.full((CHUNK, CHUNK), table_ref[h, 0], F32)
        for level in range(1, bits + 1):
            weight = jnp.where(differ >= 2 ** (level - 1), table_ref[h, level], weight)
        weights.append(jnp.where(col <= row, weight, 0.0))
    pair_ref[...] = (mine_ref[...].astype(F32) + near_ref[...].astype(F32)).astype(BF16)
    groups = [{} for _ in range(heads)]
    for c in range(chunks):
        for h in range(heads):
            base = h * 2 * chunks
            q, k, v = (x_ref[part, rows[c], lanes(h)] for part in range(3))
            tile = (nt_dot(q, k) * weights[h]).astype(BF16)
            prefix, bit = None, 0
            while (1 << bit) <= c:
                if (c >> bit) & 1:
                    term = table_ref[h, bits + bit + 1] * states[base + groups[h][bit, (c >> bit) - 1]]
                    prefix = term if prefix is None else prefix + term
                bit += 1
            if prefix is None:
                total = jnp.dot(tile, v, preferred_element_type=F32)
            else:
                total = jnp.dot(
                    jnp.concatenate([tile, q], axis=1),
                    jnp.concatenate([v, prefix.astype(BF16)], axis=0),
                    preferred_element_type=F32,
                )
            out_ref[rows[c], lanes(h)] = total
            if c < chunks - 1:
                state, bit, index = tn_dot(k, v), 0, c
                slot = len(groups[h])
                groups[h][0, c] = slot
                states[base + slot] = state
                while index & 1:
                    state = states[base + groups[h][bit, index - 1]] + state
                    bit, index = bit + 1, index >> 1
                    slot = len(groups[h])
                    groups[h][bit, index] = slot
                    states[base + slot] = state
    load.wait()
    take_apart(raw[...], stage, k_own, v_own)


def linear_call(table, planes, own_kv, mine, near):
    _, tok, width = planes.shape
    heads = width // HD
    keys = pltpu.VMEM((tok, 2 * HD), BF16)
    return pl.pallas_call(
        functools.partial(linear_kernel, heads),
        in_specs=[SMEM, VMEM, ANY, VMEM, VMEM],
        out_specs=[VMEM] * 4,
        out_shape=[pltpu.VMEM((tok, width), F32), pltpu.VMEM(mine.shape, BF16), keys, keys],
        scratch_shapes=[
            pltpu.VMEM((heads * 2 * (tok // CHUNK), HD, HD), F32),
            pltpu.VMEM((2 * tok, HD), F32),
            pltpu.VMEM((2 * tok, HD), BF16),
            pltpu.SemaphoreType.DMA(()),
        ],
        compiler_params=PARAMS,
        cost_estimate=pl.CostEstimate(
            flops=8 * tok * width * CHUNK, bytes_accessed=10 * tok * width, transcendentals=0
        ),
    )(table, planes, own_kv, mine, near)


def own_kernel(heads, block, q_ref, k_own, v_own, sums_ref, top_ref):
    tok = q_ref.shape[0]
    row = lax.broadcasted_iota(jnp.int32, (block, block), 0)
    col = lax.broadcasted_iota(jnp.int32, (block, block), 1)
    mask = jnp.where(col <= row, 0.0, NEG).astype(F32)
    mask = jnp.concatenate([mask] * heads, axis=0)
    for start in reversed(range(0, tok, block)):
        end = start + block
        q = jnp.concatenate([q_ref[start:end, lanes(h)] for h in range(heads)], axis=0)
        scores = nt_dot(jnp.concatenate([q, q], axis=1), k_own[:end, :])
        edge = scores[:, start:] + mask
        scores = jnp.concatenate([scores[:, :start], edge], axis=1) if start else edge
        top = jnp.max(scores, axis=1, keepdims=True)
        sums = jnp.dot(jnp.exp2(scores - top).astype(BF16), v_own[:end, :], preferred_element_type=F32)
        top = jnp.broadcast_to(top, (heads * block, HD))
        for h in range(heads):
            rows = slice(h * block, (h + 1) * block)
            sums_ref[h, start:end, :] = sums[rows]
            top_ref[h, start:end, :] = top[rows]


def own_call(soft_q, k_own, v_own, block):
    tok, width = soft_q.shape
    heads = width // HD
    return pl.pallas_call(
        functools.partial(own_kernel, heads, block),
        in_specs=[VMEM] * 3,
        out_specs=[VMEM] * 2,
        out_shape=[pltpu.VMEM((heads, tok, 2 * HD), F32), pltpu.VMEM((heads, tok, HD), F32)],
        compiler_params=PARAMS,
        cost_estimate=pl.CostEstimate(
            flops=3 * tok * tok * width, bytes_accessed=6 * tok * width, transcendentals=tok * tok * heads // 2
        ),
    )(soft_q, k_own, v_own)


def unpack_kernel(before_ref, k_out, v_out, stage, raw, sem):
    load = pltpu.make_async_copy(before_ref, raw, sem)
    load.start()
    load.wait()
    take_apart(raw[...], stage, k_out, v_out)


def unpack_call(before):
    rows = before.shape[0]
    keys = pltpu.VMEM((rows // 2, 2 * HD), BF16)
    return pl.pallas_call(
        unpack_kernel,
        in_specs=[ANY],
        out_specs=[VMEM] * 2,
        out_shape=[keys, keys],
        scratch_shapes=[
            pltpu.VMEM((rows, HD), F32),
            pltpu.VMEM((rows, HD), BF16),
            pltpu.SemaphoreType.DMA(()),
        ],
        compiler_params=PARAMS,
        cost_estimate=pl.CostEstimate(flops=0, bytes_accessed=8 * rows * HD, transcendentals=0),
    )(before)


def last_kernel(
    heads, block, rounds, place_ref, table_ref, q_ref, lin_ref, x_ref, k_before, v_before, sums_ref, top_ref, *refs
):
    state_refs = refs[:rounds]
    out_hbm, mixed, packed, cross, out_sems = refs[rounds:]
    tok = q_ref.shape[0]
    place = place_ref[0]
    first = place == 0
    stride = 2 * heads
    local_bits = tok.bit_length() - 1
    pairs = heads // 2 if heads % 2 == 0 else heads
    together = heads // pairs
    cross[...] = jnp.zeros_like(cross)
    for h in range(heads):
        total = jnp.zeros((HD, HD), F32)
        for bit, ref in enumerate(state_refs):
            earlier = jnp.bitwise_and(jnp.right_shift(place, bit), 1) == 1
            factor = jnp.where(earlier, table_ref[h, local_bits + bit + 1], 0.0)
            total = total + factor * ref[h].astype(F32)
        at = lanes(h % together)
        cross[h // together, at, at] = total.astype(BF16)

    def linear_rows(start):
        rows = slice(start, start + block)
        for pair in range(pairs):
            wide = slice(pair * together * HD, (pair + 1) * together * HD)
            both = jnp.dot(x_ref[0, rows, wide], cross[pair], preferred_element_type=F32) + lin_ref[rows, wide]
            for i in range(together):
                total = both[:, lanes(i)]
                norm = total * lax.rsqrt(jnp.mean(total * total, axis=1, keepdims=True) + 1e-06)
                at = start * stride + 2 * (pair * together + i)
                mixed[pl.ds(at, block, stride=stride), :] = norm

    row = lax.broadcasted_iota(jnp.int32, (block, block), 0)
    col = lax.broadcasted_iota(jnp.int32, (block, block), 1)
    mask = jnp.where(col >= row, 0.0, NEG).astype(F32)

    half = block // 2

    def copy_out(start):
        rows = pl.ds(start * stride, half * stride)
        return pltpu.make_async_copy(packed.at[rows, :], out_hbm.at[rows, :], out_sems.at[start // half])

    def send(start):
        for at in (start, start + half):
            rows = pl.ds(at * stride, half * stride)
            packed[rows, :] = mixed[rows, :].astype(BF16)
            copy_out(at).start()

    def attend(start):
        linear_rows(start)
        for h in range(heads):
            q = q_ref[start : start + block, lanes(h)]
            scores = nt_dot(jnp.concatenate([q, q], axis=1), k_before[start:, :])
            edge = scores[:, :block] + mask
            scores = jnp.concatenate([edge, scores[:, block:]], axis=1) if start + block < tok else edge
            top = jnp.max(scores, axis=1, keepdims=True)
            top_own = top_ref[h, start : start + block, :]
            both = jnp.where(first, top_own, jnp.maximum(top, top_own))
            off = jnp.where(first, FAR, both)
            probs = jnp.exp2(scores - jnp.concatenate([off] * (scores.shape[1] // HD), axis=1)).astype(BF16)
            sums = jnp.dot(probs, v_before[start:, :], preferred_element_type=F32)
            factor = jnp.exp2(top_own - both)
            sums = sums + sums_ref[h, start : start + block, :] * jnp.concatenate([factor, factor], axis=1)
            mixed[pl.ds(start * stride + 2 * h + 1, block, stride=stride), :] = sums[:, :HD] / sums[:, HD:]

    for start in range(0, tok, block):

        if start:
            send(start - block)
        attend(start)

    send(tok - block)
    for start in range(0, tok, half):
        copy_out(start).wait()


def last_call(place, table, soft_q, partial, planes, earlier, sums, top, states, block):
    tok, width = soft_q.shape
    heads = width // HD
    return pl.pallas_call(
        functools.partial(last_kernel, heads, block, len(states)),
        in_specs=[SMEM, SMEM] + [VMEM] * (7 + len(states)),
        out_specs=ANY,
        out_shape=jax.ShapeDtypeStruct((tok * 2 * heads, HD), BF16),
        scratch_shapes=[
            pltpu.VMEM((tok * 2 * heads, HD), F32),
            pltpu.VMEM((tok * 2 * heads, HD), BF16),
            pltpu.VMEM((heads // 2, 2 * HD, 2 * HD) if heads % 2 == 0 else (heads, HD, HD), BF16),
            pltpu.SemaphoreType.DMA((2 * tok // block,)),
        ],
        compiler_params=PARAMS,
        cost_estimate=pl.CostEstimate(
            flops=4 * tok * tok * width, bytes_accessed=14 * tok * width, transcendentals=tok * tok * heads // 2
        ),
    )(place, table, soft_q, partial, planes, *earlier, sums, top, *states)


def local(lin_qkv, level_weights, soft_q, soft_kv):
    tok = lin_qkv.shape[0]
    q_heads = soft_q.shape[1] // HD
    group = HEADS_SM // KV_HEADS
    block = min(256, tok // 2)
    my_seq = lax.axis_index("seq")

    kv_index = lax.axis_index("head") * q_heads // group
    kv = soft_kv.reshape(tok, 2, KV_HEADS, HD).transpose(0, 2, 1, 3)
    planes = jnp.transpose(lin_qkv, (1, 0, 2))
    place = my_seq.reshape(1)
    table = jnp.transpose(level_weights)
    own_kv, state, planes = first_call(kv_index.reshape(1), kv, planes)
    own_kv = own_kv.reshape(2 * tok, HD)
    before = passed_along(own_kv, "seq", 1)
    near = partner_2(state, "seq", 0)
    partial, group_sum, *own = linear_call(table, planes, own_kv, state, near)
    states = [near]
    for bit in range(1, lax.axis_size("seq").bit_length() - 1):
        if bit > 1:
            group_sum = (group_sum.astype(F32) + states[-1].astype(F32)).astype(BF16)
        states.append(partner_2(group_sum, "seq", bit))
    sums, top = own_call(soft_q, *own, block)
    earlier = unpack_call(before)
    out = last_call(place, table, soft_q, partial, planes, earlier, sums, top, states, block)
    out = out.reshape(tok, q_heads, 2, HD).transpose(0, 2, 1, 3)
    return out.reshape(tok, 2, q_heads * HD)


def solution(mesh):
    in_specs = (
        P(("groups", "seq"), None, "head"),
        P(None, "head"),
        P(("groups", "seq"), "head"),
        P(("groups", "seq"), None, None),
    )
    out_specs = P(("groups", "seq"), None, "head")
    return jax.shard_map(local, mesh=mesh, in_specs=in_specs, out_specs=out_specs, check_vma=False)
```

```python
import functools

import jax
import jax.numpy as jnp
import numpy as np
from jax import lax
from jax.experimental import pallas as pl
from jax.experimental.pallas import tpu as pltpu
from jax.sharding import PartitionSpec as P


HD = 128
HEADS_SM = 16
KV_HEADS = 2
CHUNK = 256
NEG = -1e30
FAR = 1e30
F32 = jnp.float32
BF16 = jnp.bfloat16
SCALE = float(np.log2(np.e) / np.sqrt(HD))
ANY = pl.BlockSpec(memory_space=pl.ANY)
SMEM = pl.BlockSpec(memory_space=pltpu.SMEM)
VMEM = pl.BlockSpec(memory_space=pltpu.VMEM)
HBM = pl.BlockSpec(memory_space=pltpu.HBM)
PARAMS = pltpu.CompilerParams(vmem_limit_bytes=24 * 2**20)


def partner_2(value, axis, distance):
    mask = 2**distance
    pairs = [(source, source ^ mask) for source in range(lax.axis_size(axis))]
    return lax.ppermute(value, axis, pairs)


def passed_along(x, axis, by):
    size = lax.axis_size(axis)
    pairs = [(i, (i + by) % size) for i in range(size)]
    return lax.ppermute(x, axis, pairs)


def nt_dot(a, b):
    return lax.dot_general(a, b, (((1,), (1,)), ((), ())), preferred_element_type=F32)


def tn_dot(a, b):
    return lax.dot_general(a, b, (((0,), (0,)), ((), ())), preferred_element_type=F32)


def lanes(h):
    return slice(h * HD, (h + 1) * HD)


def take_apart(pairs, stage, k_out, v_out):
    count = k_out.shape[0]
    stage[...] = pairs.astype(F32)
    keys = stage[pl.ds(0, count, stride=2), :] * SCALE
    high = keys.astype(BF16)
    k_out[:, 0:HD] = high
    k_out[:, HD : 2 * HD] = (keys - high.astype(F32)).astype(BF16)
    v_out[:, 0:HD] = stage[pl.ds(1, count, stride=2), :].astype(BF16)
    v_out[:, HD : 2 * HD] = jnp.ones((count, HD), BF16)


def first_kernel(heads, index_ref, kv_hbm, x_hbm, own_hbm, state_ref, x_ref, raw, sums, sems):
    half = x_ref.shape[1] // 2
    pieces = [pl.ds(0, half), pl.ds(half, half)]
    pick = pltpu.make_async_copy(kv_hbm.at[:, index_ref[0]], raw, sems.at[2])
    hand_on = pltpu.make_async_copy(raw, own_hbm, sems.at[4])
    pick.start()
    loads = [
        pltpu.make_async_copy(x_hbm.at[pl.ds(1, 2), rows, :], x_ref.at[pl.ds(1, 2), rows, :], sems.at[i])
        for i, rows in enumerate(pieces)
    ]
    loads.append(pltpu.make_async_copy(x_hbm.at[0], x_ref.at[0], sems.at[3]))
    for load in loads:
        load.start()
    pick.wait()
    hand_on.start()
    loads[0].wait()
    for h in range(heads):
        sums[h] = tn_dot(x_ref[1, pieces[0], lanes(h)], x_ref[2, pieces[0], lanes(h)])
    loads[1].wait()
    for h in range(heads):
        total = sums[h] + tn_dot(x_ref[1, pieces[1], lanes(h)], x_ref[2, pieces[1], lanes(h)])
        state_ref[h] = total.astype(BF16)
    loads[2].wait()
    hand_on.wait()


def first_call(index, kv, planes):
    tok, _, two, hd = kv.shape
    width = planes.shape[2]
    heads = width // HD
    return pl.pallas_call(
        functools.partial(first_kernel, heads),
        in_specs=[SMEM, HBM, HBM],
        out_specs=[ANY, VMEM, VMEM],
        out_shape=[
            jax.ShapeDtypeStruct((tok, two, hd), BF16),
            pltpu.VMEM((heads, HD, HD), BF16),
            pltpu.VMEM(planes.shape, BF16),
        ],
        scratch_shapes=[
            pltpu.VMEM((tok, two, hd), BF16),
            pltpu.VMEM((heads, HD, HD), F32),
            pltpu.SemaphoreType.DMA((5,)),
        ],
        compiler_params=PARAMS,
        cost_estimate=pl.CostEstimate(
            flops=2 * tok * width * HD, bytes_accessed=4 * tok * width, transcendentals=0
        ),
    )(index, pltpu.with_memory_space_constraint(kv, pltpu.HBM), pltpu.with_memory_space_constraint(planes, pltpu.HBM))


def linear_kernel(
    heads, table_ref, x_ref, own_ref, mine_ref, near_ref, out_ref, pair_ref, k_own, v_own, states, stage,
    raw, sem,
):
    load = pltpu.make_async_copy(own_ref, raw, sem)
    load.start()
    tok = x_ref.shape[1]
    chunks = tok // CHUNK
    bits = CHUNK.bit_length() - 1
    rows = [pl.ds(c * CHUNK, CHUNK) for c in range(chunks)]
    row = lax.broadcasted_iota(jnp.int32, (CHUNK, CHUNK), 0)
    col = lax.broadcasted_iota(jnp.int32, (CHUNK, CHUNK), 1)
    differ = jnp.bitwise_xor(row, col)
    weights = []
    for h in range(heads):
        weight = jnp.full((CHUNK, CHUNK), table_ref[h, 0], F32)
        for level in range(1, bits + 1):
            weight = jnp.where(differ >= 2 ** (level - 1), table_ref[h, level], weight)
        weights.append(jnp.where(col <= row, weight, 0.0))
    pair_ref[...] = (mine_ref[...].astype(F32) + near_ref[...].astype(F32)).astype(BF16)
    groups = [{} for _ in range(heads)]
    for c in range(chunks):
        for h in range(heads):
            base = h * 2 * chunks
            q, k, v = (x_ref[part, rows[c], lanes(h)] for part in range(3))
            tile = (nt_dot(q, k) * weights[h]).astype(BF16)
            prefix, bit = None, 0
            while (1 << bit) <= c:
                if (c >> bit) & 1:
                    term = table_ref[h, bits + bit + 1] * states[base + groups[h][bit, (c >> bit) - 1]]
                    prefix = term if prefix is None else prefix + term
                bit += 1
            if prefix is None:
                total = jnp.dot(tile, v, preferred_element_type=F32)
            else:
                total = jnp.dot(
                    jnp.concatenate([tile, q], axis=1),
                    jnp.concatenate([v, prefix.astype(BF16)], axis=0),
                    preferred_element_type=F32,
                )
            out_ref[rows[c], lanes(h)] = total
            if c < chunks - 1:
                state, bit, index = tn_dot(k, v), 0, c
                slot = len(groups[h])
                groups[h][0, c] = slot
                states[base + slot] = state
                while index & 1:
                    state = states[base + groups[h][bit, index - 1]] + state
                    bit, index = bit + 1, index >> 1
                    slot = len(groups[h])
                    groups[h][bit, index] = slot
                    states[base + slot] = state
    load.wait()
    take_apart(raw[...], stage, k_own, v_own)


def linear_call(table, planes, own_kv, mine, near):
    _, tok, width = planes.shape
    heads = width // HD
    keys = pltpu.VMEM((tok, 2 * HD), BF16)
    return pl.pallas_call(
        functools.partial(linear_kernel, heads),
        in_specs=[SMEM, VMEM, ANY, VMEM, VMEM],
        out_specs=[VMEM] * 4,
        out_shape=[pltpu.VMEM((tok, width), F32), pltpu.VMEM(mine.shape, BF16), keys, keys],
        scratch_shapes=[
            pltpu.VMEM((heads * 2 * (tok // CHUNK), HD, HD), F32),
            pltpu.VMEM((2 * tok, HD), F32),
            pltpu.VMEM((2 * tok, HD), BF16),
            pltpu.SemaphoreType.DMA(()),
        ],
        compiler_params=PARAMS,
        cost_estimate=pl.CostEstimate(
            flops=8 * tok * width * CHUNK, bytes_accessed=10 * tok * width, transcendentals=0
        ),
    )(table, planes, own_kv, mine, near)


def own_kernel(heads, block, q_ref, k_own, v_own, sums_ref, top_ref):
    tok = q_ref.shape[0]
    row = lax.broadcasted_iota(jnp.int32, (block, block), 0)
    col = lax.broadcasted_iota(jnp.int32, (block, block), 1)
    mask = jnp.where(col <= row, 0.0, NEG).astype(F32)
    mask = jnp.concatenate([mask] * heads, axis=0)
    for start in reversed(range(0, tok, block)):
        end = start + block
        q = jnp.concatenate([q_ref[start:end, lanes(h)] for h in range(heads)], axis=0)
        scores = nt_dot(jnp.concatenate([q, q], axis=1), k_own[:end, :])
        edge = scores[:, start:] + mask
        scores = jnp.concatenate([scores[:, :start], edge], axis=1) if start else edge
        top = jnp.max(scores, axis=1, keepdims=True)
        sums = jnp.dot(jnp.exp2(scores - top).astype(BF16), v_own[:end, :], preferred_element_type=F32)
        top = jnp.broadcast_to(top, (heads * block, HD))
        for h in range(heads):
            rows = slice(h * block, (h + 1) * block)
            sums_ref[h, start:end, :] = sums[rows]
            top_ref[h, start:end, :] = top[rows]


def own_call(soft_q, k_own, v_own, block):
    tok, width = soft_q.shape
    heads = width // HD
    return pl.pallas_call(
        functools.partial(own_kernel, heads, block),
        in_specs=[VMEM] * 3,
        out_specs=[VMEM] * 2,
        out_shape=[pltpu.VMEM((heads, tok, 2 * HD), F32), pltpu.VMEM((heads, tok, HD), F32)],
        compiler_params=PARAMS,
        cost_estimate=pl.CostEstimate(
            flops=3 * tok * tok * width, bytes_accessed=6 * tok * width, transcendentals=tok * tok * heads // 2
        ),
    )(soft_q, k_own, v_own)


def unpack_kernel(before_ref, k_out, v_out, stage, raw, sem):
    load = pltpu.make_async_copy(before_ref, raw, sem)
    load.start()
    load.wait()
    take_apart(raw[...], stage, k_out, v_out)


def unpack_call(before):
    rows = before.shape[0]
    keys = pltpu.VMEM((rows // 2, 2 * HD), BF16)
    return pl.pallas_call(
        unpack_kernel,
        in_specs=[ANY],
        out_specs=[VMEM] * 2,
        out_shape=[keys, keys],
        scratch_shapes=[
            pltpu.VMEM((rows, HD), F32),
            pltpu.VMEM((rows, HD), BF16),
            pltpu.SemaphoreType.DMA(()),
        ],
        compiler_params=PARAMS,
        cost_estimate=pl.CostEstimate(flops=0, bytes_accessed=8 * rows * HD, transcendentals=0),
    )(before)


def last_kernel(
    heads, block, rounds, place_ref, table_ref, q_ref, lin_ref, x_ref, k_before, v_before, sums_ref, top_ref, *refs
):
    state_refs = refs[:rounds]
    out_hbm, mixed, packed, cross, out_sems = refs[rounds:]
    tok = q_ref.shape[0]
    place = place_ref[0]
    first = place == 0
    stride = 2 * heads
    local_bits = tok.bit_length() - 1
    pairs = heads // 2 if heads % 2 == 0 else heads
    together = heads // pairs
    cross[...] = jnp.zeros_like(cross)
    for h in range(heads):
        total = jnp.zeros((HD, HD), F32)
        for bit, ref in enumerate(state_refs):
            earlier = jnp.bitwise_and(jnp.right_shift(place, bit), 1) == 1
            factor = jnp.where(earlier, table_ref[h, local_bits + bit + 1], 0.0)
            total = total + factor * ref[h].astype(F32)
        at = lanes(h % together)
        cross[h // together, at, at] = total.astype(BF16)

    def linear_rows(start):
        rows = slice(start, start + block)
        for pair in range(pairs):
            wide = slice(pair * together * HD, (pair + 1) * together * HD)
            both = jnp.dot(x_ref[0, rows, wide], cross[pair], preferred_element_type=F32) + lin_ref[rows, wide]
            for i in range(together):
                total = both[:, lanes(i)]
                norm = total * lax.rsqrt(jnp.mean(total * total, axis=1, keepdims=True) + 1e-06)
                at = start * stride + 2 * (pair * together + i)
                mixed[pl.ds(at, block, stride=stride), :] = norm

    row = lax.broadcasted_iota(jnp.int32, (block, block), 0)
    col = lax.broadcasted_iota(jnp.int32, (block, block), 1)
    mask = jnp.where(col >= row, 0.0, NEG).astype(F32)

    part = block // 4

    def copy_out(start):
        rows = pl.ds(start * stride, part * stride)
        return pltpu.make_async_copy(packed.at[rows, :], out_hbm.at[rows, :], out_sems.at[start // part])

    def send(start):
        for at in range(start, start + block, part):
            rows = pl.ds(at * stride, part * stride)
            packed[rows, :] = mixed[rows, :].astype(BF16)
            copy_out(at).start()

    def attend(start):
        linear_rows(start)
        for h in range(heads):
            q = q_ref[start : start + block, lanes(h)]
            scores = nt_dot(jnp.concatenate([q, q], axis=1), k_before[start:, :])
            edge = scores[:, :block] + mask
            scores = jnp.concatenate([edge, scores[:, block:]], axis=1) if start + block < tok else edge
            top = jnp.max(scores, axis=1, keepdims=True)
            top_own = top_ref[h, start : start + block, :]
            both = jnp.where(first, top_own, jnp.maximum(top, top_own))
            off = jnp.where(first, FAR, both)
            probs = jnp.exp2(scores - jnp.concatenate([off] * (scores.shape[1] // HD), axis=1)).astype(BF16)
            sums = jnp.dot(probs, v_before[start:, :], preferred_element_type=F32)
            factor = jnp.exp2(top_own - both)
            sums = sums + sums_ref[h, start : start + block, :] * jnp.concatenate([factor, factor], axis=1)
            mixed[pl.ds(start * stride + 2 * h + 1, block, stride=stride), :] = sums[:, :HD] / sums[:, HD:]

    for start in range(0, tok, block):

        if start:
            send(start - block)
        attend(start)

    send(tok - block)
    for start in range(0, tok, part):
        copy_out(start).wait()


def last_call(place, table, soft_q, partial, planes, earlier, sums, top, states, block):
    tok, width = soft_q.shape
    heads = width // HD
    return pl.pallas_call(
        functools.partial(last_kernel, heads, block, len(states)),
        in_specs=[SMEM, SMEM] + [VMEM] * (7 + len(states)),
        out_specs=ANY,
        out_shape=jax.ShapeDtypeStruct((tok * 2 * heads, HD), BF16),
        scratch_shapes=[
            pltpu.VMEM((tok * 2 * heads, HD), F32),
            pltpu.VMEM((tok * 2 * heads, HD), BF16),
            pltpu.VMEM((heads // 2, 2 * HD, 2 * HD) if heads % 2 == 0 else (heads, HD, HD), BF16),
            pltpu.SemaphoreType.DMA((4 * tok // block,)),
        ],
        compiler_params=PARAMS,
        cost_estimate=pl.CostEstimate(
            flops=4 * tok * tok * width, bytes_accessed=14 * tok * width, transcendentals=tok * tok * heads // 2
        ),
    )(place, table, soft_q, partial, planes, *earlier, sums, top, *states)


def local(lin_qkv, level_weights, soft_q, soft_kv):
    tok = lin_qkv.shape[0]
    q_heads = soft_q.shape[1] // HD
    group = HEADS_SM // KV_HEADS
    block = min(256, tok // 2)
    my_seq = lax.axis_index("seq")

    kv_index = lax.axis_index("head") * q_heads // group
    kv = soft_kv.reshape(tok, 2, KV_HEADS, HD).transpose(0, 2, 1, 3)
    planes = jnp.transpose(lin_qkv, (1, 0, 2))
    place = my_seq.reshape(1)
    table = jnp.transpose(level_weights)
    own_kv, state, planes = first_call(kv_index.reshape(1), kv, planes)
    own_kv = own_kv.reshape(2 * tok, HD)
    before = passed_along(own_kv, "seq", 1)
    near = partner_2(state, "seq", 0)
    partial, group_sum, *own = linear_call(table, planes, own_kv, state, near)
    states = [near]
    for bit in range(1, lax.axis_size("seq").bit_length() - 1):
        if bit > 1:
            group_sum = (group_sum.astype(F32) + states[-1].astype(F32)).astype(BF16)
        states.append(partner_2(group_sum, "seq", bit))
    sums, top = own_call(soft_q, *own, block)
    earlier = unpack_call(before)
    out = last_call(place, table, soft_q, partial, planes, earlier, sums, top, states, block)
    out = out.reshape(tok, q_heads, 2, HD).transpose(0, 2, 1, 3)
    return out.reshape(tok, 2, q_heads * HD)


def solution(mesh):
    in_specs = (
        P(("groups", "seq"), None, "head"),
        P(None, "head"),
        P(("groups", "seq"), "head"),
        P(("groups", "seq"), None, None),
    )
    out_specs = P(("groups", "seq"), None, "head")
    return jax.shard_map(local, mesh=mesh, in_specs=in_specs, out_specs=out_specs, check_vma=False)
```
